512 devices in a mesh: lat: 16 (over y, x_lo), lon: 32 (over x_hi, z, core).
Axes of the slice: x: 4 (x_hi: 2, x_lo: 2; x = x_hi * 2 + x_lo), y: 8, z: 8, core: 2. Of those that a mesh axis runs over, the one named last changes fastest.
Arguments:
- adjoint_in: bfloat16 [8, 100, 32, 4096], P(None, None, 'lat', 'lon'), may hold values from -6 to 6
- state: bfloat16 [2, 8, 100, 32, 4096], P(None, None, None, 'lat', 'lon'), may hold values from 0.29882812 to 1
- inverses: bfloat16 [3, 8, 100, 100], replicated
- courant_lon: float32 [32, 4096], P('lat', 'lon'), may hold values from 0.1 to 0.4
- courant_lat: float32 [32, 4096], P('lat', 'lon'), may hold values from 0.1 to 0.4
- emission: float32 [100, 32, 4096], P(None, 'lat', 'lon'), may hold values from 0.02 to 0.2
- region_id: int32 [32, 4096], P('lat', 'lon'), may hold values from 0 to 511, as said below
- stiffness: int32 [8, 32, 4096], P(None, 'lat', 'lon'), may hold values from 1 to 3
Outputs:
- adjoint_out: bfloat16 [8, 100, 32, 4096], P(None, None, 'lat', 'lon')
- emission_grad: float32 [512, 100], P(('lat', 'lon'))
The draws below stay inside these ranges and needn't reach their ends.
Inputs may be any that keep to these rules, and one draw needn't show every extreme that they name: `region_id`: constant on aligned tiles of 2 x 2 columns.
All inputs are finite; a program needn't handle non-finite values.
Results may differ from the reference program's by a relative error of at most 0.0048.
Values sent between devices are 32-bit elements; how exact they have to be, the bound alone decides.
No kernel may reach another device: no remote copies, remote signals or barrier semaphores. Data moves between devices by JAX's collectives and lax.ppermute only.
A program may use at most 64 MiB of HBM per device.

```python
import math
import jax
import jax.numpy as jnp
from jax import lax

SPEC = 100
LEV = 8
STEPS = 3
NWIN = 2
ADV = 2
CLAT = 2
CLON = 128
NLAT = 32
NLON = 4096
REGIONS = 512


def draw_inverses(key, part):
    key_diag = jax.random.fold_in(key, 11)
    key_off = jax.random.fold_in(key, 12)
    diag = jax.random.uniform(key_diag, (STEPS, LEV, SPEC), jnp.float32, 0.7, 1.2)
    off = jax.random.normal(key_off, (STEPS, LEV, SPEC, SPEC), jnp.float32) * 0.4 * SPEC ** (-0.5)
    eye = jnp.eye(SPEC, dtype=jnp.float32)
    return (off * (1.0 - eye) + diag[..., None] * eye).astype(jnp.bfloat16)


def draw_region_id(key, part):
    tiles = jax.random.randint(jax.random.fold_in(key, 21), (NLAT // 2, NLON // 2), 0, REGIONS)
    return jnp.repeat(jnp.repeat(tiles, 2, axis=0), 2, axis=1).astype(jnp.int32)


def draw_stiffness(key, part):
    tile_cols = CLON // 2
    caps = jax.random.randint(jax.random.fold_in(key, 31), (NLAT // CLAT, NLON // tile_cols), 1, STEPS + 1)
    caps = jnp.repeat(jnp.repeat(caps, CLAT, axis=0), tile_cols, axis=1)
    extra = jax.random.randint(jax.random.fold_in(key, 32), (LEV, NLAT, NLON), 0, STEPS)
    return (1 + extra % caps[None, :, :]).astype(jnp.int32)


def levels(own_key, dims, cuts, least, high):
    loudness = 1.0
    for position, blocks in cuts:
        heights = jax.random.uniform(jax.random.fold_in(jax.random.fold_in(own_key, 6), position), (blocks,), jnp.float32, least / len(cuts), high / len(cuts))
        loudness = loudness * jnp.repeat(jnp.exp(heights), dims[position] // blocks).reshape((-1,) + (1,) * (len(dims) - 1 - position))
    return loudness


def bell_draw(stream_key, shape, scale, reach, shards=(), held_as=jnp.bfloat16):
    level = levels(stream_key, shape, shards, -0.22, 0.18) if shards else 1.0
    values = jax.random.normal(stream_key, shape, jnp.float32) * scale * level
    return jnp.minimum(jnp.maximum(values, -reach), reach).astype(held_as)


def setup_inputs(seed: int = 0) -> dict:
    seeds = jax.random.split(jax.random.key(seed), 9)
    adjoint_in = bell_draw(seeds[0], (LEV, SPEC, NLAT, NLON), 1.0, 6.0, ((2, 16), (3, 32)))
    state = jnp.clip(jnp.exp(math.log(1.0) - 1.2078867 * jax.random.uniform(seeds[1], (NWIN, LEV, SPEC, NLAT, NLON), jnp.float32) ** levels(seeds[1], (NWIN, LEV, SPEC, NLAT, NLON), ((3, 16), (4, 32)), -0.2, 0.2)), 0.29882812, 1.0).astype(jnp.bfloat16)
    inverses = draw_inverses(jax.random.fold_in(seeds[8], 71), 0)
    courant_lon = jnp.clip(0.1 + 0.3 * jax.random.uniform(seeds[3], (NLAT, NLON), jnp.float32) ** levels(seeds[3], (NLAT, NLON), ((0, 16), (1, 32)), -0.2, 0.2), 0.1, 0.4)
    courant_lat = jnp.clip(0.1 + 0.3 * jax.random.uniform(seeds[4], (NLAT, NLON), jnp.float32) ** levels(seeds[4], (NLAT, NLON), ((0, 16), (1, 32)), -0.2, 0.2), 0.1, 0.4)
    emission = jnp.clip(jnp.exp(math.log(0.2) - 2.3025851 * jax.random.uniform(seeds[5], (SPEC, NLAT, NLON), jnp.float32) ** levels(seeds[5], (SPEC, NLAT, NLON), ((1, 16), (2, 32)), -0.2, 0.2)), 0.02, 0.2)
    region_id = draw_region_id(jax.random.fold_in(seeds[8], 71), 0)
    stiffness = draw_stiffness(jax.random.fold_in(seeds[8], 71), 0)
    return {"adjoint_in": adjoint_in, "state": state, "inverses": inverses, "courant_lon": courant_lon, "courant_lat": courant_lat, "emission": emission, "region_id": region_id, "stiffness": stiffness}


def transport(lam, clon, clat):
    right = jnp.roll(lam, -1, axis=2)
    down = jnp.concatenate([lam[:, 1:, :], jnp.zeros_like(lam[:, :1, :])], axis=1)
    return (1.0 - clon - clat) * lam + clat * down + clon * right


def chem_level(lam, factor, mats, klass):
    spec = lam.shape[0]
    flat = lam.reshape(spec, -1)
    yfac = factor.reshape(spec, -1).astype(jnp.float32)
    live = klass.reshape(1, -1)
    for s in reversed(range(STEPS)):
        amat = mats[s].T
        first = jnp.dot(amat, flat.astype(jnp.bfloat16), preferred_element_type=jnp.float32)
        second = jnp.dot(amat, (first * yfac).astype(jnp.bfloat16), preferred_element_type=jnp.float32)
        third = jnp.dot(amat, (second * yfac).astype(jnp.bfloat16), preferred_element_type=jnp.float32)
        cand = 0.4 * flat + 0.3 * first + 0.2 * second + 0.1 * third
        flat = jnp.where(live > s, cand, flat)
    return flat.reshape(lam.shape)


def reference(adjoint_in, state, inverses, courant_lon, courant_lat, emission, region_id, stiffness):
    lam = adjoint_in.astype(jnp.float32)
    surface = jnp.zeros(emission.shape, jnp.float32)
    mats_by_level = jnp.transpose(inverses, (1, 0, 2, 3))
    for window in reversed(range(NWIN)):
        def level_work(items):
            lam_l, factor_l, mats_l, klass_l = items
            for k in range(ADV):
                lam_l = transport(lam_l, courant_lon, courant_lat)
            return chem_level(lam_l, factor_l, mats_l, klass_l)

        lam = lax.map(level_work, (lam, state[window], mats_by_level, stiffness))
        surface = surface + lam[0]
    contrib = (surface * emission).reshape(emission.shape[0], -1).T
    grad = jax.ops.segment_sum(contrib, region_id.reshape(-1), num_segments=REGIONS)
    return lam.astype(jnp.bfloat16), grad.astype(jnp.float32)
```

```python
import functools
import jax
import jax.numpy as jnp
from jax import lax
from jax.experimental import pallas as pl
from jax.experimental.pallas import tpu as pltpu
from jax.sharding import PartitionSpec as P

STEPS = 3
EXTRA = 8
F32 = jnp.float32
BF16 = jnp.bfloat16
ANY = pl.BlockSpec(memory_space=pl.ANY)
VMEM = pl.BlockSpec(memory_space=pltpu.VMEM)


def lanes(shape):
    return lax.broadcasted_iota(jnp.int32, shape, len(shape) - 1)


def place(acc, block, slot):
    moved = pltpu.roll(block, 2 * slot, 1) if slot else block
    at = lanes(block.shape)
    return jnp.where((at >= 2 * slot) & (at < 2 * slot + 2), moved, acc)


def pack_kernel(adj, clon, clat, first, rest, west, *, rows):
    levels = adj.shape[0]
    acc = jnp.zeros((rows, adj.shape[2]), F32)
    for lev in range(levels):
        block = adj[lev].astype(F32)
        if lev == 0:
            first[0:rows] = block
        else:
            rest[(lev - 1) * rows : lev * rows] = block
        acc = place(acc, block, lev)
    west[0:rows] = acc
    for out in (first, west):
        out[rows : rows + 2] = clon[...]
        out[rows + 2 : rows + 4] = clat[...]
        out[rows + 4 : rows + 8] = jnp.zeros((4, clon.shape[1]), F32)


def pull(block, lane_from, lane_to, width):
    shift = (lane_to - lane_from) % width
    return pltpu.roll(block, shift, 1) if shift else block


def advected(own, north, west, diag, lev, slot, cour):
    rows, width = cour["rows"], own.shape[1]
    spec = rows // 2
    last = lanes((spec, width)) == width - 1
    base = lev * rows

    def pick(ref, start, parity):
        return ref[pl.ds(start + parity, spec, stride=2), :]

    r0, r1 = pick(own, base, 0), pick(own, base, 1)
    r2, r3 = pick(north, base, 0), pick(north, base, 1)
    w0, w1, d = pick(west, 0, 0), pick(west, 0, 1), pick(diag, 0, 0)
    end = width - 1
    e0, e1 = pull(w0, 2 * slot, end, width), pull(w1, 2 * slot, end, width)
    g0, g1 = pull(w0, 2 * slot + 1, end, width), pull(w1, 2 * slot + 1, end, width)
    d0 = pull(d, 2 * slot, end, width)

    def right(block, edge):
        return jnp.where(last, edge, pltpu.roll(block, width - 1, 1))

    def step(mid, down, east, at):
        return cour["keep"][at] * mid + cour["lat"][at] * down + cour["lon"][at] * east

    a0 = step(r0, r1, right(r0, e0), 0)
    a1 = step(r1, r2, right(r1, e1), 1)
    a2 = step(r2, r3, right(r2, d0), 2)
    f0 = step(e0, e1, g0, 3)
    f1 = step(e1, d0, g1, 4)
    b0 = step(a0, a1, right(a0, f0), 0)
    b1 = step(a1, a2, right(a1, f1), 1)
    return b0, b1


def courant(clon, clat, north_c, west_c, rows):
    width = clon.shape[1]

    def edge(row):
        return pltpu.roll(jnp.broadcast_to(row, (8, width)), width - 1, 1)[0:1]

    lon = [clon[0:1], clon[1:2], north_c[rows : rows + 1]]
    lat = [clat[0:1], clat[1:2], north_c[rows + 2 : rows + 3]]
    lon += [edge(west_c[rows : rows + 1]), edge(west_c[rows + 1 : rows + 2])]
    lat += [edge(west_c[rows + 2 : rows + 3]), edge(west_c[rows + 3 : rows + 4])]
    keep = [1.0 - a - b for a, b in zip(lon, lat)]
    return {"rows": rows, "lon": lon, "lat": lat, "keep": keep}


def split3(value):
    high = value.astype(BF16)
    left = value - high.astype(F32)
    mid = left.astype(BF16)
    low = (left - mid.astype(F32)).astype(BF16)
    return high, mid, low


def window_kernel(
    *refs, window, first_level, count, rows, slots, last, grad, regions
):
    refs = list(refs)
    own, north, west, diag, clon, clat, north_c, west_c, stiff, state_h, mats_h = refs[:11]
    refs = refs[11:]
    if grad:
        before, emission, region = refs[:3]
        refs = refs[3:]
    if last and not grad:
        refs = refs[1:]
    if last:
        out_h = refs.pop(0)
        if grad:
            partial = refs.pop(0)
    else:
        lam_out, west_out = refs[:2]
        refs = refs[2:]
    x_s, y_s, flat_s, state_s, mats_s, sems = refs[:6]
    refs = refs[6:]
    spec, width = rows // 2, clon.shape[1]
    get_state = pltpu.make_async_copy(
        state_h.at[window, pl.ds(first_level, count)], state_s, sems.at[0]
    )
    get_mats = pltpu.make_async_copy(
        mats_h.at[:, pl.ds(first_level, count)], mats_s, sems.at[1]
    )
    get_state.start()
    get_mats.start()
    cour = courant(clon, clat, north_c, west_c, rows)
    for lev in range(count):
        b0, b1 = advected(own, north, west, diag, lev, slots[lev], cour)
        x_s[lev, :, 0:width] = b0
        x_s[lev, :, width : 2 * width] = b1
    get_state.wait()
    for lev in range(count):
        flat_s[lev] = state_s[lev].astype(F32)
        y_s[lev, :, 0:width] = flat_s[lev, pl.ds(0, spec, stride=2), :]
        y_s[lev, :, width : 2 * width] = flat_s[lev, pl.ds(1, spec, stride=2), :]
    get_mats.wait()
    live = []
    for lev in range(count):
        both = stiff[first_level + lev]
        live.append(jnp.concatenate([both[0:1], both[1:2]], axis=1))

    def stage(i, carry):
        s = STEPS - 1 - i
        rights = [x_s[lev].astype(BF16) for lev in range(count)]
        cands = [0.4 * x_s[lev] for lev in range(count)]
        for k, share in enumerate((0.3, 0.2, 0.1)):
            prods = [
                jnp.dot(mats_s[s, lev], rights[lev], preferred_element_type=F32)
                for lev in range(count)
            ]
            cands = [cands[lev] + share * prods[lev] for lev in range(count)]
            if k < 2:
                rights = [(prods[lev] * y_s[lev]).astype(BF16) for lev in range(count)]
        for lev in range(count):
            x_s[lev] = jnp.where(live[lev] > s, cands[lev], x_s[lev])
        return carry

    lax.fori_loop(0, STEPS, stage, 0)
    acc = [jnp.zeros((spec, width), F32)] * 2
    for lev in range(count):
        for r in range(2):
            half = x_s[lev, :, r * width : (r + 1) * width]
            if last:
                flat_s[lev, pl.ds(r, spec, stride=2), :] = half
            else:
                lam_out[pl.ds(lev * rows + r, spec, stride=2), :] = half
                acc[r] = place(acc[r], half, lev)
    if not last:
        for r in range(2):
            west_out[pl.ds(r, spec, stride=2), :] = acc[r]
        return
    out_s = refs.pop(0)
    for lev in range(count):
        out_s[lev] = flat_s[lev].astype(BF16)
    put = pltpu.make_async_copy(out_s, out_h.at[pl.ds(first_level, count)], sems.at[2])
    put.start()
    if grad:
        ids = jnp.concatenate([region[0:1], region[1:2]], axis=1)
        labels = lax.broadcasted_iota(jnp.int32, (regions, 2 * width), 0)
        onehot = jnp.where(labels == ids, 1.0, 0.0).astype(BF16)
        total = []
        for r in range(2):
            now = flat_s[0, pl.ds(r, spec, stride=2), :]
            then = before[pl.ds(r, spec, stride=2), :]
            total.append((now + then) * emission[pl.ds(r, spec, stride=2), :])
        contrib = jnp.concatenate(total, axis=1)
        contrib = jnp.concatenate([contrib, jnp.zeros((width - spec, 2 * width), F32)], axis=0)
        result = jnp.zeros((regions, width), F32)
        for piece in split3(contrib):
            result = result + lax.dot_general(
                onehot, piece, (((1,), (1,)), ((), ())), preferred_element_type=F32
            )
        partial[...] = result
    put.wait()


def run_window(
    own, north, west, diag, shared, window, first_level, count, slots, last, extra=None, prior=None
):
    clon, clat, north_c, west_c, stiff, state, mats = shared
    rows, width = state.shape[2], state.shape[3]
    spec = rows // 2
    grad = extra is not None
    regions = 0
    args = [own, north, west, diag, clon, clat, north_c, west_c, stiff, state, mats]
    specs = [VMEM] * 9 + [ANY] * 2
    aliases = {}
    if grad:
        before, emission, region, regions = extra
        args += [before, emission, region]
        specs += [VMEM] * 3
    if last:
        levels = state.shape[1]
        if not grad:
            aliases = {len(args): 0}
            args.append(prior)
            specs.append(ANY)
        out_shape = [jax.ShapeDtypeStruct((levels, rows, width), BF16)]
        out_specs = [ANY]
        if grad:
            out_shape.append(jax.ShapeDtypeStruct((regions, width), F32))
            out_specs.append(VMEM)
    else:
        out_shape = [
            jax.ShapeDtypeStruct((count * rows, width), F32),
            jax.ShapeDtypeStruct((rows, width), F32),
        ]
        out_specs = [VMEM] * 2
    scratch = [
        pltpu.VMEM((count, spec, 2 * width), F32),
        pltpu.VMEM((count, spec, 2 * width), F32),
        pltpu.VMEM((count, rows, width), F32),
        pltpu.VMEM((count, rows, width), BF16),
        pltpu.VMEM((STEPS, count, spec, spec), BF16),
        pltpu.SemaphoreType.DMA((3,)),
    ]
    if last:
        scratch.append(pltpu.VMEM((count, rows, width), BF16))
    body = functools.partial(
        window_kernel,
        window=window,
        first_level=first_level,
        count=count,
        rows=rows,
        slots=slots,
        last=last,
        grad=grad,
        regions=regions,
    )
    return pl.pallas_call(
        body,
        out_shape=out_shape,
        in_specs=specs,
        out_specs=out_specs,
        scratch_shapes=scratch,
        input_output_aliases=aliases,
        name=f"window{window}_from{first_level}",
        compiler_params=pltpu.CompilerParams(vmem_limit_bytes=32 * 2**20),
    )(*args)


def to_north(block):
    bands = lax.axis_size("lat")
    return lax.ppermute(block, "lat", [(i + 1, i) for i in range(bands - 1)])


def to_west(block):
    blocks = lax.axis_size("lon")
    return lax.ppermute(block, "lon", [((j + 1) % blocks, j) for j in range(blocks)])


def to_northwest(block):
    bands, blocks = lax.axis_size("lat"), lax.axis_size("lon")
    route = [
        ((i + 1) * blocks + (j + 1) % blocks, i * blocks + j)
        for i in range(bands - 1)
        for j in range(blocks)
    ]
    return lax.ppermute(block, ("lat", "lon"), route)


def per_device(
    adjoint_in, state, inverses, courant_lon, courant_lat, emission, region_id, stiffness
):
    windows, levels, spec, lat_rows, width = state.shape
    rows = spec * lat_rows
    regions = lax.axis_size("lat") * lax.axis_size("lon")
    adj = adjoint_in.reshape(levels, rows, width)
    flat_state = state.reshape(windows, levels, rows, width)
    flat_em = emission.reshape(rows, width)
    mats = jnp.swapaxes(inverses, 2, 3)
    low1, rest1, west1 = pl.pallas_call(
        functools.partial(pack_kernel, rows=rows),
        out_shape=[
            jax.ShapeDtypeStruct((rows + EXTRA, width), F32),
            jax.ShapeDtypeStruct(((levels - 1) * rows, width), F32),
            jax.ShapeDtypeStruct((rows + EXTRA, width), F32),
        ],
        in_specs=[VMEM] * 3,
        out_specs=[VMEM] * 3,
        name="pack",
    )(adj, courant_lon, courant_lat)
    low1_n = to_north(low1)
    west1_w = to_west(west1)
    west1_d = to_northwest(west1)
    rest1_n = to_north(rest1)
    shared = (courant_lon, courant_lat, low1_n, west1_w, stiffness, flat_state, mats)
    low0, low0_p = run_window(
        low1, low1_n, west1_w, west1_d, shared, 1, 0, 1, [0], False
    )
    low_extra = (low0, flat_em, region_id, regions)
    out, partial = run_window(
        low0, to_north(low0), to_west(low0_p), to_northwest(low0_p),
        shared, 0, 0, 1, [0], True, extra=low_extra,
    )
    rest1_n, partial = lax.optimization_barrier((rest1_n, partial))
    spread = lax.all_to_all(partial, ("lat", "lon"), 0, 0, tiled=True)
    rest0, rest0_p = run_window(
        rest1, rest1_n, west1_w, west1_d, shared, 1, 1, levels - 1, list(range(1, levels)), False
    )
    out = run_window(
        rest0, to_north(rest0), to_west(rest0_p), to_northwest(rest0_p),
        shared, 0, 1, levels - 1, list(range(levels - 1)), True, prior=out,
    )[0]
    grad = jnp.sum(spread, axis=0, keepdims=True)[:, :spec]
    return out.reshape(levels, spec, lat_rows, width), grad


def solution(mesh):
    in_specs = (
        P(None, None, "lat", "lon"),
        P(None, None, None, "lat", "lon"),
        P(),
        P("lat", "lon"),
        P("lat", "lon"),
        P(None, "lat", "lon"),
        P("lat", "lon"),
        P(None, "lat", "lon"),
    )
    out_specs = (P(None, None, "lat", "lon"), P(("lat", "lon"), None))
    return jax.shard_map(
        per_device, mesh=mesh, in_specs=in_specs, out_specs=out_specs, check_vma=False
    )
```

```python
import functools
import jax
import jax.numpy as jnp
from jax import lax
from jax.experimental import pallas as pl
from jax.experimental.pallas import tpu as pltpu
from jax.sharding import PartitionSpec as P

STEPS = 3
EXTRA = 8
TAIL = 104
WIDE = 4
F32 = jnp.float32
BF16 = jnp.bfloat16
ANY = pl.BlockSpec(memory_space=pl.ANY)
HBM = pl.BlockSpec(memory_space=pltpu.HBM)
VMEM = pl.BlockSpec(memory_space=pltpu.VMEM)


def vmem(mib):
    return pltpu.CompilerParams(vmem_limit_bytes=mib * 2**20)


def lanes(shape):
    return lax.broadcasted_iota(jnp.int32, shape, len(shape) - 1)


def place(acc, block, start):
    moved = pltpu.roll(block, start, 1) if start else block
    at = lanes(block.shape)
    return jnp.where((at >= start) & (at < start + WIDE), moved, acc)


def tall(row):
    return jnp.broadcast_to(row, (8, row.shape[1]))


def pack_kernel(adj, clon, clat, stiff, state_h, first, rest, west, state_s, sem, *, rows):
    levels, _, width = adj.shape
    half = width // 2
    get = pltpu.make_async_copy(state_h.at[state_h.shape[0] - 1], state_s, sem)
    get.start()
    acc = jnp.zeros((rows, width), F32)
    grades = jnp.zeros((8, width), F32)
    for lev in range(levels):
        block = adj[lev].astype(F32)
        if lev == 0:
            first[0:rows] = block
        else:
            rest[(lev - 1) * rows : lev * rows] = block
        acc = place(acc, block, WIDE * lev)
        both = stiff[lev].astype(F32)
        grades = place(grades, tall(both[0:1]), WIDE * lev)
        grades = place(grades, tall(both[1:2]), half + WIDE * lev)
    get.wait()
    for lev in range(levels):
        acc = place(acc, state_s[lev].astype(F32), half + WIDE * lev)
    west[0:rows] = acc
    for out in (first, west):
        out[rows : rows + 2] = clon[...]
        out[rows + 2 : rows + 4] = clat[...]
        out[rows + 4 : rows + 8] = grades[0:4]


def pull(block, lane_from, lane_to, width):
    shift = (lane_to - lane_from) % width
    return pltpu.roll(block, shift, 1) if shift else block


def mixed(cour, at, mid, down, east):
    return cour["keep"][at] * mid + cour["lat"][at] * down + cour["lon"][at] * east


def with_keep(lon, lat):
    return {"lon": lon, "lat": lat, "keep": [1.0 - a - b for a, b in zip(lon, lat)]}


def advected(own, north, west, corner, lev, start, cour):
    width = own.shape[1]
    spec = west.shape[0] // 2
    end = width - 1
    last = lanes((spec, width)) == end
    base = lev * 2 * spec

    def pick(ref, first, parity):
        return ref[pl.ds(first + parity, spec, stride=2), :]

    r0, r1 = pick(own, base, 0), pick(own, base, 1)
    r2, r3 = pick(north, base, 0), pick(north, base, 1)
    w0, w1 = pick(west, 0, 0), pick(west, 0, 1)
    e0, e1 = pull(w0, start, end, width), pull(w1, start, end, width)
    g0, g1 = pull(w0, start + 1, end, width), pull(w1, start + 1, end, width)
    d0 = pull(corner, start, end, width)

    def right(block, edge):
        return jnp.where(last, edge, pltpu.roll(block, width - 1, 1))

    a0 = mixed(cour, 0, r0, r1, right(r0, e0))
    a1 = mixed(cour, 1, r1, r2, right(r1, e1))
    a2 = mixed(cour, 2, r2, r3, right(r2, d0))
    f0 = mixed(cour, 3, e0, e1, g0)
    f1 = mixed(cour, 4, e1, d0, g1)
    b0 = mixed(cour, 0, a0, a1, right(a0, f0))
    b1 = mixed(cour, 1, a1, a2, right(a1, f1))
    return b0, b1


def courant(clon, clat, north_c, west_c, rows):
    width = clon.shape[1]

    def edge(row):
        return pltpu.roll(tall(row), width - 1, 1)[0:1]

    lon = [clon[0:1], clon[1:2], north_c[rows : rows + 1]]
    lat = [clat[0:1], clat[1:2], north_c[rows + 2 : rows + 3]]
    lon += [edge(west_c[rows : rows + 1]), edge(west_c[rows + 1 : rows + 2])]
    lat += [edge(west_c[rows + 2 : rows + 3]), edge(west_c[rows + 3 : rows + 4])]
    return with_keep(lon, lat)


def strip_kernel(west, diag, mats, out, *, rows):
    spec, width = rows // 2, west.shape[1]
    half = width // 2
    levels = mats.shape[1]
    at = lanes((spec, width))

    def pick(ref, parity):
        return ref[pl.ds(parity, spec, stride=2), :]

    def spread(row):
        wide = tall(row)
        acc = jnp.zeros((8, width), F32)
        for lev in range(levels):
            acc = place(acc, wide, WIDE * lev)
        return acc[0:1]

    def right(block):
        return pltpu.roll(block, width - 1, 1)

    w0, w1, d0, d1 = pick(west, 0), pick(west, 1), pick(diag, 0), pick(diag, 1)
    lon = [spread(west[rows + i : rows + i + 1]) for i in range(2)]
    lat = [spread(west[rows + i : rows + i + 1]) for i in range(2, 4)]
    lon.append(spread(diag[rows : rows + 1]))
    lat.append(spread(diag[rows + 2 : rows + 3]))
    cour = with_keep(lon, lat)
    a0 = mixed(cour, 0, w0, w1, right(w0))
    a1 = mixed(cour, 1, w1, d0, right(w1))
    a2 = mixed(cour, 2, d0, d1, right(d0))
    b0 = mixed(cour, 0, a0, a1, right(a0))
    b1 = mixed(cour, 1, a1, a2, right(a1))
    value = jnp.where(at < half, b0, pltpu.roll(b1, half, 1))
    factor = jnp.where(at < half, pltpu.roll(w0, half, 1), w1)
    live = west[rows + 4 : rows + 5]
    group = (at & (half - 1)) // WIDE

    def times(s, right_side):
        low = right_side.astype(BF16)
        acc = jnp.dot(mats[s, 0], low, preferred_element_type=F32)
        for lev in range(1, levels):
            prod = jnp.dot(mats[s, lev], low, preferred_element_type=F32)
            acc = jnp.where(group == lev, prod, acc)
        return acc

    def stage(i, value):
        s = STEPS - 1 - i
        one = times(s, value)
        two = times(s, one * factor)
        three = times(s, two * factor)
        cand = 0.4 * value + 0.3 * one + 0.2 * two + 0.1 * three
        return jnp.where(live > s.astype(F32), cand, value)

    value = lax.fori_loop(0, STEPS, stage, value)
    out[pl.ds(0, spec, stride=2), :] = value
    out[pl.ds(1, spec, stride=2), :] = pltpu.roll(value, half, 1)


def sum_kernel(parts, out):
    out[...] = jnp.sum(parts[...], axis=0, keepdims=True)


def split3(value):
    high = value.astype(BF16)
    left = value - high.astype(F32)
    mid = left.astype(BF16)
    low = (left - mid.astype(F32)).astype(BF16)
    return high, mid, low


def window_kernel(
    *refs, window, first_level, count, rows, last, grad, regions
):
    refs = list(refs)
    own, north, west, corner_r, clon, clat, north_c, west_c, stiff, state_h, mats_h = refs[:11]
    refs = refs[11:]
    if grad:
        before, emission, region = refs[:3]
        refs = refs[3:]
    if last and not grad:
        refs = refs[1:]
    if not last:
        edge_r = refs.pop(0)
    if last:
        out_h = refs.pop(0)
        if grad:
            partial = refs.pop(0)
    else:
        lam_out = refs.pop(0)
    x_s, y_s, flat_s, state_s, mats_s, sems = refs[:6]
    refs = refs[6:]
    spec, width = rows // 2, clon.shape[1]
    get_state = pltpu.make_async_copy(
        state_h.at[window, pl.ds(first_level, count)], state_s, sems.at[0]
    )
    get_mats = pltpu.make_async_copy(
        mats_h.at[:, pl.ds(first_level, count)], mats_s, sems.at[1]
    )
    get_state.start()
    get_mats.start()
    cour = courant(clon, clat, north_c, west_c, rows)
    if last:
        corner = north[count * rows : count * rows + spec]
    else:
        corner = corner_r[pl.ds(0, spec, stride=2), :]
    west_v = west.at[0:rows]
    for lev in range(count):
        start = WIDE * (first_level + lev)
        b0, b1 = advected(own, north, west_v, corner, lev, start, cour)
        x_s[lev, :, 0:width] = b0
        x_s[lev, :, width : 2 * width] = b1
    get_state.wait()
    for lev in range(count):
        flat_s[lev] = state_s[lev].astype(F32)
        y_s[lev, :, 0:width] = flat_s[lev, pl.ds(0, spec, stride=2), :]
        y_s[lev, :, width : 2 * width] = flat_s[lev, pl.ds(1, spec, stride=2), :]
    get_mats.wait()
    live = []
    for lev in range(count):
        both = stiff[first_level + lev]
        live.append(jnp.concatenate([both[0:1], both[1:2]], axis=1))

    def stage(i, carry):
        s = STEPS - 1 - i
        rights = [x_s[lev].astype(BF16) for lev in range(count)]
        cands = [0.4 * x_s[lev] for lev in range(count)]
        for k, share in enumerate((0.3, 0.2, 0.1)):
            prods = [
                jnp.dot(mats_s[s, lev], rights[lev], preferred_element_type=F32)
                for lev in range(count)
            ]
            cands = [cands[lev] + share * prods[lev] for lev in range(count)]
            if k < 2:
                rights = [(prods[lev] * y_s[lev]).astype(BF16) for lev in range(count)]
        for lev in range(count):
            x_s[lev] = jnp.where(live[lev] > s, cands[lev], x_s[lev])
        return carry

    lax.fori_loop(0, STEPS, stage, 0)
    for lev in range(count):
        for r in range(2):
            half = x_s[lev, :, r * width : (r + 1) * width]
            if last:
                flat_s[lev, pl.ds(r, spec, stride=2), :] = half
            else:
                lam_out[pl.ds(lev * rows + r, spec, stride=2), :] = half
    if not last:
        lam_out[count * rows : count * rows + spec] = edge_r[pl.ds(0, spec, stride=2), :]
        pad = TAIL - spec
        lam_out[count * rows + spec :] = jnp.zeros((pad, width), F32)
        return
    out_s = refs.pop(0)
    for lev in range(count):
        out_s[lev] = flat_s[lev].astype(BF16)
    put = pltpu.make_async_copy(out_s, out_h.at[pl.ds(first_level, count)], sems.at[2])
    put.start()
    if grad:
        ids = jnp.concatenate([region[0:1], region[1:2]], axis=1)
        labels = lax.broadcasted_iota(jnp.int32, (regions, 2 * width), 0)
        onehot = jnp.where(labels == ids, 1.0, 0.0).astype(BF16)
        total = []
        for r in range(2):
            now = flat_s[0, pl.ds(r, spec, stride=2), :]
            then = before[pl.ds(r, spec, stride=2), :]
            total.append((now + then) * emission[pl.ds(r, spec, stride=2), :])
        contrib = jnp.concatenate(total, axis=1)
        contrib = jnp.concatenate([contrib, jnp.zeros((width - spec, 2 * width), F32)], axis=0)
        result = jnp.zeros((regions, width), F32)
        for piece in split3(contrib):
            result = result + lax.dot_general(
                onehot, piece, (((1,), (1,)), ((), ())), preferred_element_type=F32
            )
        partial[...] = result
    put.wait()


def run_window(
    own, north, west, corner, shared, window, first_level, count, last, extra=None, prior=None, edge=None
):
    clon, clat, north_c, west_c, stiff, state, mats = shared
    rows, width = state.shape[2], state.shape[3]
    spec = rows // 2
    grad = extra is not None
    regions = 0
    args = [own, north, west, corner, clon, clat, north_c, west_c, stiff, state, mats]
    specs = [VMEM] * 9 + [ANY] * 2
    aliases = {}
    if grad:
        before, emission, region, regions = extra
        args += [before, emission, region]
        specs += [VMEM] * 3
    if not last:
        args.append(edge)
        specs.append(VMEM)
    if last:
        levels = state.shape[1]
        if not grad:
            aliases = {len(args): 0}
            args.append(prior)
            specs.append(ANY)
        out_shape = [jax.ShapeDtypeStruct((levels, rows, width), BF16)]
        out_specs = [ANY]
        if grad:
            out_shape.append(jax.ShapeDtypeStruct((regions, width), F32))
            out_specs.append(VMEM)
    else:
        out_shape = [
            jax.ShapeDtypeStruct((count * rows + TAIL, width), F32),
        ]
        out_specs = [VMEM]
    scratch = [
        pltpu.VMEM((count, spec, 2 * width), F32),
        pltpu.VMEM((count, spec, 2 * width), F32),
        pltpu.VMEM((count, rows, width), F32),
        pltpu.VMEM((count, rows, width), BF16),
        pltpu.VMEM((STEPS, count, spec, spec), BF16),
        pltpu.SemaphoreType.DMA((3,)),
    ]
    if last:
        scratch.append(pltpu.VMEM((count, rows, width), BF16))
    body = functools.partial(
        window_kernel,
        window=window,
        first_level=first_level,
        count=count,
        rows=rows,
        last=last,
        grad=grad,
        regions=regions,
    )
    return pl.pallas_call(
        body,
        out_shape=out_shape,
        in_specs=specs,
        out_specs=out_specs,
        scratch_shapes=scratch,
        input_output_aliases=aliases,
        name=f"window{window}_from{first_level}",
        compiler_params=vmem(40 if count > 1 else 8),
    )(*args)


def to_north(block):
    bands = lax.axis_size("lat")
    return lax.ppermute(block, "lat", [(i + 1, i) for i in range(bands - 1)])


def to_west(block):
    blocks = lax.axis_size("lon")
    return lax.ppermute(block, "lon", [((j + 1) % blocks, j) for j in range(blocks)])


def to_northwest(block):
    bands, blocks = lax.axis_size("lat"), lax.axis_size("lon")
    route = [
        ((i + 1) * blocks + (j + 1) % blocks, i * blocks + j)
        for i in range(bands - 1)
        for j in range(blocks)
    ]
    return lax.ppermute(block, ("lat", "lon"), route)


def per_device(
    adjoint_in, state, inverses, courant_lon, courant_lat, emission, region_id, stiffness
):
    windows, levels, spec, lat_rows, width = state.shape
    rows = spec * lat_rows
    regions = lax.axis_size("lat") * lax.axis_size("lon")
    adj = adjoint_in.reshape(levels, rows, width)
    flat_state = state.reshape(windows, levels, rows, width)
    flat_em = emission.reshape(rows, width)
    mats = jnp.swapaxes(inverses, 2, 3)
    low1, rest1, west1 = pl.pallas_call(
        functools.partial(pack_kernel, rows=rows),
        out_shape=[
            jax.ShapeDtypeStruct((rows + EXTRA, width), F32),
            jax.ShapeDtypeStruct(((levels - 1) * rows, width), F32),
            jax.ShapeDtypeStruct((rows + EXTRA, width), F32),
        ],
        in_specs=[VMEM] * 4 + [HBM],
        out_specs=[VMEM] * 3,
        scratch_shapes=[pltpu.VMEM((levels, rows, width), BF16), pltpu.SemaphoreType.DMA],
        name="pack",
        compiler_params=vmem(56),
    )(adj, courant_lon, courant_lat, stiffness, flat_state)
    low1_n = to_north(low1)
    west1_w = to_west(west1)
    west1_d = to_northwest(west1)
    rest1, low1_n, west1_w, west1_d = lax.optimization_barrier(
        (rest1, low1_n, west1_w, west1_d)
    )
    rest1_n = to_north(rest1)
    shared = (courant_lon, courant_lat, low1_n, west1_w, stiffness, flat_state, mats)
    strip = pl.pallas_call(
        functools.partial(strip_kernel, rows=rows),
        out_shape=jax.ShapeDtypeStruct((rows, width), F32),
        in_specs=[VMEM] * 3,
        out_specs=VMEM,
        name="strip",
        compiler_params=vmem(8),
    )(west1_w, west1_d, mats)
    low0 = run_window(
        low1, low1_n, west1_w, west1_d, shared, 1, 0, 1, False, edge=strip
    )[0]
    low0_n = to_north(low0)
    rest1_n, low0_n = lax.optimization_barrier((rest1_n, low0_n))
    rest0 = run_window(
        rest1, rest1_n, west1_w, west1_d, shared, 1, 1, levels - 1, False, edge=strip
    )[0]
    rest0_n = to_north(rest0)
    low0_n, rest0 = lax.optimization_barrier((low0_n, rest0))
    low_extra = (low0, flat_em, region_id, regions)
    out, partial = run_window(
        low0, low0_n, strip, strip, shared, 0, 0, 1, True, extra=low_extra
    )
    spread = lax.all_to_all(partial, ("lat", "lon"), 0, 0, tiled=True)
    out = run_window(
        rest0, rest0_n, strip, strip, shared, 0, 1, levels - 1, True, prior=out
    )[0]
    out, spread = lax.optimization_barrier((out, spread))
    grad = pl.pallas_call(
        sum_kernel,
        out_shape=jax.ShapeDtypeStruct((1, width), F32),
        in_specs=[VMEM],
        out_specs=VMEM,
        name="gather_sum",
        compiler_params=vmem(4),
    )(spread)[:, :spec]
    return out.reshape(levels, spec, lat_rows, width), grad


def solution(mesh):
    in_specs = (
        P(None, None, "lat", "lon"),
        P(None, None, None, "lat", "lon"),
        P(),
        P("lat", "lon"),
        P("lat", "lon"),
        P(None, "lat", "lon"),
        P("lat", "lon"),
        P(None, "lat", "lon"),
    )
    out_specs = (P(None, None, "lat", "lon"), P(("lat", "lon"), None))
    return jax.shard_map(
        per_device, mesh=mesh, in_specs=in_specs, out_specs=out_specs, check_vma=False
    )
```

```python
import functools
import jax
import jax.numpy as jnp
from jax import lax
from jax.experimental import pallas as pl
from jax.experimental.pallas import tpu as pltpu
from jax.sharding import PartitionSpec as P

STEPS = 3
EXTRA = 8
TAIL = 104
WIDE = 4
COST = ((10_000_000, 10_000_000), (40_000_000, 10_000_000))
F32 = jnp.float32
BF16 = jnp.bfloat16
ANY = pl.BlockSpec(memory_space=pl.ANY)
HBM = pl.BlockSpec(memory_space=pltpu.HBM)
VMEM = pl.BlockSpec(memory_space=pltpu.VMEM)


def vmem(mib):
    return pltpu.CompilerParams(vmem_limit_bytes=mib * 2**20)


def lanes(shape):
    return lax.broadcasted_iota(jnp.int32, shape, len(shape) - 1)


def place(acc, block, start):
    moved = pltpu.roll(block, start, 1) if start else block
    at = lanes(block.shape)
    return jnp.where((at >= start) & (at < start + WIDE), moved, acc)


def tall(row):
    return jnp.broadcast_to(row, (8, row.shape[1]))


def pack_kernel(adj, clon, clat, stiff, state_h, first, state_s, sem, *, rows):
    levels, _, width = adj.shape
    half = width // 2
    get = pltpu.make_async_copy(state_h.at[state_h.shape[0] - 1], state_s, sem)
    get.start()
    acc = jnp.zeros((rows, width), F32)
    grades = jnp.zeros((8, width), F32)
    for lev in range(levels):
        block = adj[lev].astype(F32)
        if lev == 0:
            first[0:rows] = block
        acc = place(acc, block, WIDE * lev)
        both = stiff[lev].astype(F32)
        grades = place(grades, tall(both[0:1]), WIDE * lev)
        grades = place(grades, tall(both[1:2]), half + WIDE * lev)
    get.wait()
    for lev in range(levels):
        acc = place(acc, state_s[lev].astype(F32), half + WIDE * lev)
    first[rows : 2 * rows] = acc
    first[2 * rows : 2 * rows + 2] = clon[...]
    first[2 * rows + 2 : 2 * rows + 4] = clat[...]
    first[2 * rows + 4 : 2 * rows + 8] = grades[0:4]


def rest_kernel(adj, first, rest, *, rows):
    for lev in range(1, adj.shape[0]):
        rest[(lev - 1) * rows : lev * rows] = adj[lev].astype(F32)


def pull(block, lane_from, lane_to, width):
    shift = (lane_to - lane_from) % width
    return pltpu.roll(block, shift, 1) if shift else block


def mixed(cour, at, mid, down, east):
    return cour["keep"][at] * mid + cour["lat"][at] * down + cour["lon"][at] * east


def with_keep(lon, lat):
    return {"lon": lon, "lat": lat, "keep": [1.0 - a - b for a, b in zip(lon, lat)]}


def advected(own, north, west, corner, lev, start, cour):
    width = own.shape[1]
    spec = west.shape[0] // 2
    end = width - 1
    last = lanes((spec, width)) == end
    base = lev * 2 * spec

    def pick(ref, first, parity):
        return ref[pl.ds(first + parity, spec, stride=2), :]

    r0, r1 = pick(own, base, 0), pick(own, base, 1)
    r2, r3 = pick(north, base, 0), pick(north, base, 1)
    w0, w1 = pick(west, 0, 0), pick(west, 0, 1)
    e0, e1 = pull(w0, start, end, width), pull(w1, start, end, width)
    g0, g1 = pull(w0, start + 1, end, width), pull(w1, start + 1, end, width)
    d0 = pull(corner, start, end, width)

    def right(block, edge):
        return jnp.where(last, edge, pltpu.roll(block, width - 1, 1))

    a0 = mixed(cour, 0, r0, r1, right(r0, e0))
    a1 = mixed(cour, 1, r1, r2, right(r1, e1))
    a2 = mixed(cour, 2, r2, r3, right(r2, d0))
    f0 = mixed(cour, 3, e0, e1, g0)
    f1 = mixed(cour, 4, e1, d0, g1)
    b0 = mixed(cour, 0, a0, a1, right(a0, f0))
    b1 = mixed(cour, 1, a1, a2, right(a1, f1))
    return b0, b1


def courant(clon, clat, north_c, west_c, rows):
    width = clon.shape[1]

    def edge(row):
        return pltpu.roll(tall(row), width - 1, 1)[0:1]

    lon = [clon[0:1], clon[1:2], north_c[2 * rows : 2 * rows + 1]]
    lat = [clat[0:1], clat[1:2], north_c[2 * rows + 2 : 2 * rows + 3]]
    lon += [edge(west_c[rows : rows + 1]), edge(west_c[rows + 1 : rows + 2])]
    lat += [edge(west_c[rows + 2 : rows + 3]), edge(west_c[rows + 3 : rows + 4])]
    return with_keep(lon, lat)


def strip_kernel(both, mats, out, *, rows):
    west, diag = both.at[0 : rows + EXTRA], both.at[rows + EXTRA : 2 * (rows + EXTRA)]
    spec, width = rows // 2, both.shape[1]
    half = width // 2
    levels = mats.shape[1]
    at = lanes((spec, width))

    def pick(ref, parity):
        return ref[pl.ds(parity, spec, stride=2), :]

    def spread(row):
        wide = tall(row)
        acc = jnp.zeros((8, width), F32)
        for lev in range(levels):
            acc = place(acc, wide, WIDE * lev)
        return acc[0:1]

    def right(block):
        return pltpu.roll(block, width - 1, 1)

    w0, w1, d0, d1 = pick(west, 0), pick(west, 1), pick(diag, 0), pick(diag, 1)
    lon = [spread(west[rows + i : rows + i + 1]) for i in range(2)]
    lat = [spread(west[rows + i : rows + i + 1]) for i in range(2, 4)]
    lon.append(spread(diag[rows : rows + 1]))
    lat.append(spread(diag[rows + 2 : rows + 3]))
    cour = with_keep(lon, lat)
    a0 = mixed(cour, 0, w0, w1, right(w0))
    a1 = mixed(cour, 1, w1, d0, right(w1))
    a2 = mixed(cour, 2, d0, d1, right(d0))
    b0 = mixed(cour, 0, a0, a1, right(a0))
    b1 = mixed(cour, 1, a1, a2, right(a1))
    value = jnp.where(at < half, b0, pltpu.roll(b1, half, 1))
    factor = jnp.where(at < half, pltpu.roll(w0, half, 1), w1)
    live = west[rows + 4 : rows + 5]
    group = (at & (half - 1)) // WIDE

    def times(s, right_side):
        low = right_side.astype(BF16)
        acc = jnp.dot(mats[s, 0], low, preferred_element_type=F32)
        for lev in range(1, levels):
            prod = jnp.dot(mats[s, lev], low, preferred_element_type=F32)
            acc = jnp.where(group == lev, prod, acc)
        return acc

    def stage(i, value):
        s = STEPS - 1 - i
        one = times(s, value)
        two = times(s, one * factor)
        three = times(s, two * factor)
        cand = 0.4 * value + 0.3 * one + 0.2 * two + 0.1 * three
        return jnp.where(live > s.astype(F32), cand, value)

    value = lax.fori_loop(0, STEPS, stage, value)
    out[pl.ds(0, spec, stride=2), :] = value
    out[pl.ds(1, spec, stride=2), :] = pltpu.roll(value, half, 1)


def sum_kernel(parts, out):
    out[...] = jnp.sum(parts[...], axis=0, keepdims=True)


def split3(value):
    high = value.astype(BF16)
    left = value - high.astype(F32)
    mid = left.astype(BF16)
    low = (left - mid.astype(F32)).astype(BF16)
    return high, mid, low


def window_kernel(
    *refs, window, first_level, count, rows, last, grad, regions
):
    refs = list(refs)
    own, north, west, corner_r, clon, clat, north_c, west_c, stiff, state_h, mats_h = refs[:11]
    refs = refs[11:]
    if grad:
        before, emission, region = refs[:3]
        refs = refs[3:]
    if last and not grad:
        refs = refs[1:]
    if not last and first_level == 0:
        edge_r = refs.pop(0)
    if last:
        out_h = refs.pop(0)
        if grad:
            partial = refs.pop(0)
    else:
        lam_out = refs.pop(0)
    x_s, y_s, flat_s, state_s, mats_s, sems = refs[:6]
    refs = refs[6:]
    spec, width = rows // 2, clon.shape[1]
    get_state = pltpu.make_async_copy(
        state_h.at[window, pl.ds(first_level, count)], state_s, sems.at[0]
    )
    get_mats = pltpu.make_async_copy(
        mats_h.at[:, pl.ds(first_level, count)], mats_s, sems.at[1]
    )
    get_state.start()
    get_mats.start()
    cour = courant(clon, clat, north_c, west_c, rows)
    if last:
        corner = corner_r[rows : rows + spec]
    else:
        corner = corner_r[pl.ds(rows + EXTRA, spec, stride=2), :]
    west_v = west.at[0:rows]
    for lev in range(count):
        start = WIDE * (first_level + lev)
        b0, b1 = advected(own, north, west_v, corner, lev, start, cour)
        x_s[lev, :, 0:width] = b0
        x_s[lev, :, width : 2 * width] = b1
    get_state.wait()
    for lev in range(count):
        flat_s[lev] = state_s[lev].astype(F32)
        y_s[lev, :, 0:width] = flat_s[lev, pl.ds(0, spec, stride=2), :]
        y_s[lev, :, width : 2 * width] = flat_s[lev, pl.ds(1, spec, stride=2), :]
    get_mats.wait()
    live = []
    for lev in range(count):
        both = stiff[first_level + lev]
        live.append(jnp.concatenate([both[0:1], both[1:2]], axis=1))

    def stage(i, carry):
        s = STEPS - 1 - i
        rights = [x_s[lev].astype(BF16) for lev in range(count)]
        cands = [0.4 * x_s[lev] for lev in range(count)]
        for k, share in enumerate((0.3, 0.2, 0.1)):
            prods = [
                jnp.dot(mats_s[s, lev], rights[lev], preferred_element_type=F32)
                for lev in range(count)
            ]
            cands = [cands[lev] + share * prods[lev] for lev in range(count)]
            if k < 2:
                rights = [(prods[lev] * y_s[lev]).astype(BF16) for lev in range(count)]
        for lev in range(count):
            x_s[lev] = jnp.where(live[lev] > s, cands[lev], x_s[lev])
        return carry

    lax.fori_loop(0, STEPS, stage, 0)
    for lev in range(count):
        for r in range(2):
            half = x_s[lev, :, r * width : (r + 1) * width]
            if last:
                flat_s[lev, pl.ds(r, spec, stride=2), :] = half
            else:
                lam_out[pl.ds(lev * rows + r, spec, stride=2), :] = half
    if not last:
        if first_level == 0:
            lam_out[rows : rows + spec] = edge_r[pl.ds(0, spec, stride=2), :]
            lam_out[rows + spec :] = jnp.zeros((TAIL - spec, width), F32)
        return
    out_s = refs.pop(0)
    for lev in range(count):
        out_s[lev] = flat_s[lev].astype(BF16)
    put = pltpu.make_async_copy(out_s, out_h.at[pl.ds(first_level, count)], sems.at[2])
    put.start()
    if grad:
        ids = jnp.concatenate([region[0:1], region[1:2]], axis=1)
        labels = lax.broadcasted_iota(jnp.int32, (regions, 2 * width), 0)
        onehot = jnp.where(labels == ids, 1.0, 0.0).astype(BF16)
        total = []
        for r in range(2):
            now = flat_s[0, pl.ds(r, spec, stride=2), :]
            then = before[pl.ds(r, spec, stride=2), :]
            total.append((now + then) * emission[pl.ds(r, spec, stride=2), :])
        contrib = jnp.concatenate(total, axis=1)
        contrib = jnp.concatenate([contrib, jnp.zeros((width - spec, 2 * width), F32)], axis=0)
        result = jnp.zeros((regions, width), F32)
        for piece in split3(contrib):
            result = result + lax.dot_general(
                onehot, piece, (((1,), (1,)), ((), ())), preferred_element_type=F32
            )
        partial[...] = result
    put.wait()


def run_window(
    own, north, west, corner, shared, window, first_level, count, last, extra=None, prior=None, edge=None
):
    clon, clat, north_c, west_c, stiff, state, mats = shared
    rows, width = state.shape[2], state.shape[3]
    spec = rows // 2
    grad = extra is not None
    regions = 0
    args = [own, north, west, corner, clon, clat, north_c, west_c, stiff, state, mats]
    specs = [VMEM] * 9 + [ANY] * 2
    aliases = {}
    if grad:
        before, emission, region, regions = extra
        args += [before, emission, region]
        specs += [VMEM] * 3
    if edge is not None:
        args.append(edge)
        specs.append(VMEM)
    if last:
        levels = state.shape[1]
        if not grad:
            aliases = {len(args): 0}
            args.append(prior)
            specs.append(ANY)
        out_shape = [jax.ShapeDtypeStruct((levels, rows, width), BF16)]
        out_specs = [ANY]
        if grad:
            out_shape.append(jax.ShapeDtypeStruct((regions, width), F32))
            out_specs.append(VMEM)
    else:
        out_shape = [
            jax.ShapeDtypeStruct((count * rows + (0 if edge is None else TAIL), width), F32),
        ]
        out_specs = [VMEM]
    scratch = [
        pltpu.VMEM((count, spec, 2 * width), F32),
        pltpu.VMEM((count, spec, 2 * width), F32),
        pltpu.VMEM((count, rows, width), F32),
        pltpu.VMEM((count, rows, width), BF16),
        pltpu.VMEM((STEPS, count, spec, spec), BF16),
        pltpu.SemaphoreType.DMA((3,)),
    ]
    if last:
        scratch.append(pltpu.VMEM((count, rows, width), BF16))
    body = functools.partial(
        window_kernel,
        window=window,
        first_level=first_level,
        count=count,
        rows=rows,
        last=last,
        grad=grad,
        regions=regions,
    )
    return pl.pallas_call(
        body,
        out_shape=out_shape,
        in_specs=specs,
        out_specs=out_specs,
        scratch_shapes=scratch,
        input_output_aliases=aliases,
        name=f"window{window}_from{first_level}",
        cost_estimate=pl.CostEstimate(flops=0, transcendentals=0, bytes_accessed=COST[window][first_level]),
        compiler_params=vmem(40 if count > 1 else 8),
    )(*args)


def to_north(block):
    bands = lax.axis_size("lat")
    return lax.ppermute(block, "lat", [(i + 1, i) for i in range(bands - 1)])


def to_west(block):
    blocks = lax.axis_size("lon")
    return lax.ppermute(block, "lon", [((j + 1) % blocks, j) for j in range(blocks)])


def per_device(
    adjoint_in, state, inverses, courant_lon, courant_lat, emission, region_id, stiffness
):
    windows, levels, spec, lat_rows, width = state.shape
    rows = spec * lat_rows
    regions = lax.axis_size("lat") * lax.axis_size("lon")
    adj = adjoint_in.reshape(levels, rows, width)
    flat_state = state.reshape(windows, levels, rows, width)
    flat_em = emission.reshape(rows, width)
    mats = jnp.swapaxes(inverses, 2, 3)
    low1 = pl.pallas_call(
        functools.partial(pack_kernel, rows=rows),
        out_shape=jax.ShapeDtypeStruct((2 * rows + EXTRA, width), F32),
        in_specs=[VMEM] * 4 + [HBM],
        out_specs=VMEM,
        scratch_shapes=[pltpu.VMEM((levels, rows, width), BF16), pltpu.SemaphoreType.DMA],
        name="pack",
        compiler_params=vmem(56),
    )(adj, courant_lon, courant_lat, stiffness, flat_state)
    low1_n = to_north(low1)
    rest1 = pl.pallas_call(
        functools.partial(rest_kernel, rows=rows),
        out_shape=jax.ShapeDtypeStruct(((levels - 1) * rows, width), F32),
        in_specs=[VMEM, ANY],
        out_specs=VMEM,
        name="rest",
        compiler_params=vmem(56),
    )(adj, low1)
    rest1, low1_n = lax.optimization_barrier((rest1, low1_n))
    rest1_n = to_north(rest1)
    west1_w = to_west(jnp.concatenate([low1[rows:], low1_n[rows:]], axis=0))
    shared = (courant_lon, courant_lat, low1_n, west1_w, stiffness, flat_state, mats)
    strip = pl.pallas_call(
        functools.partial(strip_kernel, rows=rows),
        out_shape=jax.ShapeDtypeStruct((rows, width), F32),
        in_specs=[VMEM] * 2,
        out_specs=VMEM,
        name="strip",
        cost_estimate=pl.CostEstimate(flops=0, transcendentals=0, bytes_accessed=40_000_000),
        compiler_params=vmem(8),
    )(west1_w, mats)
    low0 = run_window(
        low1, low1_n, west1_w, west1_w, shared, 1, 0, 1, False, edge=strip
    )[0]
    low0_n = to_north(low0)
    rest1_n, low0_n = lax.optimization_barrier((rest1_n, low0_n))
    rest0 = run_window(
        rest1, rest1_n, west1_w, west1_w, shared, 1, 1, levels - 1, False
    )[0]
    rest0_n = to_north(rest0)
    low0_n, rest0 = lax.optimization_barrier((low0_n, rest0))
    low_extra = (low0, flat_em, region_id, regions)
    out, partial = run_window(
        low0, low0_n, strip, low0_n, shared, 0, 0, 1, True, extra=low_extra
    )
    spread = lax.all_to_all(partial, ("lat", "lon"), 0, 0, tiled=True)
    out = run_window(
        rest0, rest0_n, strip, low0_n, shared, 0, 1, levels - 1, True, prior=out
    )[0]
    out, spread = lax.optimization_barrier((out, spread))
    grad = pl.pallas_call(
        sum_kernel,
        out_shape=jax.ShapeDtypeStruct((1, width), F32),
        in_specs=[VMEM],
        out_specs=VMEM,
        name="gather_sum",
        compiler_params=vmem(4),
    )(spread)[:, :spec]
    return out.reshape(levels, spec, lat_rows, width), grad


def solution(mesh):
    in_specs = (
        P(None, None, "lat", "lon"),
        P(None, None, None, "lat", "lon"),
        P(),
        P("lat", "lon"),
        P("lat", "lon"),
        P(None, "lat", "lon"),
        P("lat", "lon"),
        P(None, "lat", "lon"),
    )
    out_specs = (P(None, None, "lat", "lon"), P(("lat", "lon"), None))
    return jax.shard_map(
        per_device, mesh=mesh, in_specs=in_specs, out_specs=out_specs, check_vma=False
    )
```

```python
import functools
import jax
import jax.numpy as jnp
from jax import lax
from jax.experimental import pallas as pl
from jax.experimental.pallas import tpu as pltpu
from jax.sharding import PartitionSpec as P

STEPS = 3
EXTRA = 8
TAIL = 104
WIDE = 4
COST = ((10_000_000, 10_000_000), (40_000_000, 10_000_000))
F32 = jnp.float32
BF16 = jnp.bfloat16
ANY = pl.BlockSpec(memory_space=pl.ANY)
HBM = pl.BlockSpec(memory_space=pltpu.HBM)
VMEM = pl.BlockSpec(memory_space=pltpu.VMEM)


def vmem(mib):
    return pltpu.CompilerParams(vmem_limit_bytes=mib * 2**20)


def lanes(shape):
    return lax.broadcasted_iota(jnp.int32, shape, len(shape) - 1)


def place(acc, block, start):
    moved = pltpu.roll(block, start, 1) if start else block
    at = lanes(block.shape)
    return jnp.where((at >= start) & (at < start + WIDE), moved, acc)


def tall(row):
    return jnp.broadcast_to(row, (8, row.shape[1]))


def folded_rows(rows):
    return -(-rows // 16) * 8


def pack_kernel(adj, clon, clat, stiff, state_h, first, state_s, sem, *, rows):
    levels, _, width = adj.shape
    half = width // 2
    get = pltpu.make_async_copy(state_h.at[state_h.shape[0] - 1], state_s, sem)
    get.start()
    acc = jnp.zeros((rows, width), F32)
    grades = jnp.zeros((8, width), F32)
    for lev in range(levels):
        block = adj[lev].astype(F32)
        if lev == 0:
            first[0:rows] = block
        acc = place(acc, block, WIDE * lev)
        both = stiff[lev].astype(F32)
        grades = place(grades, tall(both[0:1]), WIDE * lev)
        grades = place(grades, tall(both[1:2]), half + WIDE * lev)
    get.wait()
    for lev in range(levels):
        acc = place(acc, state_s[lev].astype(F32), half // 2 + WIDE * lev)
    folded = folded_rows(rows)
    upper = jnp.concatenate([acc[folded:], jnp.zeros((2 * folded - rows, width), F32)], axis=0)
    first[rows : rows + folded] = acc[0:folded] + pltpu.roll(upper, half, 1)
    at = rows + folded
    first[at : at + 2] = clon[...]
    first[at + 2 : at + 4] = clat[...]
    first[at + 4 : at + 8] = grades[0:4]


def rest_kernel(adj, first, rest, *, rows):
    for lev in range(1, adj.shape[0]):
        rest[(lev - 1) * rows : lev * rows] = adj[lev].astype(F32)


def pull(block, lane_from, lane_to, width):
    shift = (lane_to - lane_from) % width
    return pltpu.roll(block, shift, 1) if shift else block


def mixed(cour, at, mid, down, east):
    return cour["keep"][at] * mid + cour["lat"][at] * down + cour["lon"][at] * east


def with_keep(lon, lat):
    return {"lon": lon, "lat": lat, "keep": [1.0 - a - b for a, b in zip(lon, lat)]}


def advected(own, north, west, corner, lev, start, cour):
    width = own.shape[1]
    spec = west.shape[0] // 2
    end = width - 1
    last = lanes((spec, width)) == end
    base = lev * 2 * spec

    def pick(ref, first, parity):
        return ref[pl.ds(first + parity, spec, stride=2), :]

    r0, r1 = pick(own, base, 0), pick(own, base, 1)
    r2, r3 = pick(north, base, 0), pick(north, base, 1)
    w0, w1 = pick(west, 0, 0), pick(west, 0, 1)
    e0, e1 = pull(w0, start, end, width), pull(w1, start, end, width)
    g0, g1 = pull(w0, start + 1, end, width), pull(w1, start + 1, end, width)
    d0 = pull(corner, start, end, width)

    def right(block, edge):
        return jnp.where(last, edge, pltpu.roll(block, width - 1, 1))

    a0 = mixed(cour, 0, r0, r1, right(r0, e0))
    a1 = mixed(cour, 1, r1, r2, right(r1, e1))
    a2 = mixed(cour, 2, r2, r3, right(r2, d0))
    f0 = mixed(cour, 3, e0, e1, g0)
    f1 = mixed(cour, 4, e1, d0, g1)
    b0 = mixed(cour, 0, a0, a1, right(a0, f0))
    b1 = mixed(cour, 1, a1, a2, right(a1, f1))
    return b0, b1


def courant(clon, clat, north_c, west_c, rows):
    width = clon.shape[1]

    def edge(row):
        return pltpu.roll(tall(row), width - 1, 1)[0:1]

    at = rows + folded_rows(rows)
    lon = [clon[0:1], clon[1:2], north_c[at : at + 1]]
    lat = [clat[0:1], clat[1:2], north_c[at + 2 : at + 3]]
    lon += [edge(west_c[rows : rows + 1]), edge(west_c[rows + 1 : rows + 2])]
    lat += [edge(west_c[rows + 2 : rows + 3]), edge(west_c[rows + 3 : rows + 4])]
    return with_keep(lon, lat)


def strip_kernel(packed, mats, out, both, *, rows):
    folded = folded_rows(rows)
    for i in range(2):
        src, dst = i * (folded + EXTRA), i * (rows + EXTRA)
        block = packed[src : src + folded]
        both[dst : dst + folded] = block
        both[dst + folded : dst + rows] = pltpu.roll(block, block.shape[1] // 2, 1)[0 : rows - folded]
        both[dst + rows : dst + rows + EXTRA] = packed[src + folded : src + folded + EXTRA]
    west, diag = both.at[0 : rows + EXTRA], both.at[rows + EXTRA : 2 * (rows + EXTRA)]
    spec, width = rows // 2, both.shape[1]
    half = width // 2
    levels = mats.shape[1]
    at = lanes((spec, width))

    def pick(ref, parity):
        return ref[pl.ds(parity, spec, stride=2), :]

    def spread(row):
        wide = tall(row)
        acc = jnp.zeros((8, width), F32)
        for lev in range(levels):
            acc = place(acc, wide, WIDE * lev)
        return acc[0:1]

    def right(block):
        return pltpu.roll(block, width - 1, 1)

    w0, w1, d0, d1 = pick(west, 0), pick(west, 1), pick(diag, 0), pick(diag, 1)
    lon = [spread(west[rows + i : rows + i + 1]) for i in range(2)]
    lat = [spread(west[rows + i : rows + i + 1]) for i in range(2, 4)]
    lon.append(spread(diag[rows : rows + 1]))
    lat.append(spread(diag[rows + 2 : rows + 3]))
    cour = with_keep(lon, lat)
    a0 = mixed(cour, 0, w0, w1, right(w0))
    a1 = mixed(cour, 1, w1, d0, right(w1))
    a2 = mixed(cour, 2, d0, d1, right(d0))
    b0 = mixed(cour, 0, a0, a1, right(a0))
    b1 = mixed(cour, 1, a1, a2, right(a1))
    value = jnp.where(at < half, b0, pltpu.roll(b1, half, 1))
    quarter = half // 2
    factor = jnp.where(at < half, pltpu.roll(w0, width - quarter, 1), pltpu.roll(w1, quarter, 1))
    live = west[rows + 4 : rows + 5]
    group = (at & (half - 1)) // WIDE

    def times(s, right_side):
        low = right_side.astype(BF16)
        acc = jnp.dot(mats[s, 0], low, preferred_element_type=F32)
        for lev in range(1, levels):
            prod = jnp.dot(mats[s, lev], low, preferred_element_type=F32)
            acc = jnp.where(group == lev, prod, acc)
        return acc

    def stage(i, value):
        s = STEPS - 1 - i
        one = times(s, value)
        two = times(s, one * factor)
        three = times(s, two * factor)
        cand = 0.4 * value + 0.3 * one + 0.2 * two + 0.1 * three
        return jnp.where(live > s.astype(F32), cand, value)

    value = lax.fori_loop(0, STEPS, stage, value)
    out[pl.ds(0, spec, stride=2), :] = value
    out[pl.ds(1, spec, stride=2), :] = pltpu.roll(value, half, 1)


def sum_kernel(parts, out):
    out[...] = jnp.sum(parts[...], axis=0, keepdims=True)


def split3(value):
    high = value.astype(BF16)
    left = value - high.astype(F32)
    mid = left.astype(BF16)
    low = (left - mid.astype(F32)).astype(BF16)
    return high, mid, low


def window_kernel(
    *refs, window, first_level, count, rows, last, grad, regions
):
    refs = list(refs)
    own, north, west, corner_r, clon, clat, north_c, west_c, stiff, state_h, mats_h = refs[:11]
    refs = refs[11:]
    if grad:
        before, emission, region = refs[:3]
        refs = refs[3:]
    if last and not grad:
        refs = refs[1:]
    if not last and first_level == 0:
        edge_r = refs.pop(0)
    if last:
        out_h = refs.pop(0)
        if grad:
            mine, theirs = refs.pop(0), refs.pop(0)
    else:
        lam_out = refs.pop(0)
    x_s, y_s, flat_s, state_s, mats_s, sems = refs[:6]
    refs = refs[6:]
    spec, width = rows // 2, clon.shape[1]
    get_state = pltpu.make_async_copy(
        state_h.at[window, pl.ds(first_level, count)], state_s, sems.at[0]
    )
    get_mats = pltpu.make_async_copy(
        mats_h.at[:, pl.ds(first_level, count)], mats_s, sems.at[1]
    )
    get_state.start()
    get_mats.start()
    cour = courant(clon, clat, north_c, west_c, rows)
    if last:
        corner = corner_r[rows : rows + spec]
    else:
        corner = corner_r[pl.ds(rows + EXTRA, spec, stride=2), :]
    west_v = west.at[0:rows]
    for lev in range(count):
        start = WIDE * (first_level + lev)
        b0, b1 = advected(own, north, west_v, corner, lev, start, cour)
        x_s[lev, :, 0:width] = b0
        x_s[lev, :, width : 2 * width] = b1
    get_state.wait()
    for lev in range(count):
        flat_s[lev] = state_s[lev].astype(F32)
        y_s[lev, :, 0:width] = flat_s[lev, pl.ds(0, spec, stride=2), :]
        y_s[lev, :, width : 2 * width] = flat_s[lev, pl.ds(1, spec, stride=2), :]
    get_mats.wait()
    live = []
    for lev in range(count):
        both = stiff[first_level + lev]
        live.append(jnp.concatenate([both[0:1], both[1:2]], axis=1))

    def stage(i, carry):
        s = STEPS - 1 - i
        rights = [x_s[lev].astype(BF16) for lev in range(count)]
        cands = [0.4 * x_s[lev] for lev in range(count)]
        for k, share in enumerate((0.3, 0.2, 0.1)):
            prods = [
                jnp.dot(mats_s[s, lev], rights[lev], preferred_element_type=F32)
                for lev in range(count)
            ]
            cands = [cands[lev] + share * prods[lev] for lev in range(count)]
            if k < 2:
                rights = [(prods[lev] * y_s[lev]).astype(BF16) for lev in range(count)]
        for lev in range(count):
            x_s[lev] = jnp.where(live[lev] > s, cands[lev], x_s[lev])
        return carry

    lax.fori_loop(0, STEPS, stage, 0)
    for lev in range(count):
        for r in range(2):
            half = x_s[lev, :, r * width : (r + 1) * width]
            if last:
                flat_s[lev, pl.ds(r, spec, stride=2), :] = half
            else:
                lam_out[pl.ds(lev * rows + r, spec, stride=2), :] = half
    if not last:
        if first_level == 0:
            lam_out[rows : rows + spec] = edge_r[pl.ds(0, spec, stride=2), :]
            lam_out[rows + spec :] = jnp.zeros((TAIL - spec, width), F32)
        return
    out_s = refs.pop(0)
    for lev in range(count):
        out_s[lev] = flat_s[lev].astype(BF16)
    put = pltpu.make_async_copy(out_s, out_h.at[pl.ds(first_level, count)], sems.at[2])
    put.start()
    if grad:
        ids = jnp.concatenate([region[0:1], region[1:2]], axis=1)
        labels = lax.broadcasted_iota(jnp.int32, (regions, 2 * width), 0)
        onehot = jnp.where(labels == ids, 1.0, 0.0).astype(BF16)
        total = []
        for r in range(2):
            now = flat_s[0, pl.ds(r, spec, stride=2), :]
            then = before[pl.ds(r, spec, stride=2), :]
            total.append((now + then) * emission[pl.ds(r, spec, stride=2), :])
        contrib = jnp.concatenate(total, axis=1)
        contrib = jnp.concatenate([contrib, jnp.zeros((width - spec, 2 * width), F32)], axis=0)
        result = jnp.zeros((regions, width), F32)
        for piece in split3(contrib):
            result = result + lax.dot_general(
                onehot, piece, (((1,), (1,)), ((), ())), preferred_element_type=F32
            )
        mine[...] = result[0 : regions // 2]
        theirs[...] = result[regions // 2 :]
    put.wait()


def run_window(
    own, north, west, corner, shared, window, first_level, count, last, extra=None, prior=None, edge=None
):
    clon, clat, north_c, west_c, stiff, state, mats = shared
    rows, width = state.shape[2], state.shape[3]
    spec = rows // 2
    grad = extra is not None
    regions = 0
    args = [own, north, west, corner, clon, clat, north_c, west_c, stiff, state, mats]
    specs = [VMEM] * 9 + [ANY] * 2
    aliases = {}
    if grad:
        before, emission, region, regions = extra
        args += [before, emission, region]
        specs += [VMEM] * 3
    if edge is not None:
        args.append(edge)
        specs.append(VMEM)
    if last:
        levels = state.shape[1]
        if not grad:
            aliases = {len(args): 0}
            args.append(prior)
            specs.append(ANY)
        out_shape = [jax.ShapeDtypeStruct((levels, rows, width), BF16)]
        out_specs = [ANY]
        if grad:
            out_shape += [jax.ShapeDtypeStruct((regions // 2, width), F32)] * 2
            out_specs += [VMEM] * 2
    else:
        out_shape = [
            jax.ShapeDtypeStruct((count * rows + (0 if edge is None else TAIL), width), F32),
        ]
        out_specs = [VMEM]
    scratch = [
        pltpu.VMEM((count, spec, 2 * width), F32),
        pltpu.VMEM((count, spec, 2 * width), F32),
        pltpu.VMEM((count, rows, width), F32),
        pltpu.VMEM((count, rows, width), BF16),
        pltpu.VMEM((STEPS, count, spec, spec), BF16),
        pltpu.SemaphoreType.DMA((3,)),
    ]
    if last:
        scratch.append(pltpu.VMEM((count, rows, width), BF16))
    body = functools.partial(
        window_kernel,
        window=window,
        first_level=first_level,
        count=count,
        rows=rows,
        last=last,
        grad=grad,
        regions=regions,
    )
    return pl.pallas_call(
        body,
        out_shape=out_shape,
        in_specs=specs,
        out_specs=out_specs,
        scratch_shapes=scratch,
        input_output_aliases=aliases,
        name=f"window{window}_from{first_level}",
        cost_estimate=pl.CostEstimate(flops=0, transcendentals=0, bytes_accessed=COST[window][first_level]),
        compiler_params=vmem(40 if count > 1 else 8),
    )(*args)


def to_north(block):
    bands = lax.axis_size("lat")
    return lax.ppermute(block, "lat", [(i + 1, i) for i in range(bands - 1)])


def to_west(block):
    blocks = lax.axis_size("lon")
    return lax.ppermute(block, "lon", [((j + 1) % blocks, j) for j in range(blocks)])


def per_device(
    adjoint_in, state, inverses, courant_lon, courant_lat, emission, region_id, stiffness
):
    windows, levels, spec, lat_rows, width = state.shape
    rows = spec * lat_rows
    regions = lax.axis_size("lat") * lax.axis_size("lon")
    adj = adjoint_in.reshape(levels, rows, width)
    flat_state = state.reshape(windows, levels, rows, width)
    flat_em = emission.reshape(rows, width)
    mats = jnp.swapaxes(inverses, 2, 3)
    low1 = pl.pallas_call(
        functools.partial(pack_kernel, rows=rows),
        out_shape=jax.ShapeDtypeStruct((rows + folded_rows(rows) + EXTRA, width), F32),
        in_specs=[VMEM] * 4 + [HBM],
        out_specs=VMEM,
        scratch_shapes=[pltpu.VMEM((levels, rows, width), BF16), pltpu.SemaphoreType.DMA],
        name="pack",
        compiler_params=vmem(56),
    )(adj, courant_lon, courant_lat, stiffness, flat_state)
    low1_n = to_north(low1)
    rest1 = pl.pallas_call(
        functools.partial(rest_kernel, rows=rows),
        out_shape=jax.ShapeDtypeStruct(((levels - 1) * rows, width), F32),
        in_specs=[VMEM, ANY],
        out_specs=VMEM,
        name="rest",
        compiler_params=vmem(56),
    )(adj, low1)
    rest1, low1_n = lax.optimization_barrier((rest1, low1_n))
    rest1_n = to_north(rest1)
    west1_w = to_west(jnp.concatenate([low1[rows:], low1_n[rows:]], axis=0))
    strip, both = pl.pallas_call(
        functools.partial(strip_kernel, rows=rows),
        out_shape=[
            jax.ShapeDtypeStruct((rows, width), F32),
            jax.ShapeDtypeStruct((2 * (rows + EXTRA), width), F32),
        ],
        in_specs=[VMEM] * 2,
        out_specs=[VMEM] * 2,
        name="strip",
        cost_estimate=pl.CostEstimate(flops=0, transcendentals=0, bytes_accessed=40_000_000),
        compiler_params=vmem(8),
    )(west1_w, mats)
    shared = (courant_lon, courant_lat, low1_n, both, stiffness, flat_state, mats)
    low0 = run_window(
        low1, low1_n, both, both, shared, 1, 0, 1, False, edge=strip
    )[0]
    low0_n = to_north(low0)
    rest1_n, low0 = lax.optimization_barrier((rest1_n, low0))
    rest0 = run_window(
        rest1, rest1_n, both, both, shared, 1, 1, levels - 1, False
    )[0]
    low0_n, rest0 = lax.optimization_barrier((low0_n, rest0))
    rest0_n = to_north(rest0)
    parity = lax.axis_index("lon") % 2
    slot = region_id // 2 + jnp.where(region_id % 2 == parity, 0, regions // 2)
    low_extra = (low0, flat_em, slot, regions)
    out, mine, theirs = run_window(
        low0, low0_n, strip, low0_n, shared, 0, 0, 1, True, extra=low_extra
    )
    pairs = [(k ^ 1, k) for k in range(regions)]
    mine = mine + lax.ppermute(theirs, ("lat", "lon"), pairs)
    groups = [list(range(k, regions, 2)) for k in range(2)]
    spread = lax.all_to_all(
        mine, ("lat", "lon"), 0, 0, axis_index_groups=groups, tiled=True
    )
    out = run_window(
        rest0, rest0_n, strip, low0_n, shared, 0, 1, levels - 1, True, prior=out
    )[0]
    out, spread = lax.optimization_barrier((out, spread))
    grad = pl.pallas_call(
        sum_kernel,
        out_shape=jax.ShapeDtypeStruct((1, width), F32),
        in_specs=[VMEM],
        out_specs=VMEM,
        name="gather_sum",
        compiler_params=vmem(4),
    )(spread)[:, :spec]
    return out.reshape(levels, spec, lat_rows, width), grad


def solution(mesh):
    in_specs = (
        P(None, None, "lat", "lon"),
        P(None, None, None, "lat", "lon"),
        P(),
        P("lat", "lon"),
        P("lat", "lon"),
        P(None, "lat", "lon"),
        P("lat", "lon"),
        P(None, "lat", "lon"),
    )
    out_specs = (P(None, None, "lat", "lon"), P(("lat", "lon"), None))
    return jax.shard_map(
        per_device, mesh=mesh, in_specs=in_specs, out_specs=out_specs, check_vma=False
    )
```

```python
import functools
import jax
import jax.numpy as jnp
from jax import lax
from jax.experimental import pallas as pl
from jax.experimental.pallas import tpu as pltpu
from jax.sharding import PartitionSpec as P

STEPS = 3
EXTRA = 8
TAIL = 104
WIDE = 4
COST = ((10_000_000, 10_000_000), (40_000_000, 10_000_000))
F32 = jnp.float32
BF16 = jnp.bfloat16
ANY = pl.BlockSpec(memory_space=pl.ANY)
HBM = pl.BlockSpec(memory_space=pltpu.HBM)
VMEM = pl.BlockSpec(memory_space=pltpu.VMEM)


def vmem(mib):
    return pltpu.CompilerParams(vmem_limit_bytes=mib * 2**20)


def lanes(shape):
    return lax.broadcasted_iota(jnp.int32, shape, len(shape) - 1)


def place(acc, block, start):
    moved = pltpu.roll(block, start, 1) if start else block
    at = lanes(block.shape)
    return jnp.where((at >= start) & (at < start + WIDE), moved, acc)


def tall(row):
    return jnp.broadcast_to(row, (8, row.shape[1]))


def folded_rows(rows):
    return -(-rows // 16) * 8


def pack_kernel(adj, clon, clat, stiff, state_h, first, state_s, sem, *, rows):
    levels, _, width = adj.shape
    half = width // 2
    get = pltpu.make_async_copy(state_h.at[state_h.shape[0] - 1], state_s, sem)
    get.start()
    acc = jnp.zeros((rows, width), F32)
    grades = jnp.zeros((8, width), F32)
    for lev in range(levels):
        block = adj[lev].astype(F32)
        if lev == 0:
            first[0:rows] = block
        acc = place(acc, block, WIDE * lev)
        both = stiff[lev].astype(F32)
        grades = place(grades, tall(both[0:1]), WIDE * lev)
        grades = place(grades, tall(both[1:2]), half + WIDE * lev)
    get.wait()
    for lev in range(levels):
        acc = place(acc, state_s[lev].astype(F32), half // 2 + WIDE * lev)
    folded = folded_rows(rows)
    upper = jnp.concatenate([acc[folded:], jnp.zeros((2 * folded - rows, width), F32)], axis=0)
    first[rows : rows + folded] = acc[0:folded] + pltpu.roll(upper, half, 1)
    at = rows + folded
    first[at : at + 2] = clon[...]
    first[at + 2 : at + 4] = clat[...]
    first[at + 4 : at + 8] = grades[0:4]


def rest_kernel(adj, first, rest, *, rows):
    for lev in range(1, adj.shape[0]):
        rest[(lev - 1) * rows : lev * rows] = adj[lev].astype(F32)


def pull(block, lane_from, lane_to, width):
    shift = (lane_to - lane_from) % width
    return pltpu.roll(block, shift, 1) if shift else block


def mixed(cour, at, mid, down, east):
    return cour["keep"][at] * mid + cour["lat"][at] * down + cour["lon"][at] * east


def with_keep(lon, lat):
    return {"lon": lon, "lat": lat, "keep": [1.0 - a - b for a, b in zip(lon, lat)]}


def advected(own, north, west, corner, lev, start, cour):
    width = own.shape[1]
    spec = west.shape[0] // 2
    end = width - 1
    last = lanes((spec, width)) == end
    base = lev * 2 * spec

    def pick(ref, first, parity):
        return ref[pl.ds(first + parity, spec, stride=2), :]

    r0, r1 = pick(own, base, 0), pick(own, base, 1)
    r2, r3 = pick(north, base, 0), pick(north, base, 1)
    w0, w1 = pick(west, 0, 0), pick(west, 0, 1)
    e0, e1 = pull(w0, start, end, width), pull(w1, start, end, width)
    g0, g1 = pull(w0, start + 1, end, width), pull(w1, start + 1, end, width)
    d0 = pull(corner, start, end, width)

    def right(block, edge):
        return jnp.where(last, edge, pltpu.roll(block, width - 1, 1))

    a0 = mixed(cour, 0, r0, r1, right(r0, e0))
    a1 = mixed(cour, 1, r1, r2, right(r1, e1))
    a2 = mixed(cour, 2, r2, r3, right(r2, d0))
    f0 = mixed(cour, 3, e0, e1, g0)
    f1 = mixed(cour, 4, e1, d0, g1)
    b0 = mixed(cour, 0, a0, a1, right(a0, f0))
    b1 = mixed(cour, 1, a1, a2, right(a1, f1))
    return b0, b1


def courant(clon, clat, north_c, west_c, rows):
    width = clon.shape[1]

    def edge(row):
        return pltpu.roll(tall(row), width - 1, 1)[0:1]

    at = rows + folded_rows(rows)
    lon = [clon[0:1], clon[1:2], north_c[at : at + 1]]
    lat = [clat[0:1], clat[1:2], north_c[at + 2 : at + 3]]
    lon += [edge(west_c[rows : rows + 1]), edge(west_c[rows + 1 : rows + 2])]
    lat += [edge(west_c[rows + 2 : rows + 3]), edge(west_c[rows + 3 : rows + 4])]
    return with_keep(lon, lat)


def strip_kernel(packed, mats, out, both, *, rows):
    folded = folded_rows(rows)
    for i in range(2):
        src, dst = i * (folded + EXTRA), i * (rows + EXTRA)
        block = packed[src : src + folded]
        both[dst : dst + folded] = block
        both[dst + folded : dst + rows] = pltpu.roll(block, block.shape[1] // 2, 1)[0 : rows - folded]
        both[dst + rows : dst + rows + EXTRA] = packed[src + folded : src + folded + EXTRA]
    west, diag = both.at[0 : rows + EXTRA], both.at[rows + EXTRA : 2 * (rows + EXTRA)]
    spec, width = rows // 2, both.shape[1]
    half = width // 2
    levels = mats.shape[1]
    at = lanes((spec, width))

    def pick(ref, parity):
        return ref[pl.ds(parity, spec, stride=2), :]

    def spread(row):
        wide = tall(row)
        acc = jnp.zeros((8, width), F32)
        for lev in range(levels):
            acc = place(acc, wide, WIDE * lev)
        return acc[0:1]

    def right(block):
        return pltpu.roll(block, width - 1, 1)

    w0, w1, d0, d1 = pick(west, 0), pick(west, 1), pick(diag, 0), pick(diag, 1)
    lon = [spread(west[rows + i : rows + i + 1]) for i in range(2)]
    lat = [spread(west[rows + i : rows + i + 1]) for i in range(2, 4)]
    lon.append(spread(diag[rows : rows + 1]))
    lat.append(spread(diag[rows + 2 : rows + 3]))
    cour = with_keep(lon, lat)
    a0 = mixed(cour, 0, w0, w1, right(w0))
    a1 = mixed(cour, 1, w1, d0, right(w1))
    a2 = mixed(cour, 2, d0, d1, right(d0))
    b0 = mixed(cour, 0, a0, a1, right(a0))
    b1 = mixed(cour, 1, a1, a2, right(a1))
    value = jnp.where(at < half, b0, pltpu.roll(b1, half, 1))
    quarter = half // 2
    factor = jnp.where(at < half, pltpu.roll(w0, width - quarter, 1), pltpu.roll(w1, quarter, 1))
    live = west[rows + 4 : rows + 5]
    group = (at & (half - 1)) // WIDE

    def times(s, right_side):
        low = right_side.astype(BF16)
        acc = jnp.dot(mats[s, 0], low, preferred_element_type=F32)
        for lev in range(1, levels):
            prod = jnp.dot(mats[s, lev], low, preferred_element_type=F32)
            acc = jnp.where(group == lev, prod, acc)
        return acc

    def stage(i, value):
        s = STEPS - 1 - i
        one = times(s, value)
        two = times(s, one * factor)
        three = times(s, two * factor)
        cand = 0.4 * value + 0.3 * one + 0.2 * two + 0.1 * three
        return jnp.where(live > s.astype(F32), cand, value)

    value = lax.fori_loop(0, STEPS, stage, value)
    out[pl.ds(0, spec, stride=2), :] = value
    out[pl.ds(1, spec, stride=2), :] = pltpu.roll(value, half, 1)


def sum_kernel(parts, out, *, count):
    size = out.shape[0]
    if size == 1:
        out[...] = jnp.sum(parts[...], axis=0, keepdims=True)
        return
    acc = parts[0:size]
    for k in range(1, count):
        acc = acc + parts[k * size : (k + 1) * size]
    out[...] = acc


def add_parts(parts, count):
    size, width = parts.shape[0] // count, parts.shape[1]
    return pl.pallas_call(
        functools.partial(sum_kernel, count=count),
        out_shape=jax.ShapeDtypeStruct((size, width), F32),
        in_specs=[VMEM],
        out_specs=VMEM,
        name=f"add_{count}_parts",
        compiler_params=vmem(4),
    )(parts)


def split3(value):
    high = value.astype(BF16)
    left = value - high.astype(F32)
    mid = left.astype(BF16)
    low = (left - mid.astype(F32)).astype(BF16)
    return high, mid, low


def window_kernel(
    *refs, window, first_level, count, rows, last, grad, regions, near
):
    refs = list(refs)
    own, north, west, corner_r, clon, clat, north_c, west_c, stiff, state_h, mats_h = refs[:11]
    refs = refs[11:]
    if grad:
        before, emission, region = refs[:3]
        refs = refs[3:]
    if last and not grad:
        refs = refs[1:]
    if not last and first_level == 0:
        edge_r = refs.pop(0)
    if last:
        out_h = refs.pop(0)
        if grad:
            partial = refs.pop(0)
    else:
        lam_out = refs.pop(0)
    x_s, y_s, flat_s, state_s, mats_s, sems = refs[:6]
    refs = refs[6:]
    spec, width = rows // 2, clon.shape[1]
    get_state = pltpu.make_async_copy(
        state_h.at[window, pl.ds(first_level, count)], state_s, sems.at[0]
    )
    get_mats = pltpu.make_async_copy(
        mats_h.at[:, pl.ds(first_level, count)], mats_s, sems.at[1]
    )
    get_state.start()
    get_mats.start()
    cour = courant(clon, clat, north_c, west_c, rows)
    if last:
        corner = corner_r[rows : rows + spec]
    else:
        corner = corner_r[pl.ds(rows + EXTRA, spec, stride=2), :]
    west_v = west.at[0:rows]
    for lev in range(count):
        start = WIDE * (first_level + lev)
        b0, b1 = advected(own, north, west_v, corner, lev, start, cour)
        x_s[lev, :, 0:width] = b0
        x_s[lev, :, width : 2 * width] = b1
    get_state.wait()
    for lev in range(count):
        flat_s[lev] = state_s[lev].astype(F32)
        y_s[lev, :, 0:width] = flat_s[lev, pl.ds(0, spec, stride=2), :]
        y_s[lev, :, width : 2 * width] = flat_s[lev, pl.ds(1, spec, stride=2), :]
    get_mats.wait()
    live = []
    for lev in range(count):
        both = stiff[first_level + lev]
        live.append(jnp.concatenate([both[0:1], both[1:2]], axis=1))

    def stage(i, carry):
        s = STEPS - 1 - i
        rights = [x_s[lev].astype(BF16) for lev in range(count)]
        cands = [0.4 * x_s[lev] for lev in range(count)]
        for k, share in enumerate((0.3, 0.2, 0.1)):
            prods = [
                jnp.dot(mats_s[s, lev], rights[lev], preferred_element_type=F32)
                for lev in range(count)
            ]
            cands = [cands[lev] + share * prods[lev] for lev in range(count)]
            if k < 2:
                rights = [(prods[lev] * y_s[lev]).astype(BF16) for lev in range(count)]
        for lev in range(count):
            x_s[lev] = jnp.where(live[lev] > s, cands[lev], x_s[lev])
        return carry

    lax.fori_loop(0, STEPS, stage, 0)
    for lev in range(count):
        for r in range(2):
            half = x_s[lev, :, r * width : (r + 1) * width]
            if last:
                flat_s[lev, pl.ds(r, spec, stride=2), :] = half
            else:
                lam_out[pl.ds(lev * rows + r, spec, stride=2), :] = half
    if not last:
        if first_level == 0:
            lam_out[rows : rows + spec] = edge_r[pl.ds(0, spec, stride=2), :]
            lam_out[rows + spec :] = jnp.zeros((TAIL - spec, width), F32)
        return
    out_s = refs.pop(0)
    for lev in range(count):
        out_s[lev] = flat_s[lev].astype(BF16)
    put = pltpu.make_async_copy(out_s, out_h.at[pl.ds(first_level, count)], sems.at[2])
    put.start()
    if grad:
        ids = jnp.concatenate([region[0:1], region[1:2]], axis=1)
        ids = (ids & (near - 1)) * (regions // near) + lax.shift_right_logical(ids, near.bit_length() - 1)
        labels = lax.broadcasted_iota(jnp.int32, (regions, 2 * width), 0)
        onehot = jnp.where(labels == ids, 1.0, 0.0).astype(BF16)
        total = []
        for r in range(2):
            now = flat_s[0, pl.ds(r, spec, stride=2), :]
            then = before[pl.ds(r, spec, stride=2), :]
            total.append((now + then) * emission[pl.ds(r, spec, stride=2), :])
        contrib = jnp.concatenate(total, axis=1)
        contrib = jnp.concatenate([contrib, jnp.zeros((width - spec, 2 * width), F32)], axis=0)
        result = jnp.zeros((regions, width), F32)
        for piece in split3(contrib):
            result = result + lax.dot_general(
                onehot, piece, (((1,), (1,)), ((), ())), preferred_element_type=F32
            )
        partial[...] = result
    put.wait()


def run_window(
    own, north, west, corner, shared, window, first_level, count, last, extra=None, prior=None, edge=None
):
    clon, clat, north_c, west_c, stiff, state, mats = shared
    rows, width = state.shape[2], state.shape[3]
    spec = rows // 2
    grad = extra is not None
    regions, near = 0, 0
    args = [own, north, west, corner, clon, clat, north_c, west_c, stiff, state, mats]
    specs = [VMEM] * 9 + [ANY] * 2
    aliases = {}
    if grad:
        before, emission, region, regions, near = extra
        args += [before, emission, region]
        specs += [VMEM] * 3
    if edge is not None:
        args.append(edge)
        specs.append(VMEM)
    if last:
        levels = state.shape[1]
        if not grad:
            aliases = {len(args): 0}
            args.append(prior)
            specs.append(ANY)
        out_shape = [jax.ShapeDtypeStruct((levels, rows, width), BF16)]
        out_specs = [ANY]
        if grad:
            out_shape.append(jax.ShapeDtypeStruct((regions, width), F32))
            out_specs.append(VMEM)
    else:
        out_shape = [
            jax.ShapeDtypeStruct((count * rows + (0 if edge is None else TAIL), width), F32),
        ]
        out_specs = [VMEM]
    scratch = [
        pltpu.VMEM((count, spec, 2 * width), F32),
        pltpu.VMEM((count, spec, 2 * width), F32),
        pltpu.VMEM((count, rows, width), F32),
        pltpu.VMEM((count, rows, width), BF16),
        pltpu.VMEM((STEPS, count, spec, spec), BF16),
        pltpu.SemaphoreType.DMA((3,)),
    ]
    if last:
        scratch.append(pltpu.VMEM((count, rows, width), BF16))
    body = functools.partial(
        window_kernel,
        window=window,
        first_level=first_level,
        count=count,
        rows=rows,
        last=last,
        grad=grad,
        regions=regions,
        near=near,
    )
    return pl.pallas_call(
        body,
        out_shape=out_shape,
        in_specs=specs,
        out_specs=out_specs,
        scratch_shapes=scratch,
        input_output_aliases=aliases,
        name=f"window{window}_from{first_level}",
        cost_estimate=pl.CostEstimate(flops=0, transcendentals=0, bytes_accessed=COST[window][first_level]),
        compiler_params=vmem(40 if count > 1 else 8),
    )(*args)


def to_north(block):
    bands = lax.axis_size("lat")
    return lax.ppermute(block, "lat", [(i + 1, i) for i in range(bands - 1)])


def to_west(block):
    blocks = lax.axis_size("lon")
    return lax.ppermute(block, "lon", [((j + 1) % blocks, j) for j in range(blocks)])


def per_device(
    adjoint_in, state, inverses, courant_lon, courant_lat, emission, region_id, stiffness
):
    windows, levels, spec, lat_rows, width = state.shape
    rows = spec * lat_rows
    regions = lax.axis_size("lat") * lax.axis_size("lon")
    adj = adjoint_in.reshape(levels, rows, width)
    flat_state = state.reshape(windows, levels, rows, width)
    flat_em = emission.reshape(rows, width)
    mats = jnp.swapaxes(inverses, 2, 3)
    low1 = pl.pallas_call(
        functools.partial(pack_kernel, rows=rows),
        out_shape=jax.ShapeDtypeStruct((rows + folded_rows(rows) + EXTRA, width), F32),
        in_specs=[VMEM] * 4 + [HBM],
        out_specs=VMEM,
        scratch_shapes=[pltpu.VMEM((levels, rows, width), BF16), pltpu.SemaphoreType.DMA],
        name="pack",
        compiler_params=vmem(56),
    )(adj, courant_lon, courant_lat, stiffness, flat_state)
    low1_n = to_north(low1)
    rest1 = pl.pallas_call(
        functools.partial(rest_kernel, rows=rows),
        out_shape=jax.ShapeDtypeStruct(((levels - 1) * rows, width), F32),
        in_specs=[VMEM, ANY],
        out_specs=VMEM,
        name="rest",
        compiler_params=vmem(56),
    )(adj, low1)
    rest1, low1_n = lax.optimization_barrier((rest1, low1_n))
    rest1_n = to_north(rest1)
    west1_w = to_west(jnp.concatenate([low1[rows:], low1_n[rows:]], axis=0))
    strip, both = pl.pallas_call(
        functools.partial(strip_kernel, rows=rows),
        out_shape=[
            jax.ShapeDtypeStruct((rows, width), F32),
            jax.ShapeDtypeStruct((2 * (rows + EXTRA), width), F32),
        ],
        in_specs=[VMEM] * 2,
        out_specs=[VMEM] * 2,
        name="strip",
        cost_estimate=pl.CostEstimate(flops=0, transcendentals=0, bytes_accessed=40_000_000),
        compiler_params=vmem(8),
    )(west1_w, mats)
    shared = (courant_lon, courant_lat, low1_n, both, stiffness, flat_state, mats)
    low0 = run_window(
        low1, low1_n, both, both, shared, 1, 0, 1, False, edge=strip
    )[0]
    low0_n = to_north(low0)
    rest1_n, low0 = lax.optimization_barrier((rest1_n, low0))
    rest0 = run_window(
        rest1, rest1_n, both, both, shared, 1, 1, levels - 1, False
    )[0]
    low0_n, rest0 = lax.optimization_barrier((low0_n, rest0))
    rest0_n = to_north(rest0)
    bands, blocks = lax.axis_size("lat"), lax.axis_size("lon")
    near = blocks // 2
    far = regions // near
    low_extra = (low0, flat_em, region_id, regions, near)
    out, partial = run_window(
        low0, low0_n, strip, low0_n, shared, 0, 0, 1, True, extra=low_extra
    )
    line = [list(range(k * near, (k + 1) * near)) for k in range(2)]
    lines = lax.all_to_all(partial, "lon", 0, 0, axis_index_groups=line, tiled=True)
    mine = add_parts(lines, near)
    plane = [list(range(k, regions, near)) for k in range(near)]
    spread = lax.all_to_all(
        mine, ("lat", "lon"), 0, 0, axis_index_groups=plane, tiled=True
    )
    out = run_window(
        rest0, rest0_n, strip, low0_n, shared, 0, 1, levels - 1, True, prior=out
    )[0]
    out, spread = lax.optimization_barrier((out, spread))
    grad = add_parts(spread, far)[:, :spec]
    return out.reshape(levels, spec, lat_rows, width), grad


def solution(mesh):
    in_specs = (
        P(None, None, "lat", "lon"),
        P(None, None, None, "lat", "lon"),
        P(),
        P("lat", "lon"),
        P("lat", "lon"),
        P(None, "lat", "lon"),
        P("lat", "lon"),
        P(None, "lat", "lon"),
    )
    out_specs = (P(None, None, "lat", "lon"), P(("lat", "lon"), None))
    return jax.shard_map(
        per_device, mesh=mesh, in_specs=in_specs, out_specs=out_specs, check_vma=False
    )
```

```python
import functools
import jax
import jax.numpy as jnp
from jax import lax
from jax.experimental import pallas as pl
from jax.experimental.pallas import tpu as pltpu
from jax.sharding import PartitionSpec as P

STEPS = 3
EXTRA = 8
TAIL = 104
WIDE = 4
COST = ((10_000_000, 10_000_000), (40_000_000, 10_000_000))
F32 = jnp.float32
BF16 = jnp.bfloat16
ANY = pl.BlockSpec(memory_space=pl.ANY)
HBM = pl.BlockSpec(memory_space=pltpu.HBM)
VMEM = pl.BlockSpec(memory_space=pltpu.VMEM)


def vmem(mib):
    return pltpu.CompilerParams(vmem_limit_bytes=mib * 2**20)


def lanes(shape):
    return lax.broadcasted_iota(jnp.int32, shape, len(shape) - 1)


def place(acc, block, start):
    moved = pltpu.roll(block, start, 1) if start else block
    at = lanes(block.shape)
    return jnp.where((at >= start) & (at < start + WIDE), moved, acc)


def tall(row):
    return jnp.broadcast_to(row, (8, row.shape[1]))


def folded_rows(rows):
    return -(-rows // 16) * 8


def pack_kernel(adj, clon, clat, stiff, state_h, first, west, state_s, sem, *, rows):
    levels, _, width = adj.shape
    half = width // 2
    get = pltpu.make_async_copy(state_h.at[state_h.shape[0] - 1], state_s, sem)
    get.start()
    acc = jnp.zeros((rows, width), F32)
    grades = jnp.zeros((8, width), F32)
    for lev in range(levels):
        block = adj[lev].astype(F32)
        if lev == 0:
            first[0:rows] = block
        acc = place(acc, block, WIDE * lev)
        both = stiff[lev].astype(F32)
        grades = place(grades, tall(both[0:1]), WIDE * lev)
        grades = place(grades, tall(both[1:2]), half + WIDE * lev)
    get.wait()
    for lev in range(levels):
        acc = place(acc, state_s[lev].astype(F32), half // 2 + WIDE * lev)
    folded = folded_rows(rows)
    upper = jnp.concatenate([acc[folded:], jnp.zeros((2 * folded - rows, width), F32)], axis=0)
    west[0:folded] = acc[0:folded] + pltpu.roll(upper, half, 1)
    for out, at in ((first, rows), (west, folded)):
        out[at : at + 2] = clon[...]
        out[at + 2 : at + 4] = clat[...]
        out[at + 4 : at + 8] = grades[0:4]
    first[rows + EXTRA :] = jnp.zeros((folded + EXTRA, width), F32)


def rest_kernel(adj, first, rest, *, rows):
    for lev in range(1, adj.shape[0]):
        rest[(lev - 1) * rows : lev * rows] = adj[lev].astype(F32)


def pull(block, lane_from, lane_to, width):
    shift = (lane_to - lane_from) % width
    return pltpu.roll(block, shift, 1) if shift else block


def mixed(cour, at, mid, down, east):
    return cour["keep"][at] * mid + cour["lat"][at] * down + cour["lon"][at] * east


def with_keep(lon, lat):
    return {"lon": lon, "lat": lat, "keep": [1.0 - a - b for a, b in zip(lon, lat)]}


def advected(own, north, west, corner, lev, start, cour):
    width = own.shape[1]
    spec = west.shape[0] // 2
    end = width - 1
    last = lanes((spec, width)) == end
    base = lev * 2 * spec

    def pick(ref, first, parity):
        return ref[pl.ds(first + parity, spec, stride=2), :]

    r0, r1 = pick(own, base, 0), pick(own, base, 1)
    r2, r3 = pick(north, base, 0), pick(north, base, 1)
    w0, w1 = pick(west, 0, 0), pick(west, 0, 1)
    e0, e1 = pull(w0, start, end, width), pull(w1, start, end, width)
    g0, g1 = pull(w0, start + 1, end, width), pull(w1, start + 1, end, width)
    d0 = pull(corner, start, end, width)

    def right(block, edge):
        return jnp.where(last, edge, pltpu.roll(block, width - 1, 1))

    a0 = mixed(cour, 0, r0, r1, right(r0, e0))
    a1 = mixed(cour, 1, r1, r2, right(r1, e1))
    a2 = mixed(cour, 2, r2, r3, right(r2, d0))
    f0 = mixed(cour, 3, e0, e1, g0)
    f1 = mixed(cour, 4, e1, d0, g1)
    b0 = mixed(cour, 0, a0, a1, right(a0, f0))
    b1 = mixed(cour, 1, a1, a2, right(a1, f1))
    return b0, b1


def courant(clon, clat, north_c, west_c, rows):
    width = clon.shape[1]

    def edge(row):
        return pltpu.roll(tall(row), width - 1, 1)[0:1]

    at = rows
    lon = [clon[0:1], clon[1:2], north_c[at : at + 1]]
    lat = [clat[0:1], clat[1:2], north_c[at + 2 : at + 3]]
    lon += [edge(west_c[rows : rows + 1]), edge(west_c[rows + 1 : rows + 2])]
    lat += [edge(west_c[rows + 2 : rows + 3]), edge(west_c[rows + 3 : rows + 4])]
    return with_keep(lon, lat)


def strip_kernel(west_p, north, mats, out, both, *, rows):
    folded = folded_rows(rows)
    for packed, src, dst in ((west_p, 0, 0), (north, rows + EXTRA, rows + EXTRA)):
        block = packed[src : src + folded]
        both[dst : dst + folded] = block
        both[dst + folded : dst + rows] = pltpu.roll(block, block.shape[1] // 2, 1)[0 : rows - folded]
        both[dst + rows : dst + rows + EXTRA] = packed[src + folded : src + folded + EXTRA]
    west, diag = both.at[0 : rows + EXTRA], both.at[rows + EXTRA : 2 * (rows + EXTRA)]
    spec, width = rows // 2, out.shape[1]
    half = width // 2
    levels = mats.shape[1]
    at = lanes((spec, width))

    def pick(ref, parity):
        return ref[pl.ds(parity, spec, stride=2), :]

    def spread(row):
        wide = tall(row)
        acc = jnp.zeros((8, width), F32)
        for lev in range(levels):
            acc = place(acc, wide, WIDE * lev)
        return acc[0:1]

    def right(block):
        return pltpu.roll(block, width - 1, 1)

    w0, w1, d0, d1 = pick(west, 0), pick(west, 1), pick(diag, 0), pick(diag, 1)
    lon = [spread(west[rows + i : rows + i + 1]) for i in range(2)]
    lat = [spread(west[rows + i : rows + i + 1]) for i in range(2, 4)]
    lon.append(spread(diag[rows : rows + 1]))
    lat.append(spread(diag[rows + 2 : rows + 3]))
    cour = with_keep(lon, lat)
    a0 = mixed(cour, 0, w0, w1, right(w0))
    a1 = mixed(cour, 1, w1, d0, right(w1))
    a2 = mixed(cour, 2, d0, d1, right(d0))
    b0 = mixed(cour, 0, a0, a1, right(a0))
    b1 = mixed(cour, 1, a1, a2, right(a1))
    value = jnp.where(at < half, b0, pltpu.roll(b1, half, 1))
    quarter = half // 2
    factor = jnp.where(at < half, pltpu.roll(w0, width - quarter, 1), pltpu.roll(w1, quarter, 1))
    live = west[rows + 4 : rows + 5]
    group = (at & (half - 1)) // WIDE

    def times(s, right_side):
        low = right_side.astype(BF16)
        acc = jnp.dot(mats[s, 0], low, preferred_element_type=F32)
        for lev in range(1, levels):
            prod = jnp.dot(mats[s, lev], low, preferred_element_type=F32)
            acc = jnp.where(group == lev, prod, acc)
        return acc

    def stage(i, value):
        s = STEPS - 1 - i
        one = times(s, value)
        two = times(s, one * factor)
        three = times(s, two * factor)
        cand = 0.4 * value + 0.3 * one + 0.2 * two + 0.1 * three
        return jnp.where(live > s.astype(F32), cand, value)

    value = lax.fori_loop(0, STEPS, stage, value)
    out[pl.ds(0, spec, stride=2), :] = value
    out[pl.ds(1, spec, stride=2), :] = pltpu.roll(value, half, 1)


def sum_kernel(parts, out, *, count):
    size = out.shape[0]
    if size == 1:
        out[...] = jnp.sum(parts[...], axis=0, keepdims=True)
        return
    acc = parts[0:size]
    for k in range(1, count):
        acc = acc + parts[k * size : (k + 1) * size]
    out[...] = acc


def add_parts(parts, count):
    size, width = parts.shape[0] // count, parts.shape[1]
    return pl.pallas_call(
        functools.partial(sum_kernel, count=count),
        out_shape=jax.ShapeDtypeStruct((size, width), F32),
        in_specs=[VMEM],
        out_specs=VMEM,
        name=f"add_{count}_parts",
        compiler_params=vmem(4),
    )(parts)


def split3(value):
    high = value.astype(BF16)
    left = value - high.astype(F32)
    mid = left.astype(BF16)
    low = (left - mid.astype(F32)).astype(BF16)
    return high, mid, low


def window_kernel(
    *refs, window, first_level, count, rows, last, grad, regions, near
):
    refs = list(refs)
    own, north, west, corner_r, clon, clat, north_c, west_c, stiff, state_h, mats_h = refs[:11]
    refs = refs[11:]
    if grad:
        before, emission, region = refs[:3]
        refs = refs[3:]
    if last and not grad:
        refs = refs[1:]
    if not last and first_level == 0:
        edge_r = refs.pop(0)
    if last:
        out_h = refs.pop(0)
        if grad:
            partial = refs.pop(0)
    else:
        lam_out = refs.pop(0)
    x_s, y_s, flat_s, state_s, mats_s, sems = refs[:6]
    refs = refs[6:]
    spec, width = rows // 2, clon.shape[1]
    get_state = pltpu.make_async_copy(
        state_h.at[window, pl.ds(first_level, count)], state_s, sems.at[0]
    )
    get_mats = pltpu.make_async_copy(
        mats_h.at[:, pl.ds(first_level, count)], mats_s, sems.at[1]
    )
    get_state.start()
    get_mats.start()
    cour = courant(clon, clat, north_c, west_c, rows)
    if last:
        corner = corner_r[rows : rows + spec]
    else:
        corner = corner_r[pl.ds(rows + EXTRA, spec, stride=2), :]
    west_v = west.at[0:rows]
    for lev in range(count):
        start = WIDE * (first_level + lev)
        b0, b1 = advected(own, north, west_v, corner, lev, start, cour)
        x_s[lev, :, 0:width] = b0
        x_s[lev, :, width : 2 * width] = b1
    get_state.wait()
    for lev in range(count):
        flat_s[lev] = state_s[lev].astype(F32)
        y_s[lev, :, 0:width] = flat_s[lev, pl.ds(0, spec, stride=2), :]
        y_s[lev, :, width : 2 * width] = flat_s[lev, pl.ds(1, spec, stride=2), :]
    get_mats.wait()
    live = []
    for lev in range(count):
        both = stiff[first_level + lev]
        live.append(jnp.concatenate([both[0:1], both[1:2]], axis=1))

    def stage(i, carry):
        s = STEPS - 1 - i
        rights = [x_s[lev].astype(BF16) for lev in range(count)]
        cands = [0.4 * x_s[lev] for lev in range(count)]
        for k, share in enumerate((0.3, 0.2, 0.1)):
            prods = [
                jnp.dot(mats_s[s, lev], rights[lev], preferred_element_type=F32)
                for lev in range(count)
            ]
            cands = [cands[lev] + share * prods[lev] for lev in range(count)]
            if k < 2:
                rights = [(prods[lev] * y_s[lev]).astype(BF16) for lev in range(count)]
        for lev in range(count):
            x_s[lev] = jnp.where(live[lev] > s, cands[lev], x_s[lev])
        return carry

    lax.fori_loop(0, STEPS, stage, 0)
    for lev in range(count):
        for r in range(2):
            half = x_s[lev, :, r * width : (r + 1) * width]
            if last:
                flat_s[lev, pl.ds(r, spec, stride=2), :] = half
            else:
                lam_out[pl.ds(lev * rows + r, spec, stride=2), :] = half
    if not last:
        if first_level == 0:
            lam_out[rows : rows + spec] = edge_r[pl.ds(0, spec, stride=2), :]
            lam_out[rows + spec :] = jnp.zeros((TAIL - spec, width), F32)
        return
    out_s = refs.pop(0)
    for lev in range(count):
        out_s[lev] = flat_s[lev].astype(BF16)
    put = pltpu.make_async_copy(out_s, out_h.at[pl.ds(first_level, count)], sems.at[2])
    put.start()
    if grad:
        ids = jnp.concatenate([region[0:1], region[1:2]], axis=1)
        ids = (ids & (near - 1)) * (regions // near) + lax.shift_right_logical(ids, near.bit_length() - 1)
        labels = lax.broadcasted_iota(jnp.int32, (regions, 2 * width), 0)
        onehot = jnp.where(labels == ids, 1.0, 0.0).astype(BF16)
        total = []
        for r in range(2):
            now = flat_s[0, pl.ds(r, spec, stride=2), :]
            then = before[pl.ds(r, spec, stride=2), :]
            total.append((now + then) * emission[pl.ds(r, spec, stride=2), :])
        contrib = jnp.concatenate(total, axis=1)
        contrib = jnp.concatenate([contrib, jnp.zeros((width - spec, 2 * width), F32)], axis=0)
        result = jnp.zeros((regions, width), F32)
        for piece in split3(contrib):
            result = result + lax.dot_general(
                onehot, piece, (((1,), (1,)), ((), ())), preferred_element_type=F32
            )
        partial[...] = result
    put.wait()


def run_window(
    own, north, west, corner, shared, window, first_level, count, last, extra=None, prior=None, edge=None
):
    clon, clat, north_c, west_c, stiff, state, mats = shared
    rows, width = state.shape[2], state.shape[3]
    spec = rows // 2
    grad = extra is not None
    regions, near = 0, 0
    args = [own, north, west, corner, clon, clat, north_c, west_c, stiff, state, mats]
    specs = [VMEM] * 9 + [ANY] * 2
    aliases = {}
    if grad:
        before, emission, region, regions, near = extra
        args += [before, emission, region]
        specs += [VMEM] * 3
    if edge is not None:
        args.append(edge)
        specs.append(VMEM)
    if last:
        levels = state.shape[1]
        if not grad:
            aliases = {len(args): 0}
            args.append(prior)
            specs.append(ANY)
        out_shape = [jax.ShapeDtypeStruct((levels, rows, width), BF16)]
        out_specs = [ANY]
        if grad:
            out_shape.append(jax.ShapeDtypeStruct((regions, width), F32))
            out_specs.append(VMEM)
    else:
        out_shape = [
            jax.ShapeDtypeStruct((count * rows + (0 if edge is None else TAIL), width), F32),
        ]
        out_specs = [VMEM]
    scratch = [
        pltpu.VMEM((count, spec, 2 * width), F32),
        pltpu.VMEM((count, spec, 2 * width), F32),
        pltpu.VMEM((count, rows, width), F32),
        pltpu.VMEM((count, rows, width), BF16),
        pltpu.VMEM((STEPS, count, spec, spec), BF16),
        pltpu.SemaphoreType.DMA((3,)),
    ]
    if last:
        scratch.append(pltpu.VMEM((count, rows, width), BF16))
    body = functools.partial(
        window_kernel,
        window=window,
        first_level=first_level,
        count=count,
        rows=rows,
        last=last,
        grad=grad,
        regions=regions,
        near=near,
    )
    return pl.pallas_call(
        body,
        out_shape=out_shape,
        in_specs=specs,
        out_specs=out_specs,
        scratch_shapes=scratch,
        input_output_aliases=aliases,
        name=f"window{window}_from{first_level}",
        cost_estimate=pl.CostEstimate(flops=0, transcendentals=0, bytes_accessed=COST[window][first_level]),
        compiler_params=vmem(40 if count > 1 else 8),
    )(*args)


def to_north(block):
    bands = lax.axis_size("lat")
    return lax.ppermute(block, "lat", [(i + 1, i) for i in range(bands - 1)])


def to_west(block):
    blocks = lax.axis_size("lon")
    return lax.ppermute(block, "lon", [((j + 1) % blocks, j) for j in range(blocks)])


def per_device(
    adjoint_in, state, inverses, courant_lon, courant_lat, emission, region_id, stiffness
):
    windows, levels, spec, lat_rows, width = state.shape
    rows = spec * lat_rows
    regions = lax.axis_size("lat") * lax.axis_size("lon")
    adj = adjoint_in.reshape(levels, rows, width)
    flat_state = state.reshape(windows, levels, rows, width)
    flat_em = emission.reshape(rows, width)
    mats = jnp.swapaxes(inverses, 2, 3)
    folded = folded_rows(rows)
    low1, west1 = pl.pallas_call(
        functools.partial(pack_kernel, rows=rows),
        out_shape=[
            jax.ShapeDtypeStruct((rows + folded + 2 * EXTRA, width), F32),
            jax.ShapeDtypeStruct((folded + EXTRA, width), F32),
        ],
        in_specs=[VMEM] * 4 + [HBM],
        out_specs=[VMEM] * 2,
        scratch_shapes=[pltpu.VMEM((levels, rows, width), BF16), pltpu.SemaphoreType.DMA],
        name="pack",
        compiler_params=vmem(56),
    )(adj, courant_lon, courant_lat, stiffness, flat_state)
    west1_w = to_west(west1)
    low1 = lax.dynamic_update_slice(low1, west1_w, (rows + EXTRA, 0))
    low1_n = to_north(low1)
    rest1 = pl.pallas_call(
        functools.partial(rest_kernel, rows=rows),
        out_shape=jax.ShapeDtypeStruct(((levels - 1) * rows, width), F32),
        in_specs=[VMEM, ANY],
        out_specs=VMEM,
        name="rest",
        compiler_params=vmem(56),
    )(adj, west1)
    rest1, low1_n = lax.optimization_barrier((rest1, low1_n))
    rest1_n = to_north(rest1)
    strip, both = pl.pallas_call(
        functools.partial(strip_kernel, rows=rows),
        out_shape=[
            jax.ShapeDtypeStruct((rows, width), F32),
            jax.ShapeDtypeStruct((2 * (rows + EXTRA), width), F32),
        ],
        in_specs=[VMEM] * 3,
        out_specs=[VMEM] * 2,
        name="strip",
        cost_estimate=pl.CostEstimate(flops=0, transcendentals=0, bytes_accessed=40_000_000),
        compiler_params=vmem(8),
    )(west1_w, low1_n, mats)
    shared = (courant_lon, courant_lat, low1_n, both, stiffness, flat_state, mats)
    low0 = run_window(
        low1, low1_n, both, both, shared, 1, 0, 1, False, edge=strip
    )[0]
    low0_n = to_north(low0)
    rest1_n, low0 = lax.optimization_barrier((rest1_n, low0))
    rest0 = run_window(
        rest1, rest1_n, both, both, shared, 1, 1, levels - 1, False
    )[0]
    low0_n, rest0 = lax.optimization_barrier((low0_n, rest0))
    rest0_n = to_north(rest0)
    bands, blocks = lax.axis_size("lat"), lax.axis_size("lon")
    near = blocks // 2
    far = regions // near
    low_extra = (low0, flat_em, region_id, regions, near)
    out, partial = run_window(
        low0, low0_n, strip, low0_n, shared, 0, 0, 1, True, extra=low_extra
    )
    line = [list(range(k * near, (k + 1) * near)) for k in range(2)]
    lines = lax.all_to_all(partial, "lon", 0, 0, axis_index_groups=line, tiled=True)
    mine = add_parts(lines, near)
    plane = [list(range(k, regions, near)) for k in range(near)]
    spread = lax.all_to_all(
        mine, ("lat", "lon"), 0, 0, axis_index_groups=plane, tiled=True
    )
    out = run_window(
        rest0, rest0_n, strip, low0_n, shared, 0, 1, levels - 1, True, prior=out
    )[0]
    out, spread = lax.optimization_barrier((out, spread))
    grad = add_parts(spread, far)[:, :spec]
    return out.reshape(levels, spec, lat_rows, width), grad


def solution(mesh):
    in_specs = (
        P(None, None, "lat", "lon"),
        P(None, None, None, "lat", "lon"),
        P(),
        P("lat", "lon"),
        P("lat", "lon"),
        P(None, "lat", "lon"),
        P("lat", "lon"),
        P(None, "lat", "lon"),
    )
    out_specs = (P(None, None, "lat", "lon"), P(("lat", "lon"), None))
    return jax.shard_map(
        per_device, mesh=mesh, in_specs=in_specs, out_specs=out_specs, check_vma=False
    )
```

```python
import functools
import jax
import jax.numpy as jnp
from jax import lax
from jax.experimental import pallas as pl
from jax.experimental.pallas import tpu as pltpu
from jax.sharding import PartitionSpec as P

STEPS = 3
EXTRA = 8
TAIL = 104
WIDE = 4
COST = ((10_000_000, 10_000_000), (40_000_000, 10_000_000))
F32 = jnp.float32
BF16 = jnp.bfloat16
ANY = pl.BlockSpec(memory_space=pl.ANY)
HBM = pl.BlockSpec(memory_space=pltpu.HBM)
VMEM = pl.BlockSpec(memory_space=pltpu.VMEM)


def vmem(mib):
    return pltpu.CompilerParams(vmem_limit_bytes=mib * 2**20)


def lanes(shape):
    return lax.broadcasted_iota(jnp.int32, shape, len(shape) - 1)


def place(acc, block, start):
    moved = pltpu.roll(block, start, 1) if start else block
    at = lanes(block.shape)
    return jnp.where((at >= start) & (at < start + WIDE), moved, acc)


def tall(row):
    return jnp.broadcast_to(row, (8, row.shape[1]))


def folded_rows(rows):
    return -(-rows // 16) * 8


def pack_kernel(adj, clon, clat, stiff, state_h, first, state_s, sem, *, rows):
    levels, _, width = adj.shape
    half = width // 2
    get = pltpu.make_async_copy(state_h.at[state_h.shape[0] - 1], state_s, sem)
    get.start()
    acc = jnp.zeros((rows, width), F32)
    grades = jnp.zeros((8, width), F32)
    for lev in range(levels):
        block = adj[lev].astype(F32)
        acc = place(acc, block, WIDE * lev)
        both = stiff[lev].astype(F32)
        grades = place(grades, tall(both[0:1]), WIDE * lev)
        grades = place(grades, tall(both[1:2]), half + WIDE * lev)
    get.wait()
    for lev in range(levels):
        acc = place(acc, state_s[lev].astype(F32), half // 2 + WIDE * lev)
    folded = folded_rows(rows)
    upper = jnp.concatenate([acc[folded:], jnp.zeros((2 * folded - rows, width), F32)], axis=0)
    first[0:folded] = acc[0:folded] + pltpu.roll(upper, half, 1)
    first[folded : folded + 2] = clon[...]
    first[folded + 2 : folded + 4] = clat[...]
    first[folded + 4 : folded + 8] = grades[0:4]


def rest_kernel(adj, first, rest, *, rows):
    for lev in range(adj.shape[0]):
        rest[lev * rows : (lev + 1) * rows] = adj[lev].astype(F32)


def pull(block, lane_from, lane_to, width):
    shift = (lane_to - lane_from) % width
    return pltpu.roll(block, shift, 1) if shift else block


def mixed(cour, at, mid, down, east):
    return cour["keep"][at] * mid + cour["lat"][at] * down + cour["lon"][at] * east


def with_keep(lon, lat):
    return {"lon": lon, "lat": lat, "keep": [1.0 - a - b for a, b in zip(lon, lat)]}


def advected(own, north, west, corner, base, start, cour):
    width = own.shape[1]
    spec = west.shape[0] // 2
    end = width - 1
    last = lanes((spec, width)) == end

    def pick(ref, first, parity):
        return ref[pl.ds(first + parity, spec, stride=2), :]

    r0, r1 = pick(own, base, 0), pick(own, base, 1)
    r2, r3 = pick(north, base, 0), pick(north, base, 1)
    w0, w1 = pick(west, 0, 0), pick(west, 0, 1)
    e0, e1 = pull(w0, start, end, width), pull(w1, start, end, width)
    g0, g1 = pull(w0, start + 1, end, width), pull(w1, start + 1, end, width)
    d0 = pull(corner, start, end, width)

    def right(block, edge):
        return jnp.where(last, edge, pltpu.roll(block, width - 1, 1))

    a0 = mixed(cour, 0, r0, r1, right(r0, e0))
    a1 = mixed(cour, 1, r1, r2, right(r1, e1))
    a2 = mixed(cour, 2, r2, r3, right(r2, d0))
    f0 = mixed(cour, 3, e0, e1, g0)
    f1 = mixed(cour, 4, e1, d0, g1)
    b0 = mixed(cour, 0, a0, a1, right(a0, f0))
    b1 = mixed(cour, 1, a1, a2, right(a1, f1))
    return b0, b1


def courant(own_c, north_c, west_c, rows):
    width = own_c.shape[1]
    at = folded_rows(rows)

    def edge(row):
        return pltpu.roll(tall(row), width - 1, 1)[0:1]

    lon = [own_c[at : at + 1], own_c[at + 1 : at + 2], north_c[at : at + 1]]
    lat = [own_c[at + 2 : at + 3], own_c[at + 3 : at + 4], north_c[at + 2 : at + 3]]
    lon += [edge(west_c[rows : rows + 1]), edge(west_c[rows + 1 : rows + 2])]
    lat += [edge(west_c[rows + 2 : rows + 3]), edge(west_c[rows + 3 : rows + 4])]
    return with_keep(lon, lat)


def strip_kernel(packed, mats, out, both, *, rows):
    folded = folded_rows(rows)
    for i in range(2):
        src, dst = i * (folded + EXTRA), i * (rows + EXTRA)
        block = packed[src : src + folded]
        both[dst : dst + folded] = block
        both[dst + folded : dst + rows] = pltpu.roll(block, block.shape[1] // 2, 1)[0 : rows - folded]
        both[dst + rows : dst + rows + EXTRA] = packed[src + folded : src + folded + EXTRA]
    west, diag = both.at[0 : rows + EXTRA], both.at[rows + EXTRA : 2 * (rows + EXTRA)]
    spec, width = rows // 2, both.shape[1]
    half = width // 2
    levels = mats.shape[1]
    at = lanes((spec, width))

    def pick(ref, parity):
        return ref[pl.ds(parity, spec, stride=2), :]

    def spread(row):
        wide = tall(row)
        acc = jnp.zeros((8, width), F32)
        for lev in range(levels):
            acc = place(acc, wide, WIDE * lev)
        return acc[0:1]

    def right(block):
        return pltpu.roll(block, width - 1, 1)

    w0, w1, d0, d1 = pick(west, 0), pick(west, 1), pick(diag, 0), pick(diag, 1)
    lon = [spread(west[rows + i : rows + i + 1]) for i in range(2)]
    lat = [spread(west[rows + i : rows + i + 1]) for i in range(2, 4)]
    lon.append(spread(diag[rows : rows + 1]))
    lat.append(spread(diag[rows + 2 : rows + 3]))
    cour = with_keep(lon, lat)
    a0 = mixed(cour, 0, w0, w1, right(w0))
    a1 = mixed(cour, 1, w1, d0, right(w1))
    a2 = mixed(cour, 2, d0, d1, right(d0))
    b0 = mixed(cour, 0, a0, a1, right(a0))
    b1 = mixed(cour, 1, a1, a2, right(a1))
    value = jnp.where(at < half, b0, pltpu.roll(b1, half, 1))
    quarter = half // 2
    factor = jnp.where(at < half, pltpu.roll(w0, width - quarter, 1), pltpu.roll(w1, quarter, 1))
    live = west[rows + 4 : rows + 5]
    group = (at & (half - 1)) // WIDE

    def times(s, right_side):
        low = right_side.astype(BF16)
        acc = jnp.dot(mats[s, 0], low, preferred_element_type=F32)
        for lev in range(1, levels):
            prod = jnp.dot(mats[s, lev], low, preferred_element_type=F32)
            acc = jnp.where(group == lev, prod, acc)
        return acc

    def stage(i, value):
        s = STEPS - 1 - i
        one = times(s, value)
        two = times(s, one * factor)
        three = times(s, two * factor)
        cand = 0.4 * value + 0.3 * one + 0.2 * two + 0.1 * three
        return jnp.where(live > s.astype(F32), cand, value)

    value = lax.fori_loop(0, STEPS, stage, value)
    out[pl.ds(0, spec, stride=2), :] = value
    out[pl.ds(1, spec, stride=2), :] = pltpu.roll(value, half, 1)


def sum_kernel(parts, out, *, count):
    size = out.shape[0]
    if size == 1:
        out[...] = jnp.sum(parts[...], axis=0, keepdims=True)
        return
    acc = parts[0:size]
    for k in range(1, count):
        acc = acc + parts[k * size : (k + 1) * size]
    out[...] = acc


def add_parts(parts, count):
    size, width = parts.shape[0] // count, parts.shape[1]
    return pl.pallas_call(
        functools.partial(sum_kernel, count=count),
        out_shape=jax.ShapeDtypeStruct((size, width), F32),
        in_specs=[VMEM],
        out_specs=VMEM,
        name=f"add_{count}_parts",
        compiler_params=vmem(4),
    )(parts)


def split3(value):
    high = value.astype(BF16)
    left = value - high.astype(F32)
    mid = left.astype(BF16)
    low = (left - mid.astype(F32)).astype(BF16)
    return high, mid, low


def window_kernel(
    *refs, window, first_level, count, rows, offset, last, grad, regions, near
):
    refs = list(refs)
    own, north, west, corner_r, own_c, north_c, west_c, stiff, state_h, mats_h = refs[:10]
    refs = refs[10:]
    if grad:
        before, emission, region = refs[:3]
        refs = refs[3:]
    if last and not grad:
        refs = refs[1:]
    if not last and first_level == 0:
        edge_r = refs.pop(0)
    if last:
        out_h = refs.pop(0)
        if grad:
            partial = refs.pop(0)
    else:
        lam_out = refs.pop(0)
    x_s, y_s, flat_s, state_s, mats_s, sems = refs[:6]
    refs = refs[6:]
    spec, width = rows // 2, own_c.shape[1]
    get_state = pltpu.make_async_copy(
        state_h.at[window, pl.ds(first_level, count)], state_s, sems.at[0]
    )
    get_mats = pltpu.make_async_copy(
        mats_h.at[:, pl.ds(first_level, count)], mats_s, sems.at[1]
    )
    if not last and first_level == 0:
        near_s = refs.pop(0)
        gets = [
            pltpu.make_async_copy(src.at[0:rows], near_s.at[i], sems.at[3 + i])
            for i, src in enumerate((own, north))
        ]
        for get in gets:
            get.start()
        own, north = near_s.at[0], near_s.at[1]
    get_state.start()
    get_mats.start()
    cour = courant(own_c, north_c, west_c, rows)
    if last:
        corner = corner_r[rows : rows + spec]
    else:
        corner = corner_r[pl.ds(rows + EXTRA, spec, stride=2), :]
    west_v = west.at[0:rows]
    if not last and first_level == 0:
        for get in gets:
            get.wait()
    for lev in range(count):
        start = WIDE * (first_level + lev)
        b0, b1 = advected(own, north, west_v, corner, offset + lev * rows, start, cour)
        x_s[lev, :, 0:width] = b0
        x_s[lev, :, width : 2 * width] = b1
    get_state.wait()
    for lev in range(count):
        flat_s[lev] = state_s[lev].astype(F32)
        y_s[lev, :, 0:width] = flat_s[lev, pl.ds(0, spec, stride=2), :]
        y_s[lev, :, width : 2 * width] = flat_s[lev, pl.ds(1, spec, stride=2), :]
    get_mats.wait()
    live = []
    for lev in range(count):
        both = stiff[first_level + lev]
        live.append(jnp.concatenate([both[0:1], both[1:2]], axis=1))

    def stage(i, carry):
        s = STEPS - 1 - i
        rights = [x_s[lev].astype(BF16) for lev in range(count)]
        cands = [0.4 * x_s[lev] for lev in range(count)]
        for k, share in enumerate((0.3, 0.2, 0.1)):
            prods = [
                jnp.dot(mats_s[s, lev], rights[lev], preferred_element_type=F32)
                for lev in range(count)
            ]
            cands = [cands[lev] + share * prods[lev] for lev in range(count)]
            if k < 2:
                rights = [(prods[lev] * y_s[lev]).astype(BF16) for lev in range(count)]
        for lev in range(count):
            x_s[lev] = jnp.where(live[lev] > s, cands[lev], x_s[lev])
        return carry

    lax.fori_loop(0, STEPS, stage, 0)
    for lev in range(count):
        for r in range(2):
            half = x_s[lev, :, r * width : (r + 1) * width]
            if last:
                flat_s[lev, pl.ds(r, spec, stride=2), :] = half
            else:
                lam_out[pl.ds(lev * rows + r, spec, stride=2), :] = half
    if not last:
        if first_level == 0:
            lam_out[rows : rows + spec] = edge_r[pl.ds(0, spec, stride=2), :]
            lam_out[rows + spec :] = jnp.zeros((TAIL - spec, width), F32)
        return
    out_s = refs.pop(0)
    for lev in range(count):
        out_s[lev] = flat_s[lev].astype(BF16)
    put = pltpu.make_async_copy(out_s, out_h.at[pl.ds(first_level, count)], sems.at[2])
    put.start()
    if grad:
        ids = jnp.concatenate([region[0:1], region[1:2]], axis=1)
        ids = (ids & (near - 1)) * (regions // near) + lax.shift_right_logical(ids, near.bit_length() - 1)
        labels = lax.broadcasted_iota(jnp.int32, (regions, 2 * width), 0)
        onehot = jnp.where(labels == ids, 1.0, 0.0).astype(BF16)
        total = []
        for r in range(2):
            now = flat_s[0, pl.ds(r, spec, stride=2), :]
            then = before[pl.ds(r, spec, stride=2), :]
            total.append((now + then) * emission[pl.ds(r, spec, stride=2), :])
        contrib = jnp.concatenate(total, axis=1)
        contrib = jnp.concatenate([contrib, jnp.zeros((width - spec, 2 * width), F32)], axis=0)
        result = jnp.zeros((regions, width), F32)
        for piece in split3(contrib):
            result = result + lax.dot_general(
                onehot, piece, (((1,), (1,)), ((), ())), preferred_element_type=F32
            )
        partial[...] = result
    put.wait()


def run_window(
    own, north, west, corner, shared, window, first_level, count, last, extra=None, prior=None, edge=None
):
    own_c, north_c, west_c, stiff, state, mats = shared
    rows, width = state.shape[2], state.shape[3]
    spec = rows // 2
    grad = extra is not None
    regions, near = 0, 0
    args = [own, north, west, corner, own_c, north_c, west_c, stiff, state, mats]
    offset = 0 if last else first_level * rows
    sliced = not last and first_level == 0
    specs = [ANY if sliced else VMEM] * 2 + [VMEM] * 6 + [ANY] * 2
    aliases = {}
    if grad:
        before, emission, region, regions, near = extra
        args += [before, emission, region]
        specs += [VMEM] * 3
    if edge is not None:
        args.append(edge)
        specs.append(VMEM)
    if last:
        levels = state.shape[1]
        if not grad:
            aliases = {len(args): 0}
            args.append(prior)
            specs.append(ANY)
        out_shape = [jax.ShapeDtypeStruct((levels, rows, width), BF16)]
        out_specs = [ANY]
        if grad:
            out_shape.append(jax.ShapeDtypeStruct((regions, width), F32))
            out_specs.append(VMEM)
    else:
        out_shape = [
            jax.ShapeDtypeStruct((count * rows + (0 if edge is None else TAIL), width), F32),
        ]
        out_specs = [VMEM]
    scratch = [
        pltpu.VMEM((count, spec, 2 * width), F32),
        pltpu.VMEM((count, spec, 2 * width), F32),
        pltpu.VMEM((count, rows, width), F32),
        pltpu.VMEM((count, rows, width), BF16),
        pltpu.VMEM((STEPS, count, spec, spec), BF16),
        pltpu.SemaphoreType.DMA((5,)),
    ]
    if last:
        scratch.append(pltpu.VMEM((count, rows, width), BF16))
    if sliced:
        scratch.append(pltpu.VMEM((2, rows, width), F32))
    body = functools.partial(
        window_kernel,
        window=window,
        first_level=first_level,
        count=count,
        rows=rows,
        offset=offset,
        last=last,
        grad=grad,
        regions=regions,
        near=near,
    )
    return pl.pallas_call(
        body,
        out_shape=out_shape,
        in_specs=specs,
        out_specs=out_specs,
        scratch_shapes=scratch,
        input_output_aliases=aliases,
        name=f"window{window}_from{first_level}",
        cost_estimate=pl.CostEstimate(flops=0, transcendentals=0, bytes_accessed=COST[window][first_level]),
        compiler_params=vmem(40 if count > 1 else 8),
    )(*args)


def to_north(block):
    bands = lax.axis_size("lat")
    return lax.ppermute(block, "lat", [(i + 1, i) for i in range(bands - 1)])


def to_west(block):
    blocks = lax.axis_size("lon")
    return lax.ppermute(block, "lon", [((j + 1) % blocks, j) for j in range(blocks)])


def per_device(
    adjoint_in, state, inverses, courant_lon, courant_lat, emission, region_id, stiffness
):
    windows, levels, spec, lat_rows, width = state.shape
    rows = spec * lat_rows
    regions = lax.axis_size("lat") * lax.axis_size("lon")
    adj = adjoint_in.reshape(levels, rows, width)
    flat_state = state.reshape(windows, levels, rows, width)
    flat_em = emission.reshape(rows, width)
    mats = jnp.swapaxes(inverses, 2, 3)
    first = pl.pallas_call(
        functools.partial(pack_kernel, rows=rows),
        out_shape=jax.ShapeDtypeStruct((folded_rows(rows) + EXTRA, width), F32),
        in_specs=[VMEM] * 4 + [HBM],
        out_specs=VMEM,
        scratch_shapes=[pltpu.VMEM((levels, rows, width), BF16), pltpu.SemaphoreType.DMA],
        name="pack",
        compiler_params=vmem(56),
    )(adj, courant_lon, courant_lat, stiffness, flat_state)
    first_n = to_north(first)
    full1 = pl.pallas_call(
        functools.partial(rest_kernel, rows=rows),
        out_shape=jax.ShapeDtypeStruct((levels * rows, width), F32),
        in_specs=[VMEM, ANY],
        out_specs=VMEM,
        name="rest",
        compiler_params=vmem(56),
    )(adj, first)
    full1, first_n = lax.optimization_barrier((full1, first_n))
    full1_n = to_north(full1)
    west1_w = to_west(jnp.concatenate([first, first_n], axis=0))
    strip, both = pl.pallas_call(
        functools.partial(strip_kernel, rows=rows),
        out_shape=[
            jax.ShapeDtypeStruct((rows, width), F32),
            jax.ShapeDtypeStruct((2 * (rows + EXTRA), width), F32),
        ],
        in_specs=[VMEM] * 2,
        out_specs=[VMEM] * 2,
        name="strip",
        cost_estimate=pl.CostEstimate(flops=0, transcendentals=0, bytes_accessed=40_000_000),
        compiler_params=vmem(8),
    )(west1_w, mats)
    shared = (first, first_n, both, stiffness, flat_state, mats)
    low0 = run_window(
        full1, full1_n, both, both, shared, 1, 0, 1, False, edge=strip
    )[0]
    low0_n = to_north(low0)
    full1_n, low0 = lax.optimization_barrier((full1_n, low0))
    rest0 = run_window(
        full1, full1_n, both, both, shared, 1, 1, levels - 1, False
    )[0]
    low0_n, rest0 = lax.optimization_barrier((low0_n, rest0))
    rest0_n = to_north(rest0)
    bands, blocks = lax.axis_size("lat"), lax.axis_size("lon")
    near = blocks // 2
    far = regions // near
    low_extra = (low0, flat_em, region_id, regions, near)
    out, partial = run_window(
        low0, low0_n, strip, low0_n, shared, 0, 0, 1, True, extra=low_extra
    )
    line = [list(range(k * near, (k + 1) * near)) for k in range(2)]
    lines = lax.all_to_all(partial, "lon", 0, 0, axis_index_groups=line, tiled=True)
    mine = add_parts(lines, near)
    plane = [list(range(k, regions, near)) for k in range(near)]
    spread = lax.all_to_all(
        mine, ("lat", "lon"), 0, 0, axis_index_groups=plane, tiled=True
    )
    out = run_window(
        rest0, rest0_n, strip, low0_n, shared, 0, 1, levels - 1, True, prior=out
    )[0]
    out, spread = lax.optimization_barrier((out, spread))
    grad = add_parts(spread, far)[:, :spec]
    return out.reshape(levels, spec, lat_rows, width), grad


def solution(mesh):
    in_specs = (
        P(None, None, "lat", "lon"),
        P(None, None, None, "lat", "lon"),
        P(),
        P("lat", "lon"),
        P("lat", "lon"),
        P(None, "lat", "lon"),
        P("lat", "lon"),
        P(None, "lat", "lon"),
    )
    out_specs = (P(None, None, "lat", "lon"), P(("lat", "lon"), None))
    return jax.shard_map(
        per_device, mesh=mesh, in_specs=in_specs, out_specs=out_specs, check_vma=False
    )
```

```python
import functools
import jax
import jax.numpy as jnp
from jax import lax
from jax.experimental import pallas as pl
from jax.experimental.pallas import tpu as pltpu
from jax.sharding import PartitionSpec as P

STEPS = 3
EXTRA = 8
TAIL = 104
WIDE = 4
COST = ((10_000_000, 10_000_000), (40_000_000, 10_000_000))
F32 = jnp.float32
BF16 = jnp.bfloat16
ANY = pl.BlockSpec(memory_space=pl.ANY)
HBM = pl.BlockSpec(memory_space=pltpu.HBM)
VMEM = pl.BlockSpec(memory_space=pltpu.VMEM)


def vmem(mib):
    return pltpu.CompilerParams(vmem_limit_bytes=mib * 2**20)


def lanes(shape):
    return lax.broadcasted_iota(jnp.int32, shape, len(shape) - 1)


def place(acc, block, start):
    moved = pltpu.roll(block, start, 1) if start else block
    at = lanes(block.shape)
    return jnp.where((at >= start) & (at < start + WIDE), moved, acc)


def tall(row):
    return jnp.broadcast_to(row, (8, row.shape[1]))


def folded_rows(rows):
    return -(-rows // 16) * 8


def pack_kernel(adj, clon, clat, stiff, state_h, first, state_s, sem, *, rows):
    levels, _, width = adj.shape
    half = width // 2
    get = pltpu.make_async_copy(state_h.at[state_h.shape[0] - 1], state_s, sem)
    get.start()
    acc = jnp.zeros((rows, width), F32)
    grades = jnp.zeros((8, width), F32)
    for lev in range(levels):
        block = adj[lev].astype(F32)
        if lev == 0:
            first[0:rows] = block
        acc = place(acc, block, WIDE * lev)
        both = stiff[lev].astype(F32)
        grades = place(grades, tall(both[0:1]), WIDE * lev)
        grades = place(grades, tall(both[1:2]), half + WIDE * lev)
    get.wait()
    for lev in range(levels):
        acc = place(acc, state_s[lev].astype(F32), half // 2 + WIDE * lev)
    folded = folded_rows(rows)
    upper = jnp.concatenate([acc[folded:], jnp.zeros((2 * folded - rows, width), F32)], axis=0)
    first[rows : rows + folded] = acc[0:folded] + pltpu.roll(upper, half, 1)
    at = rows + folded
    first[at : at + 2] = clon[...]
    first[at + 2 : at + 4] = clat[...]
    first[at + 4 : at + 8] = grades[0:4]


def rest_kernel(adj, first, rest, *, rows):
    for lev in range(1, adj.shape[0]):
        rest[(lev - 1) * rows : lev * rows] = adj[lev].astype(F32)


def pull(block, lane_from, lane_to, width):
    shift = (lane_to - lane_from) % width
    return pltpu.roll(block, shift, 1) if shift else block


def mixed(cour, at, mid, down, east):
    return cour["keep"][at] * mid + cour["lat"][at] * down + cour["lon"][at] * east


def with_keep(lon, lat):
    return {"lon": lon, "lat": lat, "keep": [1.0 - a - b for a, b in zip(lon, lat)]}


def advected(own, north, west, corner, lev, start, cour):
    width = own.shape[1]
    spec = west.shape[0] // 2
    end = width - 1
    last = lanes((spec, width)) == end
    base = lev * 2 * spec

    def pick(ref, first, parity):
        return ref[pl.ds(first + parity, spec, stride=2), :]

    r0, r1 = pick(own, base, 0), pick(own, base, 1)
    r2, r3 = pick(north, base, 0), pick(north, base, 1)
    w0, w1 = pick(west, 0, 0), pick(west, 0, 1)
    e0, e1 = pull(w0, start, end, width), pull(w1, start, end, width)
    g0, g1 = pull(w0, start + 1, end, width), pull(w1, start + 1, end, width)
    d0 = pull(corner, start, end, width)

    def right(block, edge):
        return jnp.where(last, edge, pltpu.roll(block, width - 1, 1))

    a0 = mixed(cour, 0, r0, r1, right(r0, e0))
    a1 = mixed(cour, 1, r1, r2, right(r1, e1))
    a2 = mixed(cour, 2, r2, r3, right(r2, d0))
    f0 = mixed(cour, 3, e0, e1, g0)
    f1 = mixed(cour, 4, e1, d0, g1)
    b0 = mixed(cour, 0, a0, a1, right(a0, f0))
    b1 = mixed(cour, 1, a1, a2, right(a1, f1))
    return b0, b1


def courant(own_c, north_c, west_c, rows):
    width = own_c.shape[1]
    at = rows + folded_rows(rows)

    def edge(row):
        return pltpu.roll(tall(row), width - 1, 1)[0:1]

    lon = [own_c[at : at + 1], own_c[at + 1 : at + 2], north_c[at : at + 1]]
    lat = [own_c[at + 2 : at + 3], own_c[at + 3 : at + 4], north_c[at + 2 : at + 3]]
    lon += [edge(west_c[rows : rows + 1]), edge(west_c[rows + 1 : rows + 2])]
    lat += [edge(west_c[rows + 2 : rows + 3]), edge(west_c[rows + 3 : rows + 4])]
    return with_keep(lon, lat)


def strip_kernel(packed, mats, out, both, *, rows):
    folded = folded_rows(rows)
    for i in range(2):
        src, dst = i * (folded + EXTRA), i * (rows + EXTRA)
        block = packed[src : src + folded]
        both[dst : dst + folded] = block
        both[dst + folded : dst + rows] = pltpu.roll(block, block.shape[1] // 2, 1)[0 : rows - folded]
        both[dst + rows : dst + rows + EXTRA] = packed[src + folded : src + folded + EXTRA]
    west, diag = both.at[0 : rows + EXTRA], both.at[rows + EXTRA : 2 * (rows + EXTRA)]
    spec, width = rows // 2, both.shape[1]
    half = width // 2
    levels = mats.shape[1]
    at = lanes((spec, width))

    def pick(ref, parity):
        return ref[pl.ds(parity, spec, stride=2), :]

    def spread(row):
        wide = tall(row)
        acc = jnp.zeros((8, width), F32)
        for lev in range(levels):
            acc = place(acc, wide, WIDE * lev)
        return acc[0:1]

    def right(block):
        return pltpu.roll(block, width - 1, 1)

    w0, w1, d0, d1 = pick(west, 0), pick(west, 1), pick(diag, 0), pick(diag, 1)
    lon = [spread(west[rows + i : rows + i + 1]) for i in range(2)]
    lat = [spread(west[rows + i : rows + i + 1]) for i in range(2, 4)]
    lon.append(spread(diag[rows : rows + 1]))
    lat.append(spread(diag[rows + 2 : rows + 3]))
    cour = with_keep(lon, lat)
    a0 = mixed(cour, 0, w0, w1, right(w0))
    a1 = mixed(cour, 1, w1, d0, right(w1))
    a2 = mixed(cour, 2, d0, d1, right(d0))
    b0 = mixed(cour, 0, a0, a1, right(a0))
    b1 = mixed(cour, 1, a1, a2, right(a1))
    value = jnp.where(at < half, b0, pltpu.roll(b1, half, 1))
    quarter = half // 2
    factor = jnp.where(at < half, pltpu.roll(w0, width - quarter, 1), pltpu.roll(w1, quarter, 1))
    live = west[rows + 4 : rows + 5]
    group = (at & (half - 1)) // WIDE

    def times(s, right_side):
        low = right_side.astype(BF16)
        acc = jnp.dot(mats[s, 0], low, preferred_element_type=F32)
        for lev in range(1, levels):
            prod = jnp.dot(mats[s, lev], low, preferred_element_type=F32)
            acc = jnp.where(group == lev, prod, acc)
        return acc

    def stage(i, value):
        s = STEPS - 1 - i
        one = times(s, value)
        two = times(s, one * factor)
        three = times(s, two * factor)
        cand = 0.4 * value + 0.3 * one + 0.2 * two + 0.1 * three
        return jnp.where(live > s.astype(F32), cand, value)

    value = lax.fori_loop(0, STEPS, stage, value)
    out[pl.ds(0, spec, stride=2), :] = value
    out[pl.ds(1, spec, stride=2), :] = pltpu.roll(value, half, 1)


def sum_kernel(parts, out, *, count):
    size = out.shape[0]
    if size == 1:
        out[...] = jnp.sum(parts[...], axis=0, keepdims=True)
        return
    acc = parts[0:size]
    for k in range(1, count):
        acc = acc + parts[k * size : (k + 1) * size]
    out[...] = acc


def add_parts(parts, count):
    size, width = parts.shape[0] // count, parts.shape[1]
    return pl.pallas_call(
        functools.partial(sum_kernel, count=count),
        out_shape=jax.ShapeDtypeStruct((size, width), F32),
        in_specs=[VMEM],
        out_specs=VMEM,
        name=f"add_{count}_parts",
        compiler_params=vmem(4),
    )(parts)


def split3(value):
    high = value.astype(BF16)
    left = value - high.astype(F32)
    mid = left.astype(BF16)
    low = (left - mid.astype(F32)).astype(BF16)
    return high, mid, low


def window_kernel(
    *refs, window, first_level, count, rows, last, grad, regions
):
    refs = list(refs)
    own, north, west, corner_r, own_c, north_c, west_c, stiff, state_h, mats_h = refs[:10]
    refs = refs[10:]
    if grad:
        before, emission, region = refs[:3]
        refs = refs[3:]
    if last and not grad:
        refs = refs[1:]
    if not last and first_level == 0:
        edge_r = refs.pop(0)
    if last:
        out_h = refs.pop(0)
        if grad:
            partial = refs.pop(0)
    else:
        lam_out = refs.pop(0)
    x_s, y_s, flat_s, state_s, mats_s, sems = refs[:6]
    refs = refs[6:]
    spec, width = rows // 2, own_c.shape[1]
    get_state = pltpu.make_async_copy(
        state_h.at[window, pl.ds(first_level, count)], state_s, sems.at[0]
    )
    get_mats = pltpu.make_async_copy(
        mats_h.at[:, pl.ds(first_level, count)], mats_s, sems.at[1]
    )
    get_state.start()
    get_mats.start()
    cour = courant(own_c, north_c, west_c, rows)
    if last:
        corner = corner_r[rows : rows + spec]
    else:
        corner = corner_r[pl.ds(rows + EXTRA, spec, stride=2), :]
    west_v = west.at[0:rows]
    for lev in range(count):
        start = WIDE * (first_level + lev)
        b0, b1 = advected(own, north, west_v, corner, lev, start, cour)
        x_s[lev, :, 0:width] = b0
        x_s[lev, :, width : 2 * width] = b1
    get_state.wait()
    for lev in range(count):
        flat_s[lev] = state_s[lev].astype(F32)
        y_s[lev, :, 0:width] = flat_s[lev, pl.ds(0, spec, stride=2), :]
        y_s[lev, :, width : 2 * width] = flat_s[lev, pl.ds(1, spec, stride=2), :]
    get_mats.wait()
    live = []
    for lev in range(count):
        both = stiff[first_level + lev]
        live.append(jnp.concatenate([both[0:1], both[1:2]], axis=1))

    def stage(i, carry):
        s = STEPS - 1 - i
        rights = [x_s[lev].astype(BF16) for lev in range(count)]
        cands = [0.4 * x_s[lev] for lev in range(count)]
        for k, share in enumerate((0.3, 0.2, 0.1)):
            prods = [
                jnp.dot(mats_s[s, lev], rights[lev], preferred_element_type=F32)
                for lev in range(count)
            ]
            cands = [cands[lev] + share * prods[lev] for lev in range(count)]
            if k < 2:
                rights = [(prods[lev] * y_s[lev]).astype(BF16) for lev in range(count)]
        for lev in range(count):
            x_s[lev] = jnp.where(live[lev] > s, cands[lev], x_s[lev])
        return carry

    lax.fori_loop(0, STEPS, stage, 0)
    for lev in range(count):
        for r in range(2):
            half = x_s[lev, :, r * width : (r + 1) * width]
            if last:
                flat_s[lev, pl.ds(r, spec, stride=2), :] = half
            else:
                lam_out[pl.ds(lev * rows + r, spec, stride=2), :] = half
    if not last:
        if first_level == 0:
            lam_out[rows : rows + spec] = edge_r[pl.ds(0, spec, stride=2), :]
            lam_out[rows + spec :] = jnp.zeros((TAIL - spec, width), F32)
        return
    out_s = refs.pop(0)
    for lev in range(count):
        out_s[lev] = flat_s[lev].astype(BF16)
    put = pltpu.make_async_copy(out_s, out_h.at[pl.ds(first_level, count)], sems.at[2])
    put.start()
    if grad:
        ids = jnp.concatenate([region[0:1], region[1:2]], axis=1)
        labels = lax.broadcasted_iota(jnp.int32, (regions, 2 * width), 0)
        onehot = jnp.where(labels == ids, 1.0, 0.0).astype(BF16)
        total = []
        for r in range(2):
            now = flat_s[0, pl.ds(r, spec, stride=2), :]
            then = before[pl.ds(r, spec, stride=2), :]
            total.append((now + then) * emission[pl.ds(r, spec, stride=2), :])
        contrib = jnp.concatenate(total, axis=1)
        contrib = jnp.concatenate([contrib, jnp.zeros((width - spec, 2 * width), F32)], axis=0)
        result = jnp.zeros((regions, width), F32)
        for piece in split3(contrib):
            result = result + lax.dot_general(
                onehot, piece, (((1,), (1,)), ((), ())), preferred_element_type=F32
            )
        partial[...] = result
    put.wait()


def run_window(
    own, north, west, corner, shared, window, first_level, count, last, extra=None, prior=None, edge=None
):
    own_c, north_c, west_c, stiff, state, mats = shared
    rows, width = state.shape[2], state.shape[3]
    spec = rows // 2
    grad = extra is not None
    regions = 0
    args = [own, north, west, corner, own_c, north_c, west_c, stiff, state, mats]
    specs = [VMEM] * 8 + [ANY] * 2
    aliases = {}
    if grad:
        before, emission, region, regions = extra
        args += [before, emission, region]
        specs += [VMEM] * 3
    if edge is not None:
        args.append(edge)
        specs.append(VMEM)
    if last:
        levels = state.shape[1]
        if not grad:
            aliases = {len(args): 0}
            args.append(prior)
            specs.append(ANY)
        out_shape = [jax.ShapeDtypeStruct((levels, rows, width), BF16)]
        out_specs = [ANY]
        if grad:
            out_shape.append(jax.ShapeDtypeStruct((regions, width), F32))
            out_specs.append(VMEM)
    else:
        out_shape = [
            jax.ShapeDtypeStruct((count * rows + (0 if edge is None else TAIL), width), F32),
        ]
        out_specs = [VMEM]
    scratch = [
        pltpu.VMEM((count, spec, 2 * width), F32),
        pltpu.VMEM((count, spec, 2 * width), F32),
        pltpu.VMEM((count, rows, width), F32),
        pltpu.VMEM((count, rows, width), BF16),
        pltpu.VMEM((STEPS, count, spec, spec), BF16),
        pltpu.SemaphoreType.DMA((3,)),
    ]
    if last:
        scratch.append(pltpu.VMEM((count, rows, width), BF16))
    body = functools.partial(
        window_kernel,
        window=window,
        first_level=first_level,
        count=count,
        rows=rows,
        last=last,
        grad=grad,
        regions=regions,
    )
    return pl.pallas_call(
        body,
        out_shape=out_shape,
        in_specs=specs,
        out_specs=out_specs,
        scratch_shapes=scratch,
        input_output_aliases=aliases,
        name=f"window{window}_from{first_level}",
        cost_estimate=pl.CostEstimate(flops=0, transcendentals=0, bytes_accessed=COST[window][first_level]),
        compiler_params=vmem((16 if not last else 56) if count > 1 else 8),
    )(*args)


def to_north(block):
    bands = lax.axis_size("lat")
    return lax.ppermute(block, "lat", [(i + 1, i) for i in range(bands - 1)])


def to_west(block):
    blocks = lax.axis_size("lon")
    return lax.ppermute(block, "lon", [((j + 1) % blocks, j) for j in range(blocks)])


def per_device(
    adjoint_in, state, inverses, courant_lon, courant_lat, emission, region_id, stiffness
):
    windows, levels, spec, lat_rows, width = state.shape
    rows = spec * lat_rows
    regions = lax.axis_size("lat") * lax.axis_size("lon")
    adj = adjoint_in.reshape(levels, rows, width)
    flat_state = state.reshape(windows, levels, rows, width)
    flat_em = emission.reshape(rows, width)
    mats = jnp.swapaxes(inverses, 2, 3)
    low1 = pl.pallas_call(
        functools.partial(pack_kernel, rows=rows),
        out_shape=jax.ShapeDtypeStruct((rows + folded_rows(rows) + EXTRA, width), F32),
        in_specs=[VMEM] * 4 + [HBM],
        out_specs=VMEM,
        scratch_shapes=[pltpu.VMEM((levels, rows, width), BF16), pltpu.SemaphoreType.DMA],
        name="pack",
        compiler_params=vmem(56),
    )(adj, courant_lon, courant_lat, stiffness, flat_state)
    low1_n = to_north(low1)
    rest1 = pl.pallas_call(
        functools.partial(rest_kernel, rows=rows),
        out_shape=jax.ShapeDtypeStruct(((levels - 1) * rows, width), F32),
        in_specs=[VMEM, ANY],
        out_specs=VMEM,
        name="rest",
        compiler_params=vmem(56),
    )(adj, low1)
    rest1, low1_n = lax.optimization_barrier((rest1, low1_n))
    rest1_n = to_north(rest1)
    west1_w = to_west(jnp.concatenate([low1[rows:], low1_n[rows:]], axis=0))
    strip, both = pl.pallas_call(
        functools.partial(strip_kernel, rows=rows),
        out_shape=[
            jax.ShapeDtypeStruct((rows, width), F32),
            jax.ShapeDtypeStruct((2 * (rows + EXTRA), width), F32),
        ],
        in_specs=[VMEM] * 2,
        out_specs=[VMEM] * 2,
        name="strip",
        cost_estimate=pl.CostEstimate(flops=0, transcendentals=0, bytes_accessed=40_000_000),
        compiler_params=vmem(8),
    )(west1_w, mats)
    shared = (low1, low1_n, both, stiffness, flat_state, mats)
    low0 = run_window(
        low1, low1_n, both, both, shared, 1, 0, 1, False, edge=strip
    )[0]
    low0_n = to_north(low0)
    rest1_n, low0 = lax.optimization_barrier((rest1_n, low0))
    rest0 = run_window(
        rest1, rest1_n, both, both, shared, 1, 1, levels - 1, False
    )[0]
    low0_n, rest0 = lax.optimization_barrier((low0_n, rest0))
    rest0_n = to_north(rest0)
    low_extra = (low0, flat_em, region_id, regions)
    out, partial = run_window(
        low0, low0_n, strip, low0_n, shared, 0, 0, 1, True, extra=low_extra
    )
    spread = lax.all_to_all(partial, ("lat", "lon"), 0, 0, tiled=True)
    out = run_window(
        rest0, rest0_n, strip, low0_n, shared, 0, 1, levels - 1, True, prior=out
    )[0]
    out, spread = lax.optimization_barrier((out, spread))
    grad = add_parts(spread, regions)[:, :spec]
    return out.reshape(levels, spec, lat_rows, width), grad


def solution(mesh):
    in_specs = (
        P(None, None, "lat", "lon"),
        P(None, None, None, "lat", "lon"),
        P(),
        P("lat", "lon"),
        P("lat", "lon"),
        P(None, "lat", "lon"),
        P("lat", "lon"),
        P(None, "lat", "lon"),
    )
    out_specs = (P(None, None, "lat", "lon"), P(("lat", "lon"), None))
    return jax.shard_map(
        per_device, mesh=mesh, in_specs=in_specs, out_specs=out_specs, check_vma=False
    )
```

```python
import functools
import jax
import jax.numpy as jnp
from jax import lax
from jax.experimental import pallas as pl
from jax.experimental.pallas import tpu as pltpu
from jax.sharding import PartitionSpec as P

STEPS = 3
EXTRA = 8
TAIL = 104
WIDE = 4
COST = ((10_000_000, 10_000_000), (40_000_000, 10_000_000))
F32 = jnp.float32
BF16 = jnp.bfloat16
ANY = pl.BlockSpec(memory_space=pl.ANY)
HBM = pl.BlockSpec(memory_space=pltpu.HBM)
VMEM = pl.BlockSpec(memory_space=pltpu.VMEM)


def vmem(mib):
    return pltpu.CompilerParams(vmem_limit_bytes=mib * 2**20)


def lanes(shape):
    return lax.broadcasted_iota(jnp.int32, shape, len(shape) - 1)


def place(acc, block, start):
    moved = pltpu.roll(block, start, 1) if start else block
    at = lanes(block.shape)
    return jnp.where((at >= start) & (at < start + WIDE), moved, acc)


def tall(row):
    return jnp.broadcast_to(row, (8, row.shape[1]))


def folded_rows(rows):
    return -(-rows // 16) * 8


def pack_kernel(adj, clon, clat, stiff, state_h, first, state_s, sem, *, rows):
    levels, _, width = adj.shape
    half = width // 2
    get = pltpu.make_async_copy(state_h.at[state_h.shape[0] - 1], state_s, sem)
    get.start()
    acc = jnp.zeros((rows, width), F32)
    grades = jnp.zeros((8, width), F32)
    for lev in range(levels):
        block = adj[lev].astype(F32)
        if lev == 0:
            first[0:rows] = block
        acc = place(acc, block, WIDE * lev)
        both = stiff[lev].astype(F32)
        grades = place(grades, tall(both[0:1]), WIDE * lev)
        grades = place(grades, tall(both[1:2]), half + WIDE * lev)
    get.wait()
    for lev in range(levels):
        acc = place(acc, state_s[lev].astype(F32), half // 2 + WIDE * lev)
    folded = folded_rows(rows)
    upper = jnp.concatenate([acc[folded:], jnp.zeros((2 * folded - rows, width), F32)], axis=0)
    first[rows : rows + folded] = acc[0:folded] + pltpu.roll(upper, half, 1)
    at = rows + folded
    first[at : at + 2] = clon[...]
    first[at + 2 : at + 4] = clat[...]
    first[at + 4 : at + 8] = grades[0:4]


def rest_kernel(adj, first, rest, *, rows):
    for lev in range(1, adj.shape[0]):
        rest[(lev - 1) * rows : lev * rows] = adj[lev].astype(F32)


def pull(block, lane_from, lane_to, width):
    shift = (lane_to - lane_from) % width
    return pltpu.roll(block, shift, 1) if shift else block


def mixed(cour, at, mid, down, east):
    return cour["keep"][at] * mid + cour["lat"][at] * down + cour["lon"][at] * east


def with_keep(lon, lat):
    return {"lon": lon, "lat": lat, "keep": [1.0 - a - b for a, b in zip(lon, lat)]}


def advected(own, north, west, corner, lev, start, cour):
    width = own.shape[1]
    spec = west.shape[0] // 2
    end = width - 1
    last = lanes((spec, width)) == end
    base = lev * 2 * spec

    def pick(ref, first, parity):
        return ref[pl.ds(first + parity, spec, stride=2), :]

    r0, r1 = pick(own, base, 0), pick(own, base, 1)
    r2, r3 = pick(north, base, 0), pick(north, base, 1)
    w0, w1 = pick(west, 0, 0), pick(west, 0, 1)
    e0, e1 = pull(w0, start, end, width), pull(w1, start, end, width)
    g0, g1 = pull(w0, start + 1, end, width), pull(w1, start + 1, end, width)
    d0 = pull(corner, start, end, width)

    def right(block, edge):
        return jnp.where(last, edge, pltpu.roll(block, width - 1, 1))

    a0 = mixed(cour, 0, r0, r1, right(r0, e0))
    a1 = mixed(cour, 1, r1, r2, right(r1, e1))
    a2 = mixed(cour, 2, r2, r3, right(r2, d0))
    f0 = mixed(cour, 3, e0, e1, g0)
    f1 = mixed(cour, 4, e1, d0, g1)
    b0 = mixed(cour, 0, a0, a1, right(a0, f0))
    b1 = mixed(cour, 1, a1, a2, right(a1, f1))
    return b0, b1


def courant(own_c, north_c, west_c, rows):
    width = own_c.shape[1]
    at = rows + folded_rows(rows)

    def edge(row):
        return pltpu.roll(tall(row), width - 1, 1)[0:1]

    lon = [own_c[at : at + 1], own_c[at + 1 : at + 2], north_c[at : at + 1]]
    lat = [own_c[at + 2 : at + 3], own_c[at + 3 : at + 4], north_c[at + 2 : at + 3]]
    lon += [edge(west_c[rows : rows + 1]), edge(west_c[rows + 1 : rows + 2])]
    lat += [edge(west_c[rows + 2 : rows + 3]), edge(west_c[rows + 3 : rows + 4])]
    return with_keep(lon, lat)


def strip_start(west, diag, levels, rows):
    spec, width = rows // 2, west.shape[1]
    half, quarter = width // 2, width // 4
    at = lanes((spec, width))

    def pick(ref, parity):
        return ref[pl.ds(parity, spec, stride=2), :]

    def spread(row):
        wide = tall(row)
        acc = jnp.zeros((8, width), F32)
        for lev in range(levels):
            acc = place(acc, wide, WIDE * lev)
        return acc[0:1]

    def right(block):
        return pltpu.roll(block, width - 1, 1)

    w0, w1, d0, d1 = pick(west, 0), pick(west, 1), pick(diag, 0), pick(diag, 1)
    lon = [spread(west[rows + i : rows + i + 1]) for i in range(2)]
    lat = [spread(west[rows + i : rows + i + 1]) for i in range(2, 4)]
    lon.append(spread(diag[rows : rows + 1]))
    lat.append(spread(diag[rows + 2 : rows + 3]))
    cour = with_keep(lon, lat)
    a0 = mixed(cour, 0, w0, w1, right(w0))
    a1 = mixed(cour, 1, w1, d0, right(w1))
    a2 = mixed(cour, 2, d0, d1, right(d0))
    b0 = mixed(cour, 0, a0, a1, right(a0))
    b1 = mixed(cour, 1, a1, a2, right(a1))
    value = jnp.where(at < half, b0, pltpu.roll(b1, half, 1))
    factor = jnp.where(at < half, pltpu.roll(w0, width - quarter, 1), pltpu.roll(w1, quarter, 1))
    return value, factor, west[rows + 4 : rows + 5], (at & (half - 1)) // WIDE


def first_kernel(
    own, north, packed, stiff, state_h, mats_h, lam_out, strip_out, both,
    x_s, y_s, flat_s, state_s, mats_s, sems, *, rows
):
    spec, width = rows // 2, own.shape[1]
    levels, folded = mats_s.shape[1], folded_rows(rows)
    get_state = pltpu.make_async_copy(state_h.at[state_h.shape[0] - 1, 0], state_s, sems.at[0])
    get_mats = pltpu.make_async_copy(mats_h, mats_s, sems.at[1])
    get_state.start()
    get_mats.start()
    for i in range(2):
        src, dst = i * (folded + EXTRA), i * (rows + EXTRA)
        block = packed[src : src + folded]
        both[dst : dst + folded] = block
        both[dst + folded : dst + rows] = pltpu.roll(block, width // 2, 1)[0 : rows - folded]
        both[dst + rows : dst + rows + EXTRA] = packed[src + folded : src + folded + EXTRA]
    west, diag = both.at[0 : rows + EXTRA], both.at[rows + EXTRA : 2 * (rows + EXTRA)]
    value, factor, grade, group = strip_start(west, diag, levels, rows)
    cour = courant(own, north, west, rows)
    corner = diag[pl.ds(0, spec, stride=2), :]
    b0, b1 = advected(own, north, both.at[0:rows], corner, 0, 0, cour)
    x_s[:, 0:width] = b0
    x_s[:, width : 2 * width] = b1
    get_state.wait()
    flat_s[...] = state_s[...].astype(F32)
    y_s[:, 0:width] = flat_s[pl.ds(0, spec, stride=2), :]
    y_s[:, width : 2 * width] = flat_s[pl.ds(1, spec, stride=2), :]
    get_mats.wait()
    live = jnp.concatenate([stiff[0][0:1], stiff[0][1:2]], axis=1)

    def stage(i, value):
        s = STEPS - 1 - i
        main, side = x_s[...].astype(BF16), value.astype(BF16)
        cand, edge = 0.4 * x_s[...], 0.4 * value
        for k, share in enumerate((0.3, 0.2, 0.1)):
            prod = jnp.dot(mats_s[s, 0], main, preferred_element_type=F32)
            part = jnp.dot(mats_s[s, 0], side, preferred_element_type=F32)
            for lev in range(1, levels):
                one = jnp.dot(mats_s[s, lev], side, preferred_element_type=F32)
                part = jnp.where(group == lev, one, part)
            cand, edge = cand + share * prod, edge + share * part
            if k < 2:
                main, side = (prod * y_s[...]).astype(BF16), (part * factor).astype(BF16)
        x_s[...] = jnp.where(live > s, cand, x_s[...])
        return jnp.where(grade > s.astype(F32), edge, value)

    value = lax.fori_loop(0, STEPS, stage, value)
    for r in range(2):
        lam_out[pl.ds(r, spec, stride=2), :] = x_s[:, r * width : (r + 1) * width]
    lam_out[rows : rows + spec] = value
    lam_out[rows + spec :] = jnp.zeros((TAIL - spec, width), F32)
    strip_out[pl.ds(0, spec, stride=2), :] = value
    strip_out[pl.ds(1, spec, stride=2), :] = pltpu.roll(value, width // 2, 1)


def sum_kernel(parts, out, *, count):
    size = out.shape[0]
    if size == 1:
        out[...] = jnp.sum(parts[...], axis=0, keepdims=True)
        return
    acc = parts[0:size]
    for k in range(1, count):
        acc = acc + parts[k * size : (k + 1) * size]
    out[...] = acc


def add_parts(parts, count):
    size, width = parts.shape[0] // count, parts.shape[1]
    return pl.pallas_call(
        functools.partial(sum_kernel, count=count),
        out_shape=jax.ShapeDtypeStruct((size, width), F32),
        in_specs=[VMEM],
        out_specs=VMEM,
        name=f"add_{count}_parts",
        compiler_params=vmem(4),
    )(parts)


def split3(value):
    high = value.astype(BF16)
    left = value - high.astype(F32)
    mid = left.astype(BF16)
    low = (left - mid.astype(F32)).astype(BF16)
    return high, mid, low


def window_kernel(
    *refs, window, first_level, count, rows, last, grad, regions
):
    refs = list(refs)
    own, north, west, corner_r, own_c, north_c, west_c, stiff, state_h, mats_h = refs[:10]
    refs = refs[10:]
    if grad:
        before, emission, region = refs[:3]
        refs = refs[3:]
    if last and not grad:
        refs = refs[1:]
    if last:
        out_h = refs.pop(0)
        if grad:
            partial = refs.pop(0)
    else:
        lam_out = refs.pop(0)
    x_s, y_s, flat_s, state_s, mats_s, sems = refs[:6]
    refs = refs[6:]
    spec, width = rows // 2, own_c.shape[1]
    get_state = pltpu.make_async_copy(
        state_h.at[window, pl.ds(first_level, count)], state_s, sems.at[0]
    )
    get_mats = pltpu.make_async_copy(
        mats_h.at[:, pl.ds(first_level, count)], mats_s, sems.at[1]
    )
    gets = []
    if not last:
        own_s, north_s, level_sems = refs[:3]
        for lev in range(count):
            part = pl.ds(lev * rows, rows)
            gets.append(
                [
                    pltpu.make_async_copy(src.at[part], dst.at[part], level_sems.at[i, lev])
                    for i, (src, dst) in enumerate(((own, own_s), (north, north_s)))
                ]
            )
            for get in gets[lev]:
                get.start()
        own, north = own_s, north_s
    get_state.start()
    get_mats.start()
    cour = courant(own_c, north_c, west_c, rows)
    if last:
        corner = corner_r[rows : rows + spec]
    else:
        corner = corner_r[pl.ds(rows + EXTRA, spec, stride=2), :]
    west_v = west.at[0:rows]
    for lev in range(count):
        start = WIDE * (first_level + lev)
        for get in gets[lev] if gets else ():
            get.wait()
        b0, b1 = advected(own, north, west_v, corner, lev, start, cour)
        x_s[lev, :, 0:width] = b0
        x_s[lev, :, width : 2 * width] = b1
    get_state.wait()
    for lev in range(count):
        flat_s[lev] = state_s[lev].astype(F32)
        y_s[lev, :, 0:width] = flat_s[lev, pl.ds(0, spec, stride=2), :]
        y_s[lev, :, width : 2 * width] = flat_s[lev, pl.ds(1, spec, stride=2), :]
    get_mats.wait()
    live = []
    for lev in range(count):
        both = stiff[first_level + lev]
        live.append(jnp.concatenate([both[0:1], both[1:2]], axis=1))

    def stage(i, carry):
        s = STEPS - 1 - i
        rights = [x_s[lev].astype(BF16) for lev in range(count)]
        cands = [0.4 * x_s[lev] for lev in range(count)]
        for k, share in enumerate((0.3, 0.2, 0.1)):
            prods = [
                jnp.dot(mats_s[s, lev], rights[lev], preferred_element_type=F32)
                for lev in range(count)
            ]
            cands = [cands[lev] + share * prods[lev] for lev in range(count)]
            if k < 2:
                rights = [(prods[lev] * y_s[lev]).astype(BF16) for lev in range(count)]
        for lev in range(count):
            x_s[lev] = jnp.where(live[lev] > s, cands[lev], x_s[lev])
        return carry

    lax.fori_loop(0, STEPS, stage, 0)
    for lev in range(count):
        for r in range(2):
            half = x_s[lev, :, r * width : (r + 1) * width]
            if last:
                flat_s[lev, pl.ds(r, spec, stride=2), :] = half
            else:
                lam_out[pl.ds(lev * rows + r, spec, stride=2), :] = half
    if not last:
        return
    out_s = refs.pop(0)
    for lev in range(count):
        out_s[lev] = flat_s[lev].astype(BF16)
    put = pltpu.make_async_copy(out_s, out_h.at[pl.ds(first_level, count)], sems.at[2])
    put.start()
    if grad:
        ids = jnp.concatenate([region[0:1], region[1:2]], axis=1)
        labels = lax.broadcasted_iota(jnp.int32, (regions, 2 * width), 0)
        onehot = jnp.where(labels == ids, 1.0, 0.0).astype(BF16)
        total = []
        for r in range(2):
            now = flat_s[0, pl.ds(r, spec, stride=2), :]
            then = before[pl.ds(r, spec, stride=2), :]
            total.append((now + then) * emission[pl.ds(r, spec, stride=2), :])
        contrib = jnp.concatenate(total, axis=1)
        contrib = jnp.concatenate([contrib, jnp.zeros((width - spec, 2 * width), F32)], axis=0)
        result = jnp.zeros((regions, width), F32)
        for piece in split3(contrib):
            result = result + lax.dot_general(
                onehot, piece, (((1,), (1,)), ((), ())), preferred_element_type=F32
            )
        partial[...] = result
    put.wait()


def run_window(
    own, north, west, corner, shared, window, first_level, count, last, extra=None, prior=None
):
    own_c, north_c, west_c, stiff, state, mats = shared
    rows, width = state.shape[2], state.shape[3]
    spec = rows // 2
    grad = extra is not None
    regions = 0
    args = [own, north, west, corner, own_c, north_c, west_c, stiff, state, mats]
    specs = [VMEM if last else ANY] * 2 + [VMEM] * 6 + [ANY] * 2
    aliases = {}
    if grad:
        before, emission, region, regions = extra
        args += [before, emission, region]
        specs += [VMEM] * 3
    if last:
        levels = state.shape[1]
        if not grad:
            aliases = {len(args): 0}
            args.append(prior)
            specs.append(ANY)
        out_shape = [jax.ShapeDtypeStruct((levels, rows, width), BF16)]
        out_specs = [ANY]
        if grad:
            out_shape.append(jax.ShapeDtypeStruct((regions, width), F32))
            out_specs.append(VMEM)
    else:
        out_shape = [
            jax.ShapeDtypeStruct((count * rows, width), F32),
        ]
        out_specs = [VMEM]
    scratch = [
        pltpu.VMEM((count, spec, 2 * width), F32),
        pltpu.VMEM((count, spec, 2 * width), F32),
        pltpu.VMEM((count, rows, width), F32),
        pltpu.VMEM((count, rows, width), BF16),
        pltpu.VMEM((STEPS, count, spec, spec), BF16),
        pltpu.SemaphoreType.DMA((3,)),
    ]
    if last:
        scratch.append(pltpu.VMEM((count, rows, width), BF16))
    else:
        scratch += [pltpu.VMEM((count * rows, width), F32)] * 2
        scratch.append(pltpu.SemaphoreType.DMA((2, count)))
    body = functools.partial(
        window_kernel,
        window=window,
        first_level=first_level,
        count=count,
        rows=rows,
        last=last,
        grad=grad,
        regions=regions,
    )
    return pl.pallas_call(
        body,
        out_shape=out_shape,
        in_specs=specs,
        out_specs=out_specs,
        scratch_shapes=scratch,
        input_output_aliases=aliases,
        name=f"window{window}_from{first_level}",
        cost_estimate=pl.CostEstimate(flops=0, transcendentals=0, bytes_accessed=COST[window][first_level]),
        compiler_params=vmem((16 if last else 52) if count > 1 else 8),
    )(*args)


def to_north(block):
    bands = lax.axis_size("lat")
    return lax.ppermute(block, "lat", [(i + 1, i) for i in range(bands - 1)])


def to_west(block):
    blocks = lax.axis_size("lon")
    return lax.ppermute(block, "lon", [((j + 1) % blocks, j) for j in range(blocks)])


def per_device(
    adjoint_in, state, inverses, courant_lon, courant_lat, emission, region_id, stiffness
):
    windows, levels, spec, lat_rows, width = state.shape
    rows = spec * lat_rows
    regions = lax.axis_size("lat") * lax.axis_size("lon")
    adj = adjoint_in.reshape(levels, rows, width)
    flat_state = state.reshape(windows, levels, rows, width)
    flat_em = emission.reshape(rows, width)
    mats = jnp.swapaxes(inverses, 2, 3)
    low1 = pl.pallas_call(
        functools.partial(pack_kernel, rows=rows),
        out_shape=jax.ShapeDtypeStruct((rows + folded_rows(rows) + EXTRA, width), F32),
        in_specs=[VMEM] * 4 + [HBM],
        out_specs=VMEM,
        scratch_shapes=[pltpu.VMEM((levels, rows, width), BF16), pltpu.SemaphoreType.DMA],
        name="pack",
        compiler_params=vmem(56),
    )(adj, courant_lon, courant_lat, stiffness, flat_state)
    low1_n = to_north(low1)
    rest1 = pl.pallas_call(
        functools.partial(rest_kernel, rows=rows),
        out_shape=jax.ShapeDtypeStruct(((levels - 1) * rows, width), F32),
        in_specs=[VMEM, ANY],
        out_specs=VMEM,
        name="rest",
        compiler_params=vmem(56),
    )(adj, low1)
    rest1, low1_n = lax.optimization_barrier((rest1, low1_n))
    rest1_n = to_north(rest1)
    west1_w = to_west(jnp.concatenate([low1[rows:], low1_n[rows:]], axis=0))
    low0, strip, both = pl.pallas_call(
        functools.partial(first_kernel, rows=rows),
        out_shape=[
            jax.ShapeDtypeStruct((rows + TAIL, width), F32),
            jax.ShapeDtypeStruct((rows, width), F32),
            jax.ShapeDtypeStruct((2 * (rows + EXTRA), width), F32),
        ],
        in_specs=[VMEM] * 4 + [ANY] * 2,
        out_specs=[VMEM] * 3,
        scratch_shapes=[
            pltpu.VMEM((spec, 2 * width), F32),
            pltpu.VMEM((spec, 2 * width), F32),
            pltpu.VMEM((rows, width), F32),
            pltpu.VMEM((rows, width), BF16),
            pltpu.VMEM((STEPS, levels, spec, spec), BF16),
            pltpu.SemaphoreType.DMA((2,)),
        ],
        cost_estimate=pl.CostEstimate(flops=0, transcendentals=0, bytes_accessed=60_000_000),
        name="first",
        compiler_params=vmem(8),
    )(low1, low1_n, west1_w, stiffness, flat_state, mats)
    shared = (low1, low1_n, both, stiffness, flat_state, mats)
    low0_n = to_north(low0)
    rest1_n, low0 = lax.optimization_barrier((rest1_n, low0))
    rest0 = run_window(
        rest1, rest1_n, both, both, shared, 1, 1, levels - 1, False
    )[0]
    low0_n, rest0 = lax.optimization_barrier((low0_n, rest0))
    rest0_n = to_north(rest0)
    low_extra = (low0, flat_em, region_id, regions)
    out, partial = run_window(
        low0, low0_n, strip, low0_n, shared, 0, 0, 1, True, extra=low_extra
    )
    spread = lax.all_to_all(partial, ("lat", "lon"), 0, 0, tiled=True)
    out = run_window(
        rest0, rest0_n, strip, low0_n, shared, 0, 1, levels - 1, True, prior=out
    )[0]
    out, spread = lax.optimization_barrier((out, spread))
    grad = add_parts(spread, regions)[:, :spec]
    return out.reshape(levels, spec, lat_rows, width), grad


def solution(mesh):
    in_specs = (
        P(None, None, "lat", "lon"),
        P(None, None, None, "lat", "lon"),
        P(),
        P("lat", "lon"),
        P("lat", "lon"),
        P(None, "lat", "lon"),
        P("lat", "lon"),
        P(None, "lat", "lon"),
    )
    out_specs = (P(None, None, "lat", "lon"), P(("lat", "lon"), None))
    return jax.shard_map(
        per_device, mesh=mesh, in_specs=in_specs, out_specs=out_specs, check_vma=False
    )
```

```python
import functools
import jax
import jax.numpy as jnp
from jax import lax
from jax.experimental import pallas as pl
from jax.experimental.pallas import tpu as pltpu
from jax.sharding import PartitionSpec as P

STEPS = 3
EXTRA = 8
TAIL = 104
WIDE = 4
COST = ((10_000_000, 10_000_000), (40_000_000, 10_000_000))
F32 = jnp.float32
BF16 = jnp.bfloat16
ANY = pl.BlockSpec(memory_space=pl.ANY)
HBM = pl.BlockSpec(memory_space=pltpu.HBM)
VMEM = pl.BlockSpec(memory_space=pltpu.VMEM)


def vmem(mib):
    return pltpu.CompilerParams(vmem_limit_bytes=mib * 2**20)


def lanes(shape):
    return lax.broadcasted_iota(jnp.int32, shape, len(shape) - 1)


def place(acc, block, start):
    moved = pltpu.roll(block, start, 1) if start else block
    at = lanes(block.shape)
    return jnp.where((at >= start) & (at < start + WIDE), moved, acc)


def tall(row):
    return jnp.broadcast_to(row, (8, row.shape[1]))


def folded_rows(rows):
    return -(-rows // 16) * 8


def fold(acc, rows):
    width, folded = acc.shape[1], folded_rows(rows)
    upper = jnp.concatenate([acc[folded:], jnp.zeros((2 * folded - rows, width), F32)], axis=0)
    return acc[0:folded] + pltpu.roll(upper, width // 2, 1)


def pack_kernel(adj, clon, clat, stiff, first, *, rows):
    levels, _, width = adj.shape
    acc = jnp.zeros((rows, width), F32)
    grades = jnp.zeros((8, width), F32)
    for lev in range(levels):
        block = adj[lev].astype(F32)
        if lev == 0:
            first[0:rows] = block
        acc = place(acc, block, WIDE * lev)
        both = stiff[lev].astype(F32)
        grades = place(grades, tall(both[0:1]), WIDE * lev)
        grades = place(grades, tall(both[1:2]), width // 2 + WIDE * lev)
    at = rows + folded_rows(rows)
    first[rows:at] = fold(acc, rows)
    first[at : at + 2] = clon[...]
    first[at + 2 : at + 4] = clat[...]
    first[at + 4 : at + 8] = grades[0:4]


def rest_kernel(adj, first, state_h, rest, west, state_s, sem, *, rows):
    levels, _, width = adj.shape
    get = pltpu.make_async_copy(state_h.at[state_h.shape[0] - 1], state_s, sem)
    get.start()
    for lev in range(1, levels):
        rest[(lev - 1) * rows : lev * rows] = adj[lev].astype(F32)
    get.wait()
    acc = jnp.zeros((rows, width), F32)
    for lev in range(levels):
        acc = place(acc, state_s[lev].astype(F32), width // 4 + WIDE * lev)
    at = folded_rows(rows)
    west[0:at] = first[rows : rows + at] + fold(acc, rows)
    west[at:] = first[rows + at :]


def pull(block, lane_from, lane_to, width):
    shift = (lane_to - lane_from) % width
    return pltpu.roll(block, shift, 1) if shift else block


def mixed(cour, at, mid, down, east):
    return cour["keep"][at] * mid + cour["lat"][at] * down + cour["lon"][at] * east


def with_keep(lon, lat):
    return {"lon": lon, "lat": lat, "keep": [1.0 - a - b for a, b in zip(lon, lat)]}


def advected(own, north, west, corner, lev, start, cour):
    width = own.shape[1]
    spec = west.shape[0] // 2
    end = width - 1
    last = lanes((spec, width)) == end
    base = lev * 2 * spec

    def pick(ref, first, parity):
        return ref[pl.ds(first + parity, spec, stride=2), :]

    r0, r1 = pick(own, base, 0), pick(own, base, 1)
    r2, r3 = pick(north, base, 0), pick(north, base, 1)
    w0, w1 = pick(west, 0, 0), pick(west, 0, 1)
    e0, e1 = pull(w0, start, end, width), pull(w1, start, end, width)
    g0, g1 = pull(w0, start + 1, end, width), pull(w1, start + 1, end, width)
    d0 = pull(corner, start, end, width)

    def right(block, edge):
        return jnp.where(last, edge, pltpu.roll(block, width - 1, 1))

    a0 = mixed(cour, 0, r0, r1, right(r0, e0))
    a1 = mixed(cour, 1, r1, r2, right(r1, e1))
    a2 = mixed(cour, 2, r2, r3, right(r2, d0))
    f0 = mixed(cour, 3, e0, e1, g0)
    f1 = mixed(cour, 4, e1, d0, g1)
    b0 = mixed(cour, 0, a0, a1, right(a0, f0))
    b1 = mixed(cour, 1, a1, a2, right(a1, f1))
    return b0, b1


def courant(own_c, north_c, west_c, rows):
    width = own_c.shape[1]
    at = rows + folded_rows(rows)

    def edge(row):
        return pltpu.roll(tall(row), width - 1, 1)[0:1]

    lon = [own_c[at : at + 1], own_c[at + 1 : at + 2], north_c[at : at + 1]]
    lat = [own_c[at + 2 : at + 3], own_c[at + 3 : at + 4], north_c[at + 2 : at + 3]]
    lon += [edge(west_c[rows : rows + 1]), edge(west_c[rows + 1 : rows + 2])]
    lat += [edge(west_c[rows + 2 : rows + 3]), edge(west_c[rows + 3 : rows + 4])]
    return with_keep(lon, lat)


def strip_kernel(packed, mats, out, both, *, rows):
    folded = folded_rows(rows)
    for i in range(2):
        src, dst = i * (folded + EXTRA), i * (rows + EXTRA)
        block = packed[src : src + folded]
        both[dst : dst + folded] = block
        both[dst + folded : dst + rows] = pltpu.roll(block, block.shape[1] // 2, 1)[0 : rows - folded]
        both[dst + rows : dst + rows + EXTRA] = packed[src + folded : src + folded + EXTRA]
    west, diag = both.at[0 : rows + EXTRA], both.at[rows + EXTRA : 2 * (rows + EXTRA)]
    spec, width = rows // 2, both.shape[1]
    half = width // 2
    levels = mats.shape[1]
    at = lanes((spec, width))

    def pick(ref, parity):
        return ref[pl.ds(parity, spec, stride=2), :]

    def spread(row):
        wide = tall(row)
        acc = jnp.zeros((8, width), F32)
        for lev in range(levels):
            acc = place(acc, wide, WIDE * lev)
        return acc[0:1]

    def right(block):
        return pltpu.roll(block, width - 1, 1)

    w0, w1, d0, d1 = pick(west, 0), pick(west, 1), pick(diag, 0), pick(diag, 1)
    lon = [spread(west[rows + i : rows + i + 1]) for i in range(2)]
    lat = [spread(west[rows + i : rows + i + 1]) for i in range(2, 4)]
    lon.append(spread(diag[rows : rows + 1]))
    lat.append(spread(diag[rows + 2 : rows + 3]))
    cour = with_keep(lon, lat)
    a0 = mixed(cour, 0, w0, w1, right(w0))
    a1 = mixed(cour, 1, w1, d0, right(w1))
    a2 = mixed(cour, 2, d0, d1, right(d0))
    b0 = mixed(cour, 0, a0, a1, right(a0))
    b1 = mixed(cour, 1, a1, a2, right(a1))
    value = jnp.where(at < half, b0, pltpu.roll(b1, half, 1))
    quarter = half // 2
    factor = jnp.where(at < half, pltpu.roll(w0, width - quarter, 1), pltpu.roll(w1, quarter, 1))
    live = west[rows + 4 : rows + 5]
    group = (at & (half - 1)) // WIDE

    def times(s, right_side):
        low = right_side.astype(BF16)
        acc = jnp.dot(mats[s, 0], low, preferred_element_type=F32)
        for lev in range(1, levels):
            prod = jnp.dot(mats[s, lev], low, preferred_element_type=F32)
            acc = jnp.where(group == lev, prod, acc)
        return acc

    def stage(i, value):
        s = STEPS - 1 - i
        one = times(s, value)
        two = times(s, one * factor)
        three = times(s, two * factor)
        cand = 0.4 * value + 0.3 * one + 0.2 * two + 0.1 * three
        return jnp.where(live > s.astype(F32), cand, value)

    value = lax.fori_loop(0, STEPS, stage, value)
    out[pl.ds(0, spec, stride=2), :] = value
    out[pl.ds(1, spec, stride=2), :] = pltpu.roll(value, half, 1)


def sum_kernel(parts, out, *, count):
    size = out.shape[0]
    if size == 1:
        out[...] = jnp.sum(parts[...], axis=0, keepdims=True)
        return
    acc = parts[0:size]
    for k in range(1, count):
        acc = acc + parts[k * size : (k + 1) * size]
    out[...] = acc


def add_parts(parts, count):
    size, width = parts.shape[0] // count, parts.shape[1]
    return pl.pallas_call(
        functools.partial(sum_kernel, count=count),
        out_shape=jax.ShapeDtypeStruct((size, width), F32),
        in_specs=[VMEM],
        out_specs=VMEM,
        name=f"add_{count}_parts",
        compiler_params=vmem(4),
    )(parts)


def split3(value):
    high = value.astype(BF16)
    left = value - high.astype(F32)
    mid = left.astype(BF16)
    low = (left - mid.astype(F32)).astype(BF16)
    return high, mid, low


def window_kernel(
    *refs, window, first_level, count, rows, last, grad, regions
):
    refs = list(refs)
    own, north, west, corner_r, own_c, north_c, west_c, stiff, state_h, mats_h = refs[:10]
    refs = refs[10:]
    if grad:
        before, emission, region = refs[:3]
        refs = refs[3:]
    if last and not grad:
        refs = refs[1:]
    if not last and first_level == 0:
        edge_r = refs.pop(0)
    if last:
        out_h = refs.pop(0)
        if grad:
            partial = refs.pop(0)
    else:
        lam_out = refs.pop(0)
    x_s, y_s, flat_s, state_s, mats_s, sems = refs[:6]
    refs = refs[6:]
    spec, width = rows // 2, own_c.shape[1]
    get_state = pltpu.make_async_copy(
        state_h.at[window, pl.ds(first_level, count)], state_s, sems.at[0]
    )
    get_mats = pltpu.make_async_copy(
        mats_h.at[:, pl.ds(first_level, count)], mats_s, sems.at[1]
    )
    get_state.start()
    get_mats.start()
    cour = courant(own_c, north_c, west_c, rows)
    if last:
        corner = corner_r[rows : rows + spec]
    else:
        corner = corner_r[pl.ds(rows + EXTRA, spec, stride=2), :]
    west_v = west.at[0:rows]
    for lev in range(count):
        start = WIDE * (first_level + lev)
        b0, b1 = advected(own, north, west_v, corner, lev, start, cour)
        x_s[lev, :, 0:width] = b0
        x_s[lev, :, width : 2 * width] = b1
    get_state.wait()
    for lev in range(count):
        flat_s[lev] = state_s[lev].astype(F32)
        y_s[lev, :, 0:width] = flat_s[lev, pl.ds(0, spec, stride=2), :]
        y_s[lev, :, width : 2 * width] = flat_s[lev, pl.ds(1, spec, stride=2), :]
    get_mats.wait()
    live = []
    for lev in range(count):
        both = stiff[first_level + lev]
        live.append(jnp.concatenate([both[0:1], both[1:2]], axis=1))

    def stage(i, carry):
        s = STEPS - 1 - i
        rights = [x_s[lev].astype(BF16) for lev in range(count)]
        cands = [0.4 * x_s[lev] for lev in range(count)]
        for k, share in enumerate((0.3, 0.2, 0.1)):
            prods = [
                jnp.dot(mats_s[s, lev], rights[lev], preferred_element_type=F32)
                for lev in range(count)
            ]
            cands = [cands[lev] + share * prods[lev] for lev in range(count)]
            if k < 2:
                rights = [(prods[lev] * y_s[lev]).astype(BF16) for lev in range(count)]
        for lev in range(count):
            x_s[lev] = jnp.where(live[lev] > s, cands[lev], x_s[lev])
        return carry

    lax.fori_loop(0, STEPS, stage, 0)
    for lev in range(count):
        for r in range(2):
            half = x_s[lev, :, r * width : (r + 1) * width]
            if last:
                flat_s[lev, pl.ds(r, spec, stride=2), :] = half
            else:
                lam_out[pl.ds(lev * rows + r, spec, stride=2), :] = half
    if not last:
        if first_level == 0:
            lam_out[rows : rows + spec] = edge_r[pl.ds(0, spec, stride=2), :]
            lam_out[rows + spec :] = jnp.zeros((TAIL - spec, width), F32)
        return
    out_s = refs.pop(0)
    for lev in range(count):
        out_s[lev] = flat_s[lev].astype(BF16)
    put = pltpu.make_async_copy(out_s, out_h.at[pl.ds(first_level, count)], sems.at[2])
    put.start()
    if grad:
        ids = jnp.concatenate([region[0:1], region[1:2]], axis=1)
        labels = lax.broadcasted_iota(jnp.int32, (regions, 2 * width), 0)
        onehot = jnp.where(labels == ids, 1.0, 0.0).astype(BF16)
        total = []
        for r in range(2):
            now = flat_s[0, pl.ds(r, spec, stride=2), :]
            then = before[pl.ds(r, spec, stride=2), :]
            total.append((now + then) * emission[pl.ds(r, spec, stride=2), :])
        contrib = jnp.concatenate(total, axis=1)
        contrib = jnp.concatenate([contrib, jnp.zeros((width - spec, 2 * width), F32)], axis=0)
        result = jnp.zeros((regions, width), F32)
        for piece in split3(contrib):
            result = result + lax.dot_general(
                onehot, piece, (((1,), (1,)), ((), ())), preferred_element_type=F32
            )
        partial[...] = result
    put.wait()


def run_window(
    own, north, west, corner, shared, window, first_level, count, last, extra=None, prior=None, edge=None
):
    own_c, north_c, west_c, stiff, state, mats = shared
    rows, width = state.shape[2], state.shape[3]
    spec = rows // 2
    grad = extra is not None
    regions = 0
    args = [own, north, west, corner, own_c, north_c, west_c, stiff, state, mats]
    specs = [VMEM] * 8 + [ANY] * 2
    aliases = {}
    if grad:
        before, emission, region, regions = extra
        args += [before, emission, region]
        specs += [VMEM] * 3
    if edge is not None:
        args.append(edge)
        specs.append(VMEM)
    if last:
        levels = state.shape[1]
        if not grad:
            aliases = {len(args): 0}
            args.append(prior)
            specs.append(ANY)
        out_shape = [jax.ShapeDtypeStruct((levels, rows, width), BF16)]
        out_specs = [ANY]
        if grad:
            out_shape.append(jax.ShapeDtypeStruct((regions, width), F32))
            out_specs.append(VMEM)
    else:
        out_shape = [
            jax.ShapeDtypeStruct((count * rows + (0 if edge is None else TAIL), width), F32),
        ]
        out_specs = [VMEM]
    scratch = [
        pltpu.VMEM((count, spec, 2 * width), F32),
        pltpu.VMEM((count, spec, 2 * width), F32),
        pltpu.VMEM((count, rows, width), F32),
        pltpu.VMEM((count, rows, width), BF16),
        pltpu.VMEM((STEPS, count, spec, spec), BF16),
        pltpu.SemaphoreType.DMA((3,)),
    ]
    if last:
        scratch.append(pltpu.VMEM((count, rows, width), BF16))
    body = functools.partial(
        window_kernel,
        window=window,
        first_level=first_level,
        count=count,
        rows=rows,
        last=last,
        grad=grad,
        regions=regions,
    )
    return pl.pallas_call(
        body,
        out_shape=out_shape,
        in_specs=specs,
        out_specs=out_specs,
        scratch_shapes=scratch,
        input_output_aliases=aliases,
        name=f"window{window}_from{first_level}",
        cost_estimate=pl.CostEstimate(flops=0, transcendentals=0, bytes_accessed=COST[window][first_level]),
        compiler_params=vmem((16 if not last else 56) if count > 1 else 8),
    )(*args)


def to_north(block):
    bands = lax.axis_size("lat")
    return lax.ppermute(block, "lat", [(i + 1, i) for i in range(bands - 1)])


def to_west(block):
    blocks = lax.axis_size("lon")
    return lax.ppermute(block, "lon", [((j + 1) % blocks, j) for j in range(blocks)])


def per_device(
    adjoint_in, state, inverses, courant_lon, courant_lat, emission, region_id, stiffness
):
    windows, levels, spec, lat_rows, width = state.shape
    rows = spec * lat_rows
    regions = lax.axis_size("lat") * lax.axis_size("lon")
    adj = adjoint_in.reshape(levels, rows, width)
    flat_state = state.reshape(windows, levels, rows, width)
    flat_em = emission.reshape(rows, width)
    mats = jnp.swapaxes(inverses, 2, 3)
    low1 = pl.pallas_call(
        functools.partial(pack_kernel, rows=rows),
        out_shape=jax.ShapeDtypeStruct((rows + folded_rows(rows) + EXTRA, width), F32),
        in_specs=[VMEM] * 4,
        out_specs=VMEM,
        name="pack",
        compiler_params=vmem(56),
    )(adj, courant_lon, courant_lat, stiffness)
    low1_n = to_north(low1)
    rest1, west1 = pl.pallas_call(
        functools.partial(rest_kernel, rows=rows),
        out_shape=[
            jax.ShapeDtypeStruct(((levels - 1) * rows, width), F32),
            jax.ShapeDtypeStruct((folded_rows(rows) + EXTRA, width), F32),
        ],
        in_specs=[VMEM] * 2 + [HBM],
        out_specs=[VMEM] * 2,
        scratch_shapes=[pltpu.VMEM((levels, rows, width), BF16), pltpu.SemaphoreType.DMA],
        name="rest",
        compiler_params=vmem(56),
    )(adj, low1, flat_state)
    rest1, low1_n = lax.optimization_barrier((rest1, low1_n))
    rest1_n = to_north(rest1)
    west1_w = to_west(jnp.concatenate([west1, low1_n[rows:]], axis=0))
    strip, both = pl.pallas_call(
        functools.partial(strip_kernel, rows=rows),
        out_shape=[
            jax.ShapeDtypeStruct((rows, width), F32),
            jax.ShapeDtypeStruct((2 * (rows + EXTRA), width), F32),
        ],
        in_specs=[VMEM] * 2,
        out_specs=[VMEM] * 2,
        name="strip",
        cost_estimate=pl.CostEstimate(flops=0, transcendentals=0, bytes_accessed=40_000_000),
        compiler_params=vmem(8),
    )(west1_w, mats)
    shared = (low1, low1_n, both, stiffness, flat_state, mats)
    low0 = run_window(
        low1, low1_n, both, both, shared, 1, 0, 1, False, edge=strip
    )[0]
    low0_n = to_north(low0)
    rest1_n, low0 = lax.optimization_barrier((rest1_n, low0))
    rest0 = run_window(
        rest1, rest1_n, both, both, shared, 1, 1, levels - 1, False
    )[0]
    low0_n, rest0 = lax.optimization_barrier((low0_n, rest0))
    rest0_n = to_north(rest0)
    low_extra = (low0, flat_em, region_id, regions)
    out, partial = run_window(
        low0, low0_n, strip, low0_n, shared, 0, 0, 1, True, extra=low_extra
    )
    spread = lax.all_to_all(partial, ("lat", "lon"), 0, 0, tiled=True)
    out = run_window(
        rest0, rest0_n, strip, low0_n, shared, 0, 1, levels - 1, True, prior=out
    )[0]
    out, spread = lax.optimization_barrier((out, spread))
    grad = add_parts(spread, regions)[:, :spec]
    return out.reshape(levels, spec, lat_rows, width), grad


def solution(mesh):
    in_specs = (
        P(None, None, "lat", "lon"),
        P(None, None, None, "lat", "lon"),
        P(),
        P("lat", "lon"),
        P("lat", "lon"),
        P(None, "lat", "lon"),
        P("lat", "lon"),
        P(None, "lat", "lon"),
    )
    out_specs = (P(None, None, "lat", "lon"), P(("lat", "lon"), None))
    return jax.shard_map(
        per_device, mesh=mesh, in_specs=in_specs, out_specs=out_specs, check_vma=False
    )
```

```python
import functools
import jax
import jax.numpy as jnp
from jax import lax
from jax.experimental import pallas as pl
from jax.experimental.pallas import tpu as pltpu
from jax.sharding import PartitionSpec as P

STEPS = 3
EXTRA = 8
TAIL = 104
WIDE = 4
COST = ((10_000_000, 10_000_000), (40_000_000, 10_000_000))
F32 = jnp.float32
BF16 = jnp.bfloat16
ANY = pl.BlockSpec(memory_space=pl.ANY)
HBM = pl.BlockSpec(memory_space=pltpu.HBM)
VMEM = pl.BlockSpec(memory_space=pltpu.VMEM)


def vmem(mib):
    return pltpu.CompilerParams(vmem_limit_bytes=mib * 2**20)


def lanes(shape):
    return lax.broadcasted_iota(jnp.int32, shape, len(shape) - 1)


def place(acc, block, start):
    moved = pltpu.roll(block, start, 1) if start else block
    at = lanes(block.shape)
    return jnp.where((at >= start) & (at < start + WIDE), moved, acc)


def tall(row):
    return jnp.broadcast_to(row, (8, row.shape[1]))


def folded_rows(rows):
    return -(-rows // 16) * 8


def fold(acc, rows):
    width, folded = acc.shape[1], folded_rows(rows)
    upper = jnp.concatenate([acc[folded:], jnp.zeros((2 * folded - rows, width), F32)], axis=0)
    return acc[0:folded] + pltpu.roll(upper, width // 2, 1)


def pack_kernel(adj_h, clon, clat, stiff, first, adj, sems, *, rows):
    levels, _, width = adj.shape
    gets = [
        pltpu.make_async_copy(adj_h.at[lev], adj.at[lev], sems.at[lev]) for lev in range(levels)
    ]
    for get in gets:
        get.start()
    acc = jnp.zeros((rows, width), F32)
    grades = jnp.zeros((8, width), F32)
    for lev in range(levels):
        gets[lev].wait()
        block = adj[lev].astype(F32)
        if lev == 0:
            first[0:rows] = block
        acc = place(acc, block, WIDE * lev)
        both = stiff[lev].astype(F32)
        grades = place(grades, tall(both[0:1]), WIDE * lev)
        grades = place(grades, tall(both[1:2]), width // 2 + WIDE * lev)
    at = rows + folded_rows(rows)
    first[rows:at] = fold(acc, rows)
    first[at : at + 2] = clon[...]
    first[at + 2 : at + 4] = clat[...]
    first[at + 4 : at + 8] = grades[0:4]


def rest_kernel(adj, first, state_h, rest, west, state_s, sem, *, rows):
    levels, _, width = adj.shape
    get = pltpu.make_async_copy(state_h.at[state_h.shape[0] - 1], state_s, sem)
    get.start()
    for lev in range(1, levels):
        rest[(lev - 1) * rows : lev * rows] = adj[lev].astype(F32)
    get.wait()
    acc = jnp.zeros((rows, width), F32)
    for lev in range(levels):
        acc = place(acc, state_s[lev].astype(F32), width // 4 + WIDE * lev)
    at = folded_rows(rows)
    west[0:at] = first[rows : rows + at] + fold(acc, rows)
    west[at:] = first[rows + at :]


def pull(block, lane_from, lane_to, width):
    shift = (lane_to - lane_from) % width
    return pltpu.roll(block, shift, 1) if shift else block


def mixed(cour, at, mid, down, east):
    return cour["keep"][at] * mid + cour["lat"][at] * down + cour["lon"][at] * east


def with_keep(lon, lat):
    return {"lon": lon, "lat": lat, "keep": [1.0 - a - b for a, b in zip(lon, lat)]}


def advected(own, north, west, corner, lev, start, cour):
    width = own.shape[1]
    spec = west.shape[0] // 2
    end = width - 1
    last = lanes((spec, width)) == end
    base = lev * 2 * spec

    def pick(ref, first, parity):
        return ref[pl.ds(first + parity, spec, stride=2), :]

    r0, r1 = pick(own, base, 0), pick(own, base, 1)
    r2, r3 = pick(north, base, 0), pick(north, base, 1)
    w0, w1 = pick(west, 0, 0), pick(west, 0, 1)
    e0, e1 = pull(w0, start, end, width), pull(w1, start, end, width)
    g0, g1 = pull(w0, start + 1, end, width), pull(w1, start + 1, end, width)
    d0 = pull(corner, start, end, width)

    def right(block, edge):
        return jnp.where(last, edge, pltpu.roll(block, width - 1, 1))

    a0 = mixed(cour, 0, r0, r1, right(r0, e0))
    a1 = mixed(cour, 1, r1, r2, right(r1, e1))
    a2 = mixed(cour, 2, r2, r3, right(r2, d0))
    f0 = mixed(cour, 3, e0, e1, g0)
    f1 = mixed(cour, 4, e1, d0, g1)
    b0 = mixed(cour, 0, a0, a1, right(a0, f0))
    b1 = mixed(cour, 1, a1, a2, right(a1, f1))
    return b0, b1


def courant(own_c, north_c, west_c, rows):
    width = own_c.shape[1]
    at = rows + folded_rows(rows)

    def edge(row):
        return pltpu.roll(tall(row), width - 1, 1)[0:1]

    lon = [own_c[at : at + 1], own_c[at + 1 : at + 2], north_c[at : at + 1]]
    lat = [own_c[at + 2 : at + 3], own_c[at + 3 : at + 4], north_c[at + 2 : at + 3]]
    lon += [edge(west_c[rows : rows + 1]), edge(west_c[rows + 1 : rows + 2])]
    lat += [edge(west_c[rows + 2 : rows + 3]), edge(west_c[rows + 3 : rows + 4])]
    return with_keep(lon, lat)


def strip_kernel(packed, mats, out, both, *, rows):
    folded = folded_rows(rows)
    for i in range(2):
        src, dst = i * (folded + EXTRA), i * (rows + EXTRA)
        block = packed[src : src + folded]
        both[dst : dst + folded] = block
        both[dst + folded : dst + rows] = pltpu.roll(block, block.shape[1] // 2, 1)[0 : rows - folded]
        both[dst + rows : dst + rows + EXTRA] = packed[src + folded : src + folded + EXTRA]
    west, diag = both.at[0 : rows + EXTRA], both.at[rows + EXTRA : 2 * (rows + EXTRA)]
    spec, width = rows // 2, both.shape[1]
    half = width // 2
    levels = mats.shape[1]
    at = lanes((spec, width))

    def pick(ref, parity):
        return ref[pl.ds(parity, spec, stride=2), :]

    def spread(row):
        wide = tall(row)
        acc = jnp.zeros((8, width), F32)
        for lev in range(levels):
            acc = place(acc, wide, WIDE * lev)
        return acc[0:1]

    def right(block):
        return pltpu.roll(block, width - 1, 1)

    w0, w1, d0, d1 = pick(west, 0), pick(west, 1), pick(diag, 0), pick(diag, 1)
    lon = [spread(west[rows + i : rows + i + 1]) for i in range(2)]
    lat = [spread(west[rows + i : rows + i + 1]) for i in range(2, 4)]
    lon.append(spread(diag[rows : rows + 1]))
    lat.append(spread(diag[rows + 2 : rows + 3]))
    cour = with_keep(lon, lat)
    a0 = mixed(cour, 0, w0, w1, right(w0))
    a1 = mixed(cour, 1, w1, d0, right(w1))
    a2 = mixed(cour, 2, d0, d1, right(d0))
    b0 = mixed(cour, 0, a0, a1, right(a0))
    b1 = mixed(cour, 1, a1, a2, right(a1))
    value = jnp.where(at < half, b0, pltpu.roll(b1, half, 1))
    quarter = half // 2
    factor = jnp.where(at < half, pltpu.roll(w0, width - quarter, 1), pltpu.roll(w1, quarter, 1))
    live = west[rows + 4 : rows + 5]
    group = (at & (half - 1)) // WIDE

    def times(s, right_side):
        low = right_side.astype(BF16)
        acc = jnp.dot(mats[s, 0], low, preferred_element_type=F32)
        for lev in range(1, levels):
            prod = jnp.dot(mats[s, lev], low, preferred_element_type=F32)
            acc = jnp.where(group == lev, prod, acc)
        return acc

    def stage(i, value):
        s = STEPS - 1 - i
        one = times(s, value)
        two = times(s, one * factor)
        three = times(s, two * factor)
        cand = 0.4 * value + 0.3 * one + 0.2 * two + 0.1 * three
        return jnp.where(live > s.astype(F32), cand, value)

    value = lax.fori_loop(0, STEPS, stage, value)
    out[pl.ds(0, spec, stride=2), :] = value
    out[pl.ds(1, spec, stride=2), :] = pltpu.roll(value, half, 1)


def sum_kernel(parts, out, *, count):
    size = out.shape[0]
    if size == 1:
        out[...] = jnp.sum(parts[...], axis=0, keepdims=True)
        return
    acc = parts[0:size]
    for k in range(1, count):
        acc = acc + parts[k * size : (k + 1) * size]
    out[...] = acc


def add_parts(parts, count):
    size, width = parts.shape[0] // count, parts.shape[1]
    return pl.pallas_call(
        functools.partial(sum_kernel, count=count),
        out_shape=jax.ShapeDtypeStruct((size, width), F32),
        in_specs=[VMEM],
        out_specs=VMEM,
        name=f"add_{count}_parts",
        compiler_params=vmem(4),
    )(parts)


def split3(value):
    high = value.astype(BF16)
    left = value - high.astype(F32)
    mid = left.astype(BF16)
    low = (left - mid.astype(F32)).astype(BF16)
    return high, mid, low


def window_kernel(
    *refs, window, first_level, count, rows, last, grad, regions
):
    refs = list(refs)
    own, north, west, corner_r, own_c, north_c, west_c, stiff, state_h, mats_h = refs[:10]
    refs = refs[10:]
    if grad:
        before, emission, region = refs[:3]
        refs = refs[3:]
    if last and not grad:
        refs = refs[1:]
    if not last and first_level == 0:
        edge_r = refs.pop(0)
    if last:
        out_h = refs.pop(0)
        if grad:
            partial = refs.pop(0)
    else:
        lam_out = refs.pop(0)
    x_s, y_s, flat_s, state_s, mats_s, sems = refs[:6]
    refs = refs[6:]
    spec, width = rows // 2, own_c.shape[1]
    get_state = pltpu.make_async_copy(
        state_h.at[window, pl.ds(first_level, count)], state_s, sems.at[0]
    )
    get_mats = pltpu.make_async_copy(
        mats_h.at[:, pl.ds(first_level, count)], mats_s, sems.at[1]
    )
    get_state.start()
    get_mats.start()
    cour = courant(own_c, north_c, west_c, rows)
    if last:
        corner = corner_r[rows : rows + spec]
    else:
        corner = corner_r[pl.ds(rows + EXTRA, spec, stride=2), :]
    west_v = west.at[0:rows]
    for lev in range(count):
        start = WIDE * (first_level + lev)
        b0, b1 = advected(own, north, west_v, corner, lev, start, cour)
        x_s[lev, :, 0:width] = b0
        x_s[lev, :, width : 2 * width] = b1
    if grad:
        onehot = refs[1]
        ids = jnp.concatenate([region[0:1], region[1:2]], axis=1)
        labels = lax.broadcasted_iota(jnp.int32, (regions, 2 * width), 0)
        onehot[...] = jnp.where(labels == ids, 1.0, 0.0).astype(BF16)
    get_state.wait()
    for lev in range(count):
        flat_s[lev] = state_s[lev].astype(F32)
        y_s[lev, :, 0:width] = flat_s[lev, pl.ds(0, spec, stride=2), :]
        y_s[lev, :, width : 2 * width] = flat_s[lev, pl.ds(1, spec, stride=2), :]
    get_mats.wait()
    live = []
    for lev in range(count):
        both = stiff[first_level + lev]
        live.append(jnp.concatenate([both[0:1], both[1:2]], axis=1))

    def stage(i, carry):
        s = STEPS - 1 - i
        rights = [x_s[lev].astype(BF16) for lev in range(count)]
        cands = [0.4 * x_s[lev] for lev in range(count)]
        for k, share in enumerate((0.3, 0.2, 0.1)):
            prods = [
                jnp.dot(mats_s[s, lev], rights[lev], preferred_element_type=F32)
                for lev in range(count)
            ]
            cands = [cands[lev] + share * prods[lev] for lev in range(count)]
            if k < 2:
                rights = [(prods[lev] * y_s[lev]).astype(BF16) for lev in range(count)]
        for lev in range(count):
            x_s[lev] = jnp.where(live[lev] > s, cands[lev], x_s[lev])
        return carry

    lax.fori_loop(0, STEPS, stage, 0)
    for lev in range(count):
        for r in range(2):
            half = x_s[lev, :, r * width : (r + 1) * width]
            if last:
                flat_s[lev, pl.ds(r, spec, stride=2), :] = half
            else:
                lam_out[pl.ds(lev * rows + r, spec, stride=2), :] = half
    if not last:
        if first_level == 0:
            lam_out[rows : rows + spec] = edge_r[pl.ds(0, spec, stride=2), :]
            lam_out[rows + spec :] = jnp.zeros((TAIL - spec, width), F32)
        return
    out_s = refs.pop(0)
    for lev in range(count):
        out_s[lev] = flat_s[lev].astype(BF16)
    put = pltpu.make_async_copy(out_s, out_h.at[pl.ds(first_level, count)], sems.at[2])
    put.start()
    if grad:
        total = []
        for r in range(2):
            now = flat_s[0, pl.ds(r, spec, stride=2), :]
            then = before[pl.ds(r, spec, stride=2), :]
            total.append((now + then) * emission[pl.ds(r, spec, stride=2), :])
        contrib = jnp.concatenate(total, axis=1)
        contrib = jnp.concatenate([contrib, jnp.zeros((width - spec, 2 * width), F32)], axis=0)
        result = jnp.zeros((regions, width), F32)
        for piece in split3(contrib):
            result = result + lax.dot_general(
                onehot[...], piece, (((1,), (1,)), ((), ())), preferred_element_type=F32
            )
        partial[...] = result
    put.wait()


def run_window(
    own, north, west, corner, shared, window, first_level, count, last, extra=None, prior=None, edge=None
):
    own_c, north_c, west_c, stiff, state, mats = shared
    rows, width = state.shape[2], state.shape[3]
    spec = rows // 2
    grad = extra is not None
    regions = 0
    args = [own, north, west, corner, own_c, north_c, west_c, stiff, state, mats]
    specs = [VMEM] * 8 + [ANY] * 2
    aliases = {}
    if grad:
        before, emission, region, regions = extra
        args += [before, emission, region]
        specs += [VMEM] * 3
    if edge is not None:
        args.append(edge)
        specs.append(VMEM)
    if last:
        levels = state.shape[1]
        if not grad:
            aliases = {len(args): 0}
            args.append(prior)
            specs.append(ANY)
        out_shape = [jax.ShapeDtypeStruct((levels, rows, width), BF16)]
        out_specs = [ANY]
        if grad:
            out_shape.append(jax.ShapeDtypeStruct((regions, width), F32))
            out_specs.append(VMEM)
    else:
        out_shape = [
            jax.ShapeDtypeStruct((count * rows + (0 if edge is None else TAIL), width), F32),
        ]
        out_specs = [VMEM]
    scratch = [
        pltpu.VMEM((count, spec, 2 * width), F32),
        pltpu.VMEM((count, spec, 2 * width), F32),
        pltpu.VMEM((count, rows, width), F32),
        pltpu.VMEM((count, rows, width), BF16),
        pltpu.VMEM((STEPS, count, spec, spec), BF16),
        pltpu.SemaphoreType.DMA((3,)),
    ]
    if last:
        scratch.append(pltpu.VMEM((count, rows, width), BF16))
    if grad:
        scratch.append(pltpu.VMEM((regions, 2 * width), BF16))
    body = functools.partial(
        window_kernel,
        window=window,
        first_level=first_level,
        count=count,
        rows=rows,
        last=last,
        grad=grad,
        regions=regions,
    )
    return pl.pallas_call(
        body,
        out_shape=out_shape,
        in_specs=specs,
        out_specs=out_specs,
        scratch_shapes=scratch,
        input_output_aliases=aliases,
        name=f"window{window}_from{first_level}",
        cost_estimate=pl.CostEstimate(flops=0, transcendentals=0, bytes_accessed=COST[window][first_level]),
        compiler_params=vmem((16 if not last else 56) if count > 1 else 8),
    )(*args)


def to_north(block):
    bands = lax.axis_size("lat")
    return lax.ppermute(block, "lat", [(i + 1, i) for i in range(bands - 1)])


def to_west(block):
    blocks = lax.axis_size("lon")
    return lax.ppermute(block, "lon", [((j + 1) % blocks, j) for j in range(blocks)])


def per_device(
    adjoint_in, state, inverses, courant_lon, courant_lat, emission, region_id, stiffness
):
    windows, levels, spec, lat_rows, width = state.shape
    rows = spec * lat_rows
    regions = lax.axis_size("lat") * lax.axis_size("lon")
    adj = adjoint_in.reshape(levels, rows, width)
    flat_state = state.reshape(windows, levels, rows, width)
    flat_em = emission.reshape(rows, width)
    mats = jnp.swapaxes(inverses, 2, 3)
    low1 = pl.pallas_call(
        functools.partial(pack_kernel, rows=rows),
        out_shape=jax.ShapeDtypeStruct((rows + folded_rows(rows) + EXTRA, width), F32),
        in_specs=[HBM] + [VMEM] * 3,
        out_specs=VMEM,
        scratch_shapes=[
            pltpu.VMEM((levels, rows, width), BF16),
            pltpu.SemaphoreType.DMA((levels,)),
        ],
        name="pack",
        compiler_params=vmem(56),
    )(adj, courant_lon, courant_lat, stiffness)
    low1_n = to_north(low1)
    rest1, west1 = pl.pallas_call(
        functools.partial(rest_kernel, rows=rows),
        out_shape=[
            jax.ShapeDtypeStruct(((levels - 1) * rows, width), F32),
            jax.ShapeDtypeStruct((folded_rows(rows) + EXTRA, width), F32),
        ],
        in_specs=[VMEM] * 2 + [HBM],
        out_specs=[VMEM] * 2,
        scratch_shapes=[pltpu.VMEM((levels, rows, width), BF16), pltpu.SemaphoreType.DMA],
        name="rest",
        compiler_params=vmem(56),
    )(adj, low1, flat_state)
    rest1, low1_n = lax.optimization_barrier((rest1, low1_n))
    rest1_n = to_north(rest1)
    west1_w = to_west(jnp.concatenate([west1, low1_n[rows:]], axis=0))
    strip, both = pl.pallas_call(
        functools.partial(strip_kernel, rows=rows),
        out_shape=[
            jax.ShapeDtypeStruct((rows, width), F32),
            jax.ShapeDtypeStruct((2 * (rows + EXTRA), width), F32),
        ],
        in_specs=[VMEM] * 2,
        out_specs=[VMEM] * 2,
        name="strip",
        cost_estimate=pl.CostEstimate(flops=0, transcendentals=0, bytes_accessed=40_000_000),
        compiler_params=vmem(8),
    )(west1_w, mats)
    shared = (low1, low1_n, both, stiffness, flat_state, mats)
    low0 = run_window(
        low1, low1_n, both, both, shared, 1, 0, 1, False, edge=strip
    )[0]
    low0_n = to_north(low0)
    rest1_n, low0 = lax.optimization_barrier((rest1_n, low0))
    rest0 = run_window(
        rest1, rest1_n, both, both, shared, 1, 1, levels - 1, False
    )[0]
    low0_n, rest0 = lax.optimization_barrier((low0_n, rest0))
    rest0_n = to_north(rest0)
    low_extra = (low0, flat_em, region_id, regions)
    out, partial = run_window(
        low0, low0_n, strip, low0_n, shared, 0, 0, 1, True, extra=low_extra
    )
    spread = lax.all_to_all(partial, ("lat", "lon"), 0, 0, tiled=True)
    out = run_window(
        rest0, rest0_n, strip, low0_n, shared, 0, 1, levels - 1, True, prior=out
    )[0]
    out, spread = lax.optimization_barrier((out, spread))
    grad = add_parts(spread, regions)[:, :spec]
    return out.reshape(levels, spec, lat_rows, width), grad


def solution(mesh):
    in_specs = (
        P(None, None, "lat", "lon"),
        P(None, None, None, "lat", "lon"),
        P(),
        P("lat", "lon"),
        P("lat", "lon"),
        P(None, "lat", "lon"),
        P("lat", "lon"),
        P(None, "lat", "lon"),
    )
    out_specs = (P(None, None, "lat", "lon"), P(("lat", "lon"), None))
    return jax.shard_map(
        per_device, mesh=mesh, in_specs=in_specs, out_specs=out_specs, check_vma=False
    )
```
